32 devices in a mesh: seq: 16 (over z, y, core), chan: 2 (over x).
Axes of the slice: x: 2, y: 2, z: 4, core: 2. Of those that a mesh axis runs over, the one named last changes fastest.
Arguments:
- v_stream: bfloat16 [4096, 8192], P('chan', 'seq'), may hold values from -6 to 6
- gate_one: bfloat16 [4096, 8192], P('chan', 'seq'), may hold values from -6 to 6
- gate_two: bfloat16 [4096, 8192], P('chan', 'seq'), may hold values from -6 to 6
- short_filter: float32 [4096, 128], P('chan'), may hold values from -0.5 to 0.5
- decay_rates: float32 [4096, 16], P('chan'), may hold values from 6.1035157e-06 to 0.03
- residues: float32 [4096, 16], P('chan'), may hold values from -1.5 to 1.5
- skip_bias: float32 [4096], P('chan'), may hold values from -3 to 3
Outputs:
- hyena_out: bfloat16 [4096, 8192], P('chan', 'seq')
The draws below stay inside these ranges and needn't reach their ends.
All inputs are finite; a program needn't handle non-finite values.
Results may differ from the reference program's by a relative error of at most 0.005.
Values may be sent and summed in bfloat16 or wider, within the bound.
No kernel may reach another device: no remote copies, remote signals or barrier semaphores. Data moves between devices by JAX's collectives and lax.ppermute only.
A program may use at most 192 MiB of HBM per device.

```python
import math
import jax
import jax.numpy as jnp
from jax import lax

D = 4096
K = 128
MODES = 16
TOKENS = 8192


def steps_of(stream_key, shape, shards, least, high):
    factor_of, own = 1.0, jax.random.fold_in(stream_key, 6)
    for axis_at, shards_of in shards:
        steps = jnp.exp(jax.random.uniform(jax.random.fold_in(own, axis_at), (shards_of,), jnp.float32, least / len(shards), high / len(shards)))
        factor_of = factor_of * jnp.repeat(steps, shape[axis_at] // shards_of).reshape([-1 if axis == axis_at else 1 for axis in range(len(shape))])
    return factor_of


def normal_values(key, dims, spread, reach, cuts=(), held_as=jnp.bfloat16):
    values = spread * jax.random.normal(key, dims, jnp.float32)
    if cuts:
        values = values * steps_of(key, dims, cuts, -0.22, 0.18)
    return jnp.clip(values, -reach, reach).astype(held_as)


def setup_inputs(seed: int = 0) -> dict:
    arg_keys = jax.random.split(jax.random.key(seed), 8)
    v_stream = normal_values(arg_keys[0], (D, TOKENS), 1.0, 6.0, ((0, 2), (1, 16)))
    gate_one = normal_values(arg_keys[1], (D, TOKENS), 1.0, 6.0, ((0, 2), (1, 16)))
    gate_two = normal_values(arg_keys[2], (D, TOKENS), 1.0, 6.0, ((0, 2), (1, 16)))
    short_filter = normal_values(arg_keys[3], (D, K), K ** -0.5, 0.5, ((0, 2),), jnp.float32)
    decay_rates = jnp.clip(jnp.exp(math.log(0.03) - 8.500088 * jax.random.uniform(arg_keys[4], (D, MODES), jnp.float32) ** steps_of(arg_keys[4], (D, MODES), ((0, 2),), -0.2, 0.2)), 6.10351571594947e-06, 0.03)
    residues = normal_values(arg_keys[5], (D, MODES), 0.25, 1.5, ((0, 2),), jnp.float32)
    skip_bias = normal_values(arg_keys[6], (D,), 0.5, 3.0, ((0, 2),), jnp.float32)
    return {"v_stream": v_stream, "gate_one": gate_one, "gate_two": gate_two, "short_filter": short_filter, "decay_rates": decay_rates, "residues": residues, "skip_bias": skip_bias}


def reference(v_stream, gate_one, gate_two, short_filter, decay_rates, residues, skip_bias):
    channels, seq_len = v_stream.shape
    block_size = math.gcd(channels, 128)
    num_blocks = channels // block_size
    fft_len = 2 * seq_len
    positions = jnp.arange(seq_len, dtype=jnp.float32)

    def one_block(pieces):
        v_blk, gate_a, gate_b, taps, rates, weights, bias = pieces
        short = jnp.fft.irfft(jnp.fft.rfft(v_blk.astype(jnp.float32), fft_len, axis=1) * jnp.fft.rfft(taps, fft_len, axis=1), fft_len, axis=1)[:, :seq_len]
        mixed = (gate_a.astype(jnp.float32) * short).astype(jnp.bfloat16)
        mixed_wide = mixed.astype(jnp.float32)
        scaled = weights * jnp.sqrt(2.0 * rates + 2.0 / seq_len)
        decay = jnp.exp(-rates[:, :, None] * positions[None, None, :])
        filter_values = jnp.einsum('cm,cmt->ct', scaled, decay, precision=lax.Precision.HIGHEST)
        long_conv = jnp.fft.irfft(jnp.fft.rfft(mixed_wide, fft_len, axis=1) * jnp.fft.rfft(filter_values, fft_len, axis=1), fft_len, axis=1)[:, :seq_len]
        skipped = long_conv + bias[:, None] * mixed_wide
        return (gate_b.astype(jnp.float32) * skipped).astype(jnp.bfloat16)

    def split_rows(array):
        return array.reshape((num_blocks, block_size) + array.shape[1:])
    result = lax.map(one_block, (split_rows(v_stream), split_rows(gate_one), split_rows(gate_two), split_rows(short_filter), split_rows(decay_rates), split_rows(residues), split_rows(skip_bias)))
    return result.reshape(channels, seq_len)
```

```python
import functools
import math

import jax
import jax.numpy as jnp
import numpy as np
from jax import lax
from jax.experimental import pallas as pl
from jax.experimental.pallas import tpu as pltpu
from jax.sharding import PartitionSpec as P

LANES = 128
SUBS = 8
TILE = LANES * SUBS
BLOCK = 128
ROWS = 256
STEPS = 8
F32, BF16 = jnp.float32, jnp.bfloat16


def halves(table):
    high = table.astype(jnp.bfloat16)
    low = (table - high.astype(np.float64)).astype(jnp.bfloat16)
    return high, low


def window_tables():
    size = 2 * BLOCK
    phase = 2.0 * math.pi / size * np.outer(np.arange(size), np.arange(BLOCK) + 0.5)
    forward = np.concatenate([np.cos(phase), -np.sin(phase)], axis=1)
    inverse = forward[BLOCK:].T / BLOCK
    return halves(forward), halves(inverse)


def mm(left, right):
    return jnp.dot(left, right, preferred_element_type=F32)


def split(value):
    high = value.astype(BF16)
    return high, (value - high.astype(F32)).astype(BF16)


def apply_window(window, spectrum, fwd_hi, fwd_lo, inv_hi, inv_lo):
    image = mm(window, fwd_hi[...]) + mm(window, fwd_lo[...])
    re, im = image[:, :BLOCK], image[:, BLOCK:]
    h_re, h_im = spectrum[:, :BLOCK], spectrum[:, BLOCK:]
    product = jnp.concatenate([re * h_re - im * h_im, re * h_im + im * h_re], axis=1)
    high, low = split(product)
    return mm(high, inv_hi[...]) + mm(low, inv_hi[...]) + mm(high, inv_lo[...])


def put_mixed(store, first_row, block_at, short, gate):
    mixed = (gate.astype(F32) * short).astype(BF16).astype(F32)
    for piece in range(ROWS // LANES):
        group = first_row // LANES + piece
        turned = mixed[piece * LANES : (piece + 1) * LANES].T
        store[pl.ds(block_at * BLOCK * SUBS + group, BLOCK, stride=SUBS), :] = turned


def end_states(store, mixed_ref, rates_ref, start):
    modes = rates_ref.shape[0]
    steps = store.shape[0] // SUBS
    decay = [jnp.exp(-rates_ref[mode]) for mode in range(modes)]

    def turn(index, states):
        at = pl.multiple_of(index * STEPS * SUBS, STEPS * SUBS)
        values = store[pl.ds(at, STEPS * SUBS), :]
        mixed_ref[pl.ds(at, STEPS * SUBS), :] = values.astype(BF16)
        for step in range(STEPS):
            value = values[step * SUBS : (step + 1) * SUBS]
            states = tuple(d * s + value for d, s in zip(decay, states))
        return states

    return lax.fori_loop(0, steps // STEPS, turn, start)


def inner_kernel(v_ref, gate_ref, taps_ref, rates_ref, fwd_hi, fwd_lo, inv_hi, inv_lo, spec_ref, mixed_ref, state_ref, store):
    windows = v_ref.shape[1] // BLOCK - 1
    for first in range(0, TILE, ROWS):
        rows = slice(first, first + ROWS)
        tap_hi, tap_lo = split(taps_ref[rows])
        head_hi, head_lo = fwd_hi[:BLOCK], fwd_lo[:BLOCK]
        spectrum = mm(tap_hi, head_hi) + mm(tap_lo, head_hi) + mm(tap_hi, head_lo)
        spec_ref[rows] = spectrum
        for window in range(windows):
            at = window * BLOCK
            short = apply_window(v_ref[rows, at : at + 2 * BLOCK], spectrum, fwd_hi, fwd_lo, inv_hi, inv_lo)
            put_mixed(store, first, window, short, gate_ref[rows, at + BLOCK : at + 2 * BLOCK])
    zeros = tuple(jnp.zeros((SUBS, LANES), F32) for _ in range(rates_ref.shape[0]))
    for mode, state in enumerate(end_states(store, mixed_ref, rates_ref, zeros)):
        state_ref[mode] = state


def rim_kernel(inner, before_ref, v_ref, gate_ref, spec_ref, rates_ref, inner_ref, fwd_hi, fwd_lo, inv_hi, inv_lo, mixed_ref, state_ref, store):
    for first in range(0, TILE, ROWS):
        rows = slice(first, first + ROWS)
        window = jnp.concatenate([before_ref[rows], v_ref[rows]], axis=1)
        short = apply_window(window, spec_ref[rows], fwd_hi, fwd_lo, inv_hi, inv_lo)
        put_mixed(store, first, 0, short, gate_ref[rows])
    zeros = tuple(jnp.zeros((SUBS, LANES), F32) for _ in range(rates_ref.shape[0]))
    for mode, state in enumerate(end_states(store, mixed_ref, rates_ref, zeros)):
        state_ref[mode] = jnp.exp(-float(inner) * rates_ref[mode]) * state + inner_ref[mode]


def outer_kernel(seq_total, rim_ref, inner_ref, gate_ref, rates_ref, weights_ref, bias_ref, start_ref, out_ref, store):
    modes = rates_ref.shape[0]
    decay = [jnp.exp(-rates_ref[mode]) for mode in range(modes)]
    scaled = [weights_ref[mode] * jnp.sqrt(2.0 * rates_ref[mode] + 2.0 / seq_total) for mode in range(modes)]
    bias = bias_ref[...]
    states = tuple(start_ref[mode] for mode in range(modes))
    first = 0
    for source in (rim_ref, inner_ref):

        def turn(index, states, source=source, first=first):
            at = pl.multiple_of(index * STEPS * SUBS, STEPS * SUBS)
            values = source[pl.ds(at, STEPS * SUBS), :].astype(F32)
            sums = []
            for step in range(STEPS):
                value = values[step * SUBS : (step + 1) * SUBS]
                states = tuple(d * s + value for d, s in zip(decay, states))
                parts = [c * s for c, s in zip(scaled, states)] + [bias * value]
                while len(parts) > 1:
                    parts = [sum(parts[i : i + 2][1:], parts[i]) for i in range(0, len(parts), 2)]
                sums.append(parts[0])
            store[pl.ds(first * SUBS + at, STEPS * SUBS), :] = jnp.concatenate(sums, axis=0)
            return states

        count = source.shape[0] // SUBS
        states = lax.fori_loop(0, count // STEPS, turn, states)
        first += count
    for group in range(SUBS):
        rows = slice(group * LANES, (group + 1) * LANES)
        for block in range(first // BLOCK):
            cols = slice(block * BLOCK, (block + 1) * BLOCK)
            turned = store[pl.ds(block * BLOCK * SUBS + group, BLOCK, stride=SUBS), :].T
            out_ref[rows, cols] = (gate_ref[rows, cols].astype(F32) * turned).astype(BF16)


def call(kernel, tiles, in_specs, out_specs, out_shape, steps, flops, moved):
    return pl.pallas_call(
        kernel,
        grid=(tiles,),
        in_specs=in_specs,
        out_specs=out_specs,
        out_shape=out_shape,
        scratch_shapes=[pltpu.VMEM((steps * SUBS, LANES), F32)],
        compiler_params=pltpu.CompilerParams(vmem_limit_bytes=48 << 20),
        cost_estimate=pl.CostEstimate(flops=flops, bytes_accessed=moved, transcendentals=0),
    )


def rows_spec(width, column=0):
    return pl.BlockSpec((TILE, width), lambda i: (i, column))


def modes_spec(modes):
    return pl.BlockSpec((modes, SUBS, LANES), lambda i: (0, i, 0))


def steps_spec(steps):
    return pl.BlockSpec((None, steps * SUBS, LANES), lambda i: (i, 0, 0))


def whole_spec(table):
    return pl.BlockSpec(table.shape, lambda i: (0, 0))


def on_device(v_stream, gate_one, gate_two, short_filter, decay_rates, residues, skip_bias):
    real_channels, tokens = v_stream.shape
    modes = decay_rates.shape[1]
    shards = lax.axis_size("seq")
    tail = v_stream[:, tokens - BLOCK :]
    before = lax.ppermute(tail, "seq", [(i, i + 1) for i in range(shards - 1)])
    extra = -real_channels % TILE

    def padded(array):
        return jnp.pad(array, ((0, extra),) + ((0, 0),) * (array.ndim - 1)) if extra else array

    v_stream, gate_one, gate_two, short_filter = map(padded, (v_stream, gate_one, gate_two, short_filter))
    decay_rates, residues, skip_bias, before = map(padded, (decay_rates, residues, skip_bias, before))
    channels = real_channels + extra
    tiles, groups = channels // TILE, channels // LANES
    rates = decay_rates.T.reshape(modes, groups, LANES)
    weights = residues.T.reshape(modes, groups, LANES)
    bias = skip_bias.reshape(groups, LANES)
    (fwd_hi, fwd_lo), (inv_hi, inv_lo) = window_tables()
    tables = [jnp.asarray(t) for t in (fwd_hi, fwd_lo, inv_hi, inv_lo)]
    table_specs = [whole_spec(t) for t in tables]
    inner = tokens - BLOCK
    shape = jax.ShapeDtypeStruct
    spectrum, inner_mixed, inner_state = call(
        inner_kernel,
        tiles,
        [rows_spec(tokens), rows_spec(tokens), rows_spec(BLOCK), modes_spec(modes)] + table_specs,
        [rows_spec(2 * BLOCK), steps_spec(inner), modes_spec(modes)],
        [
            shape((channels, 2 * BLOCK), F32),
            shape((tiles, inner * SUBS, LANES), BF16),
            shape((modes, groups, LANES), F32),
        ],
        inner,
        channels * inner * 2600,
        channels * tokens * 8,
    )(v_stream, gate_one, short_filter, rates, *tables)
    rim_mixed, end_state = call(
        functools.partial(rim_kernel, inner),
        tiles,
        [rows_spec(BLOCK), rows_spec(BLOCK), rows_spec(BLOCK), rows_spec(2 * BLOCK), modes_spec(modes), modes_spec(modes)]
        + table_specs,
        [steps_spec(BLOCK), modes_spec(modes)],
        [shape((tiles, BLOCK * SUBS, LANES), BF16), shape((modes, groups, LANES), F32)],
        BLOCK,
        channels * BLOCK * 2600,
        channels * BLOCK * 16,
    )(before, v_stream, gate_one, spectrum, rates, inner_state, *tables)

    me = lax.axis_index("seq")
    pieces = end_state.reshape(shards, -1, LANES)
    moved = lax.all_to_all(pieces, "seq", split_axis=0, concat_axis=0, tiled=True)
    own_rates = lax.dynamic_index_in_dim(rates.reshape(shards, -1, LANES), me, 0, keepdims=False)
    reach = jnp.exp(-float(tokens) * own_rates)
    carried = [jnp.zeros_like(reach)]
    for shard in range(shards - 1):
        carried.append(reach * carried[-1] + moved[shard])
    start = lax.all_to_all(jnp.stack(carried), "seq", split_axis=0, concat_axis=0, tiled=True)
    start = start.reshape(modes, groups, LANES)

    hyena_out = call(
        functools.partial(outer_kernel, tokens * shards),
        tiles,
        [
            steps_spec(BLOCK),
            steps_spec(inner),
            rows_spec(tokens),
            modes_spec(modes),
            modes_spec(modes),
            pl.BlockSpec((SUBS, LANES), lambda i: (i, 0)),
            modes_spec(modes),
        ],
        rows_spec(tokens),
        shape((channels, tokens), BF16),
        tokens,
        channels * tokens * 70,
        channels * tokens * 6,
    )(rim_mixed, inner_mixed, gate_two, rates, weights, bias, start)
    return hyena_out[:real_channels]


def solution(mesh):
    in_specs = (
        P("chan", "seq"),
        P("chan", "seq"),
        P("chan", "seq"),
        P("chan", None),
        P("chan", None),
        P("chan", None),
        P("chan"),
    )
    out_specs = P("chan", "seq")
    return jax.shard_map(
        on_device, mesh=mesh, in_specs=in_specs, out_specs=out_specs, check_vma=False
    )
```

```python
import functools
import math

import jax
import jax.numpy as jnp
import numpy as np
from jax import lax
from jax.experimental import pallas as pl
from jax.experimental.pallas import tpu as pltpu
from jax.sharding import PartitionSpec as P

LANES = 128
SUBS = 8
TILE = LANES * SUBS
BLOCK = 128
ROWS = 256
STEPS = 8
F32, BF16 = jnp.float32, jnp.bfloat16


def halves(table):
    high = table.astype(jnp.bfloat16)
    low = (table - high.astype(np.float64)).astype(jnp.bfloat16)
    return high, low


def window_tables():
    size = 2 * BLOCK
    phase = 2.0 * math.pi / size * np.outer(np.arange(size), np.arange(BLOCK) + 0.5)
    forward = np.concatenate([np.cos(phase), -np.sin(phase)], axis=1)
    signs = np.tile((-1.0) ** np.arange(BLOCK), 2)
    inverse = forward[BLOCK:].T / BLOCK
    even = np.concatenate(halves(forward[:BLOCK]), axis=0)
    odd = np.concatenate(halves(forward[:BLOCK] * signs), axis=0)
    back = np.concatenate(halves(inverse), axis=1)
    return np.concatenate([even, odd, back], axis=1)


EVEN, ODD, BACK = (slice(i * 2 * BLOCK, (i + 1) * 2 * BLOCK) for i in range(3))


def mm(left, right):
    return jnp.dot(left, right, preferred_element_type=F32)


def split(value):
    high = value.astype(BF16)
    return high, (value - high.astype(F32)).astype(BF16)


def twice(block):
    return jnp.concatenate([block, block], axis=1)


def parts(image):
    return image[:, :BLOCK], image[:, BLOCK:]


def apply_window(earlier, later, spectrum, tables):
    (e_re, e_im), (l_re, l_im), (h_re, h_im) = parts(earlier), parts(later), parts(spectrum)
    re, im = e_re + l_im, e_im - l_re
    high, low = split(jnp.concatenate([re * h_re - im * h_im, re * h_im + im * h_re], axis=1))
    both = mm(high, tables[:, BACK])
    return both[:, :BLOCK] + both[:, BLOCK:] + mm(low, tables[:, BACK][:, :BLOCK])


def put_mixed(store, first_row, block_at, short, gate):
    mixed = (gate.astype(F32) * short).astype(BF16).astype(F32)
    for piece in range(ROWS // LANES):
        group = first_row // LANES + piece
        turned = mixed[piece * LANES : (piece + 1) * LANES].T
        store[pl.ds(block_at * BLOCK * SUBS + group, BLOCK, stride=SUBS), :] = turned


def end_states(store, mixed_ref, rates_ref):
    modes = rates_ref.shape[0]
    steps = store.shape[0] // SUBS
    decay = [jnp.exp(-rates_ref[mode]) for mode in range(modes)]

    def turn(index, states):
        at = pl.multiple_of(index * STEPS * SUBS, STEPS * SUBS)
        values = store[pl.ds(at, STEPS * SUBS), :]
        mixed_ref[pl.ds(at, STEPS * SUBS), :] = values.astype(BF16)
        for step in range(STEPS):
            value = values[step * SUBS : (step + 1) * SUBS]
            states = tuple(d * s + value for d, s in zip(decay, states))
        return states

    zeros = tuple(jnp.zeros((SUBS, LANES), F32) for _ in range(modes))
    return lax.fori_loop(0, steps // STEPS, turn, zeros)


def inner_kernel(v_ref, gate_ref, taps_ref, rates_ref, tables, spec_ref, mixed_ref, state_ref, store):
    blocks = v_ref.shape[1] // BLOCK
    sign = 1.0 - 2.0 * (lax.broadcasted_iota(jnp.int32, (1, 2 * BLOCK), 1) % 2).astype(F32)
    for first in range(0, TILE, ROWS):
        rows = slice(first, first + ROWS)
        tap_hi, tap_lo = split(taps_ref[rows])
        spectrum = mm(twice(tap_hi), tables[:, EVEN]) + mm(tap_lo, tables[:BLOCK, EVEN])
        turned = spectrum * sign
        spec_ref[rows] = turned
        earlier = mm(twice(v_ref[rows, :BLOCK]), tables[:, EVEN])
        for block in range(1, blocks):
            at = slice(block * BLOCK, (block + 1) * BLOCK)
            later = mm(twice(v_ref[rows, at]), tables[:, ODD if block % 2 else EVEN])
            short = apply_window(earlier, later, spectrum if block % 2 else turned, tables)
            put_mixed(store, first, block - 1, short, gate_ref[rows, at])
            earlier = later
    for mode, state in enumerate(end_states(store, mixed_ref, rates_ref)):
        state_ref[mode] = state


def rim_kernel(inner, place_ref, before_ref, v_ref, gate_ref, spec_ref, rates_ref, inner_ref, tables, *rest):
    mixed_ref, *piece_refs, store, ends = rest
    for first in range(0, TILE, ROWS):
        rows = slice(first, first + ROWS)
        earlier = mm(twice(before_ref[rows]), tables[:, ODD])
        later = mm(twice(v_ref[rows]), tables[:, EVEN])
        short = apply_window(earlier, later, spec_ref[rows], tables)
        put_mixed(store, first, 0, short, gate_ref[rows])
    for mode, state in enumerate(end_states(store, mixed_ref, rates_ref)):
        ends[mode] = jnp.exp(-float(inner) * rates_ref[mode]) * state + inner_ref[mode]
    plane = len(piece_refs)
    share = ends.shape[0] // plane
    for ahead, piece in enumerate(piece_refs):
        piece[...] = ends[pl.ds(lax.rem(place_ref[0] + ahead, plane) * share, share)]


def decayed(rates, positions):
    return jnp.exp(-lax.convert_element_type(positions, F32) * rates)


def total_kernel(tokens, place_ref, rates_ref, *rest):
    *ends, total_ref = rest
    plane, share = len(ends), total_ref.shape[0]
    place = place_ref[0]
    for mode in range(share):
        rates = rates_ref[place * share + mode]
        total = None
        for behind, end in enumerate(ends):
            owner = lax.rem(place - behind + plane, plane)
            term = decayed(rates, tokens * (plane - 1 - owner)) * end[mode]
            total = term if total is None else total + term
        total_ref[mode] = total


def start_kernel(tokens, planes, place_ref, rates_ref, *rest):
    plane = (len(rest) - (planes - 1)) // 2
    ends, totals, starts = rest[:plane], rest[plane : plane + planes - 1], rest[plane + planes - 1 :]
    share = starts[0].shape[0]
    place = place_ref[0]
    for mode in range(share):
        rates = rates_ref[place * share + mode]
        base = totals[0][mode]
        for behind in range(1, planes - 1):
            base = base + jnp.exp(-float(tokens * plane * behind) * rates) * totals[behind][mode]
        for ahead in range(plane):
            target = lax.rem(place + ahead, plane)
            start = decayed(rates, tokens * target) * base
            for behind, end in enumerate(ends):
                owner = lax.rem(place - behind + plane, plane)
                gap = target - 1 - owner
                term = decayed(rates, tokens * jnp.maximum(gap, 0)) * end[mode]
                start = start + jnp.where(gap >= 0, term, 0.0)
            starts[ahead][mode] = start


def outer_kernel(seq_total, place_ref, rim_ref, inner_ref, gate_ref, rates_ref, weights_ref, bias_ref, *rest):
    *start_refs, out_ref, store, begin = rest
    modes, plane = rates_ref.shape[0], len(start_refs)
    share = modes // plane
    for behind, ref in enumerate(start_refs):
        begin[pl.ds(lax.rem(place_ref[0] - behind + plane, plane) * share, share)] = ref[...]
    decay = [jnp.exp(-rates_ref[mode]) for mode in range(modes)]
    scaled = [weights_ref[mode] * jnp.sqrt(2.0 * rates_ref[mode] + 2.0 / seq_total) for mode in range(modes)]
    bias = bias_ref[...]
    states = tuple(begin[mode] for mode in range(modes))
    first = 0
    for source in (rim_ref, inner_ref):

        def turn(index, states, source=source, first=first):
            at = pl.multiple_of(index * STEPS * SUBS, STEPS * SUBS)
            values = source[pl.ds(at, STEPS * SUBS), :].astype(F32)
            sums = []
            for step in range(STEPS):
                value = values[step * SUBS : (step + 1) * SUBS]
                states = tuple(d * s + value for d, s in zip(decay, states))
                terms = [c * s for c, s in zip(scaled, states)] + [bias * value]
                while len(terms) > 1:
                    terms = [sum(terms[i : i + 2][1:], terms[i]) for i in range(0, len(terms), 2)]
                sums.append(terms[0])
            store[pl.ds(first * SUBS + at, STEPS * SUBS), :] = jnp.concatenate(sums, axis=0)
            return states

        count = source.shape[0] // SUBS
        states = lax.fori_loop(0, count // STEPS, turn, states)
        first += count
    for group in range(SUBS):
        rows = slice(group * LANES, (group + 1) * LANES)
        for block in range(first // BLOCK):
            cols = slice(block * BLOCK, (block + 1) * BLOCK)
            turned = store[pl.ds(block * BLOCK * SUBS + group, BLOCK, stride=SUBS), :].T
            out_ref[rows, cols] = (gate_ref[rows, cols].astype(F32) * turned).astype(BF16)


SCALAR = pl.BlockSpec(memory_space=pltpu.SMEM)


def call(kernel, tiles, in_specs, out_specs, out_shape, scratch, flops, moved, room):
    return pl.pallas_call(
        kernel,
        grid=(tiles,),
        in_specs=in_specs,
        out_specs=out_specs,
        out_shape=out_shape,
        scratch_shapes=scratch,
        compiler_params=pltpu.CompilerParams(vmem_limit_bytes=room << 20),
        cost_estimate=pl.CostEstimate(flops=flops, bytes_accessed=moved, transcendentals=0),
    )


def rows_spec(width, column=0):
    return pl.BlockSpec((TILE, width), lambda i: (i, column))


def modes_spec(modes):
    return pl.BlockSpec((modes, SUBS, LANES), lambda i: (0, i, 0))


def steps_spec(steps):
    return pl.BlockSpec((None, steps * SUBS, LANES), lambda i: (i, 0, 0))


def steps_scratch(steps):
    return pltpu.VMEM((steps * SUBS, LANES), F32)


def on_device(v_stream, gate_one, gate_two, short_filter, decay_rates, residues, skip_bias):
    real_channels, tokens = v_stream.shape
    modes = decay_rates.shape[1]
    shards = lax.axis_size("seq")
    before = lax.ppermute(v_stream[:, tokens - BLOCK :], "seq", [(i, i + 1) for i in range(shards - 1)])
    extra = -real_channels % TILE

    def padded(array):
        return jnp.pad(array, ((0, extra),) + ((0, 0),) * (array.ndim - 1)) if extra else array

    v_stream, gate_one, gate_two, short_filter = map(padded, (v_stream, gate_one, gate_two, short_filter))
    decay_rates, residues, skip_bias, before = map(padded, (decay_rates, residues, skip_bias, before))
    channels = real_channels + extra
    tiles, groups = channels // TILE, channels // LANES
    rates = decay_rates.T.reshape(modes, groups, LANES)
    weights = residues.T.reshape(modes, groups, LANES)
    bias = skip_bias.reshape(groups, LANES)
    tables = jnp.asarray(window_tables())
    tables_spec = pl.BlockSpec(tables.shape, lambda i: (0, 0))
    planes = 4 if shards % 4 == 0 else 1
    plane = shards // planes
    share = modes // plane
    place = (lax.axis_index("seq") % plane).astype(jnp.int32).reshape(1)
    inner = tokens - BLOCK
    shape = jax.ShapeDtypeStruct
    per_mode = shape((modes, groups, LANES), F32)
    piece = shape((share, groups, LANES), F32)
    spectrum, inner_mixed, inner_state = call(
        inner_kernel,
        tiles,
        [rows_spec(tokens), rows_spec(tokens), rows_spec(BLOCK), modes_spec(modes), tables_spec],
        [rows_spec(2 * BLOCK), steps_spec(inner), modes_spec(modes)],
        [shape((channels, 2 * BLOCK), F32), shape((tiles, inner * SUBS, LANES), BF16), per_mode],
        [steps_scratch(inner)],
        channels * inner * 2600,
        channels * tokens * 8,
        56,
    )(v_stream, gate_one, short_filter, rates, tables)
    rim_mixed, *ends = call(
        functools.partial(rim_kernel, inner),
        tiles,
        [SCALAR, rows_spec(BLOCK), rows_spec(BLOCK), rows_spec(BLOCK), rows_spec(2 * BLOCK)]
        + [modes_spec(modes), modes_spec(modes), tables_spec],
        [steps_spec(BLOCK)] + [modes_spec(share)] * plane,
        [shape((tiles, BLOCK * SUBS, LANES), BF16)] + [piece] * plane,
        [steps_scratch(BLOCK), pltpu.VMEM((modes, SUBS, LANES), F32)],
        channels * BLOCK * 2600,
        channels * BLOCK * 16,
        40,
    )(place, before, v_stream, gate_one, spectrum, rates, inner_state, tables)

    def round_plane(pieces):
        turned = [pieces[0]]
        for ahead in range(1, plane):
            route = [(g * plane + i, g * plane + (i + ahead) % plane) for g in range(planes) for i in range(plane)]
            turned.append(lax.ppermute(pieces[ahead], "seq", route))
        return turned

    arrived = round_plane(ends)
    pieces_spec, rates_spec = modes_spec(share), modes_spec(modes)
    total = call(
        functools.partial(total_kernel, tokens),
        tiles,
        [SCALAR, rates_spec] + [pieces_spec] * plane,
        pieces_spec,
        piece,
        [],
        1 << 20,
        1 << 18,
        4,
    )(place, rates, *arrived)
    totals = [
        lax.ppermute(total, "seq", [(i, i + step * plane) for i in range(shards - step * plane)])
        for step in range(1, planes)
    ]
    starts = call(
        functools.partial(start_kernel, tokens, planes),
        tiles,
        [SCALAR, rates_spec] + [pieces_spec] * (plane + planes - 1),
        [pieces_spec] * plane,
        [piece] * plane,
        [],
        1 << 20,
        1 << 18,
        4,
    )(place, rates, *arrived, *totals)
    starts = round_plane(starts)

    hyena_out = call(
        functools.partial(outer_kernel, tokens * shards),
        tiles,
        [SCALAR, steps_spec(BLOCK), steps_spec(inner), rows_spec(tokens), rates_spec, rates_spec]
        + [pl.BlockSpec((SUBS, LANES), lambda i: (i, 0))]
        + [pieces_spec] * plane,
        rows_spec(tokens),
        shape((channels, tokens), BF16),
        [steps_scratch(tokens), pltpu.VMEM((modes, SUBS, LANES), F32)],
        channels * tokens * 70,
        channels * tokens * 6,
        40,
    )(place, rim_mixed, inner_mixed, gate_two, rates, weights, bias, *starts)
    return hyena_out[:real_channels]


def solution(mesh):
    in_specs = (
        P("chan", "seq"),
        P("chan", "seq"),
        P("chan", "seq"),
        P("chan", None),
        P("chan", None),
        P("chan", None),
        P("chan"),
    )
    out_specs = P("chan", "seq")
    return jax.shard_map(
        on_device, mesh=mesh, in_specs=in_specs, out_specs=out_specs, check_vma=False
    )
```

```python
import functools
import math

import jax
import jax.numpy as jnp
import numpy as np
from jax import lax
from jax.experimental import pallas as pl
from jax.experimental.pallas import tpu as pltpu
from jax.sharding import PartitionSpec as P

LANES = 128
SUBS = 8
TILE = LANES * SUBS
BLOCK = 128
ROWS = 512
ROOM = 56
STEPS = 8
F32, BF16 = jnp.float32, jnp.bfloat16


def halves(table):
    high = table.astype(jnp.bfloat16)
    low = (table - high.astype(np.float64)).astype(jnp.bfloat16)
    return high, low


def window_tables():
    size = 2 * BLOCK
    phase = 2.0 * math.pi / size * np.outer(np.arange(size), np.arange(BLOCK) + 0.5)
    forward = np.concatenate([np.cos(phase), -np.sin(phase)], axis=1)
    signs = np.tile((-1.0) ** np.arange(BLOCK), 2)
    inverse = forward[BLOCK:].T / BLOCK
    even = np.concatenate(halves(forward[:BLOCK]), axis=0)
    odd = np.concatenate(halves(forward[:BLOCK] * signs), axis=0)
    back = np.concatenate(halves(inverse), axis=1)
    return np.concatenate([even, odd, back], axis=1)


EVEN, ODD, BACK = (slice(i * 2 * BLOCK, (i + 1) * 2 * BLOCK) for i in range(3))


def mm(left, right):
    return jnp.dot(left, right, preferred_element_type=F32)


def split(value):
    high = value.astype(BF16)
    return high, (value - high.astype(F32)).astype(BF16)


def twice(block):
    return jnp.concatenate([block, block], axis=1)


def parts(image):
    return image[:, :BLOCK], image[:, BLOCK:]


def apply_window(earlier, later, spectrum, tables):
    (e_re, e_im), (l_re, l_im), (h_re, h_im) = parts(earlier), parts(later), parts(spectrum)
    re, im = e_re + l_im, e_im - l_re
    high, low = split(jnp.concatenate([re * h_re - im * h_im, re * h_im + im * h_re], axis=1))
    both = mm(high, tables[:, BACK])
    return both[:, :BLOCK] + both[:, BLOCK:] + mm(low, tables[:, BACK][:, :BLOCK])


def put_mixed(store, first_row, block_at, short, gate):
    mixed = (gate.astype(F32) * short).astype(BF16).astype(F32)
    for piece in range(ROWS // LANES):
        group = first_row // LANES + piece
        turned = mixed[piece * LANES : (piece + 1) * LANES].T
        store[pl.ds(block_at * BLOCK * SUBS + group, BLOCK, stride=SUBS), :] = turned


def end_states(store, mixed_ref, rates_ref):
    modes = rates_ref.shape[0]
    steps = store.shape[0] // SUBS
    decay = [jnp.exp(-rates_ref[mode]) for mode in range(modes)]

    def turn(index, states):
        at = pl.multiple_of(index * STEPS * SUBS, STEPS * SUBS)
        values = store[pl.ds(at, STEPS * SUBS), :]
        mixed_ref[pl.ds(at, STEPS * SUBS), :] = values.astype(BF16)
        for step in range(STEPS):
            value = values[step * SUBS : (step + 1) * SUBS]
            states = tuple(d * s + value for d, s in zip(decay, states))
        return states

    zeros = tuple(jnp.zeros((SUBS, LANES), F32) for _ in range(modes))
    return lax.fori_loop(0, steps // STEPS, turn, zeros)


def inner_kernel(v_ref, gate_ref, taps_ref, rates_ref, tables, spec_ref, mixed_ref, state_ref, store):
    blocks = v_ref.shape[1] // BLOCK
    sign = 1.0 - 2.0 * (lax.broadcasted_iota(jnp.int32, (1, 2 * BLOCK), 1) % 2).astype(F32)
    for first in range(0, TILE, ROWS):
        rows = slice(first, first + ROWS)
        tap_hi, tap_lo = split(taps_ref[rows])
        spectrum = mm(twice(tap_hi), tables[:, EVEN]) + mm(tap_lo, tables[:BLOCK, EVEN])
        turned = spectrum * sign
        spec_ref[rows] = turned
        earlier = mm(twice(v_ref[rows, :BLOCK]), tables[:, EVEN])
        for block in range(1, blocks):
            at = slice(block * BLOCK, (block + 1) * BLOCK)
            later = mm(twice(v_ref[rows, at]), tables[:, ODD if block % 2 else EVEN])
            short = apply_window(earlier, later, spectrum if block % 2 else turned, tables)
            put_mixed(store, first, block - 1, short, gate_ref[rows, at])
            earlier = later
    for mode, state in enumerate(end_states(store, mixed_ref, rates_ref)):
        state_ref[mode] = state


def rim_kernel(inner, before_ref, v_ref, gate_ref, spec_ref, rates_ref, inner_ref, tables, mixed_ref, ends_ref, store):
    for first in range(0, TILE, ROWS):
        rows = slice(first, first + ROWS)
        earlier = mm(twice(before_ref[rows]), tables[:, ODD])
        later = mm(twice(v_ref[rows]), tables[:, EVEN])
        short = apply_window(earlier, later, spec_ref[rows], tables)
        put_mixed(store, first, 0, short, gate_ref[rows])
    for mode, state in enumerate(end_states(store, mixed_ref, rates_ref)):
        ends_ref[mode] = jnp.exp(-float(inner) * rates_ref[mode]) * state + inner_ref[mode]


def scan_kernel(tokens, place_ref, rates_ref, ends_ref, starts_ref):
    reach = jnp.exp(-float(tokens) * rates_ref[place_ref[0]])
    start = jnp.zeros_like(reach)
    starts_ref[0] = start
    for shard in range(1, ends_ref.shape[0]):
        start = reach * start + ends_ref[shard - 1]
        starts_ref[shard] = start


def added(terms):
    while len(terms) > 1:
        terms = [sum(terms[i : i + 2][1:], terms[i]) for i in range(0, len(terms), 2)]
    return terms[0]


def scales(rates_ref, weights_ref, seq_total):
    modes = rates_ref.shape[0]
    decay = [jnp.exp(-rates_ref[mode]) for mode in range(modes)]
    scaled = [weights_ref[mode] * jnp.sqrt(2.0 * rates_ref[mode] + 2.0 / seq_total) for mode in range(modes)]
    return decay, scaled


def local_kernel(seq_total, rim_ref, inner_ref, rates_ref, weights_ref, bias_ref, *rest):
    sums_ref = rest[-1]
    decay, scaled = scales(rates_ref, weights_ref, seq_total)
    bias = bias_ref[...]
    states = tuple(jnp.zeros((SUBS, LANES), F32) for _ in decay)
    first = 0
    for source in (rim_ref, inner_ref):

        def turn(index, states, source=source, first=first):
            at = pl.multiple_of(index * STEPS * SUBS, STEPS * SUBS)
            values = source[pl.ds(at, STEPS * SUBS), :].astype(F32)
            for step in range(STEPS):
                value = values[step * SUBS : (step + 1) * SUBS]
                states = tuple(d * s + value for d, s in zip(decay, states))
                total = added([c * s for c, s in zip(scaled, states)] + [bias * value])
                sums_ref[pl.ds(first * SUBS + at + step * SUBS, SUBS), :] = total
            return states

        count = source.shape[0] // SUBS
        states = lax.fori_loop(0, count // STEPS, turn, states)
        first += count


def outer_kernel(seq_total, sums_ref, gate_ref, rates_ref, weights_ref, start_ref, out_ref, store):
    decay, scaled = scales(rates_ref, weights_ref, seq_total)
    states = tuple(c * start_ref[mode] for mode, c in enumerate(scaled))
    steps = BLOCK // SUBS

    def carry(index, states):
        at = pl.multiple_of(index * steps * SUBS, steps * SUBS)
        for step in range(steps):
            states = tuple(d * s for d, s in zip(decay, states))
            where = pl.ds(at + step * SUBS, SUBS)
            store[where, :] = sums_ref[where, :] + added(list(states))
        return states

    def finish(block, group):
        rows = pl.ds(pl.multiple_of(group * LANES, LANES), LANES)
        cols = pl.ds(pl.multiple_of(block * BLOCK, BLOCK), BLOCK)
        turned = store[pl.ds(block * BLOCK * SUBS + group, BLOCK, stride=SUBS), :].T
        out_ref[rows, cols] = (gate_ref[rows, cols].astype(F32) * turned).astype(BF16)

    def both(index, states):
        finish(index // SUBS - 1, index % SUBS)
        return carry(index, states)

    blocks = store.shape[0] // SUBS // BLOCK
    states = lax.fori_loop(0, SUBS, carry, states)
    lax.fori_loop(SUBS, blocks * SUBS, both, states)
    for group in range(SUBS):
        finish(blocks - 1, group)


SCALAR = pl.BlockSpec(memory_space=pltpu.SMEM)
WHOLE = pl.BlockSpec(memory_space=pltpu.VMEM)


def call(kernel, tiles, in_specs, out_specs, out_shape, scratch, flops, moved, room):
    return pl.pallas_call(
        kernel,
        grid=(tiles,),
        in_specs=in_specs,
        out_specs=out_specs,
        out_shape=out_shape,
        scratch_shapes=scratch,
        compiler_params=pltpu.CompilerParams(vmem_limit_bytes=room << 20),
        cost_estimate=pl.CostEstimate(flops=flops, bytes_accessed=moved, transcendentals=0),
    )


def rows_spec(width, column=0):
    return pl.BlockSpec((TILE, width), lambda i: (i, column))


def modes_spec(modes):
    return pl.BlockSpec((modes, SUBS, LANES), lambda i: (0, i, 0))


def steps_spec(steps):
    return pl.BlockSpec((None, steps * SUBS, LANES), lambda i: (i, 0, 0))


def steps_scratch(steps):
    return pltpu.VMEM((steps * SUBS, LANES), F32)


def on_device(v_stream, gate_one, gate_two, short_filter, decay_rates, residues, skip_bias):
    real_channels, tokens = v_stream.shape
    modes = decay_rates.shape[1]
    shards = lax.axis_size("seq")
    before = lax.ppermute(v_stream[:, tokens - BLOCK :], "seq", [(i, i + 1) for i in range(shards - 1)])
    extra = -real_channels % TILE

    def padded(array):
        return jnp.pad(array, ((0, extra),) + ((0, 0),) * (array.ndim - 1)) if extra else array

    v_stream, gate_one, gate_two, short_filter = map(padded, (v_stream, gate_one, gate_two, short_filter))
    decay_rates, residues, skip_bias, before = map(padded, (decay_rates, residues, skip_bias, before))
    channels = real_channels + extra
    tiles, groups = channels // TILE, channels // LANES
    rates = decay_rates.T.reshape(modes, groups, LANES)
    weights = residues.T.reshape(modes, groups, LANES)
    bias = skip_bias.reshape(groups, LANES)
    tables = jnp.asarray(window_tables())
    tables_spec = pl.BlockSpec(tables.shape, lambda i: (0, 0))
    place = lax.axis_index("seq").astype(jnp.int32).reshape(1)
    inner = tokens - BLOCK
    seq_total = tokens * shards
    shape = jax.ShapeDtypeStruct
    per_mode = shape((modes, groups, LANES), F32)
    spectrum, inner_mixed, inner_state = call(
        inner_kernel,
        tiles,
        [rows_spec(tokens), rows_spec(tokens), rows_spec(BLOCK), modes_spec(modes), tables_spec],
        [rows_spec(2 * BLOCK), steps_spec(inner), modes_spec(modes)],
        [shape((channels, 2 * BLOCK), F32), shape((tiles, inner * SUBS, LANES), BF16), per_mode],
        [steps_scratch(inner)],
        channels * inner * 2600,
        channels * tokens * 8,
        ROOM,
    )(v_stream, gate_one, short_filter, rates, tables)
    rim_mixed, end_state = call(
        functools.partial(rim_kernel, inner),
        tiles,
        [rows_spec(BLOCK), rows_spec(BLOCK), rows_spec(BLOCK), rows_spec(2 * BLOCK)]
        + [modes_spec(modes), modes_spec(modes), tables_spec],
        [steps_spec(BLOCK), modes_spec(modes)],
        [shape((tiles, BLOCK * SUBS, LANES), BF16), per_mode],
        [steps_scratch(BLOCK)],
        channels * BLOCK * 2600,
        channels * BLOCK * 16,
        ROOM,
    )(before, v_stream, gate_one, spectrum, rates, inner_state, tables)

    def local(first, count, sums, rim_mixed, inner_mixed):
        def shifted(spec):
            return pl.BlockSpec(spec.block_shape, lambda i: spec.index_map(i + first))

        return pl.pallas_call(
            functools.partial(local_kernel, seq_total),
            grid=(count,),
            in_specs=[
                shifted(steps_spec(BLOCK)),
                shifted(steps_spec(inner)),
                shifted(modes_spec(modes)),
                shifted(modes_spec(modes)),
                shifted(pl.BlockSpec((SUBS, LANES), lambda i: (i, 0))),
            ]
            + [pl.BlockSpec(memory_space=pl.ANY)] * len(sums),
            out_specs=shifted(steps_spec(tokens)),
            out_shape=shape((tiles, tokens * SUBS, LANES), F32),
            input_output_aliases={5: 0} if sums else {},
            compiler_params=pltpu.CompilerParams(vmem_limit_bytes=ROOM << 20),
            cost_estimate=pl.CostEstimate(
                flops=count * TILE * tokens * 70, bytes_accessed=count * TILE * tokens * 6, transcendentals=0
            ),
        )(rim_mixed, inner_mixed, rates, weights, bias, *sums)

    moved = lax.all_to_all(end_state.reshape(shards, -1, LANES), "seq", split_axis=0, concat_axis=0, tiled=True)
    early = (tiles + 1) // 2
    sums = local(0, early, (), rim_mixed, inner_mixed)
    moved, sums = lax.optimization_barrier((moved, sums))
    carried = pl.pallas_call(
        functools.partial(scan_kernel, tokens),
        in_specs=[SCALAR, WHOLE, WHOLE],
        out_specs=WHOLE,
        out_shape=shape(moved.shape, F32),
        compiler_params=pltpu.CompilerParams(vmem_limit_bytes=4 << 20),
    )(place, rates.reshape(moved.shape), moved)
    start = lax.all_to_all(carried, "seq", split_axis=0, concat_axis=0, tiled=True).reshape(per_mode.shape)

    if early < tiles:
        rim_later, inner_later, _ = lax.optimization_barrier((rim_mixed, inner_mixed, carried))
        sums = local(early, tiles - early, (sums,), rim_later, inner_later)

    hyena_out = call(
        functools.partial(outer_kernel, seq_total),
        tiles,
        [steps_spec(tokens), rows_spec(tokens)] + [modes_spec(modes)] * 3,
        rows_spec(tokens),
        shape((channels, tokens), BF16),
        [steps_scratch(tokens)],
        channels * tokens * 40,
        channels * tokens * 8,
        ROOM,
    )(sums, gate_two, rates, weights, start)
    return hyena_out[:real_channels]


def solution(mesh):
    in_specs = (
        P("chan", "seq"),
        P("chan", "seq"),
        P("chan", "seq"),
        P("chan", None),
        P("chan", None),
        P("chan", None),
        P("chan"),
    )
    out_specs = P("chan", "seq")
    return jax.shard_map(
        on_device, mesh=mesh, in_specs=in_specs, out_specs=out_specs, check_vma=False
    )
```

```python
import functools
import math

import jax
import jax.numpy as jnp
import numpy as np
from jax import lax
from jax.experimental import pallas as pl
from jax.experimental.pallas import tpu as pltpu
from jax.sharding import PartitionSpec as P

LANES = 128
SUBS = 8
TILE = LANES * SUBS
BLOCK = 128
ROWS = 1024
STEPS = 8
F32, BF16 = jnp.float32, jnp.bfloat16


def halves(table):
    high = table.astype(jnp.bfloat16)
    low = (table - high.astype(np.float64)).astype(jnp.bfloat16)
    return high, low


def window_tables():
    size = 2 * BLOCK
    phase = 2.0 * math.pi / size * np.outer(np.arange(size), np.arange(BLOCK) + 0.5)
    forward = np.concatenate([np.cos(phase), -np.sin(phase)], axis=1)
    signs = np.tile((-1.0) ** np.arange(BLOCK), 2)
    inverse = forward[BLOCK:].T / BLOCK
    even = np.concatenate(halves(forward[:BLOCK]), axis=0)
    odd = np.concatenate(halves(forward[:BLOCK] * signs), axis=0)
    back = np.concatenate(halves(inverse), axis=1)
    return np.concatenate([even, odd, back], axis=1)


EVEN, ODD, BACK = (slice(i * 2 * BLOCK, (i + 1) * 2 * BLOCK) for i in range(3))


def mm(left, right):
    return jnp.dot(left, right, preferred_element_type=F32)


def split(value):
    high = value.astype(BF16)
    return high, (value - high.astype(F32)).astype(BF16)


def twice(block):
    return jnp.concatenate([block, block], axis=1)


def parts(image):
    return image[:, :BLOCK], image[:, BLOCK:]


def apply_window(earlier, later, spectrum, tables):
    (e_re, e_im), (l_re, l_im), (h_re, h_im) = parts(earlier), parts(later), parts(spectrum)
    re, im = e_re + l_im, e_im - l_re
    high, low = split(jnp.concatenate([re * h_re - im * h_im, re * h_im + im * h_re], axis=1))
    both = mm(high, tables[:, BACK])
    return both[:, :BLOCK] + both[:, BLOCK:] + mm(low, tables[:, BACK][:, :BLOCK])


def put_mixed(store, first_row, block_at, short, gate):
    mixed = (gate.astype(F32) * short).astype(BF16).astype(F32)
    for piece in range(ROWS // LANES):
        group = first_row // LANES + piece
        turned = mixed[piece * LANES : (piece + 1) * LANES].T
        store[pl.ds(block_at * BLOCK * SUBS + group, BLOCK, stride=SUBS), :] = turned


def lay_out(rows_ref, store):
    modes = rows_ref.shape[0]
    for group in range(SUBS):
        store[pl.ds(group, modes, stride=SUBS), :] = rows_ref[:, group * LANES : (group + 1) * LANES]


def end_states(store, mixed_ref, rates_ref):
    modes = rates_ref.shape[0]
    steps = store.shape[0] // SUBS
    decay = [jnp.exp(-rates_ref[mode]) for mode in range(modes)]

    def turn(index, states):
        at = pl.multiple_of(index * STEPS * SUBS, STEPS * SUBS)
        values = store[pl.ds(at, STEPS * SUBS), :]
        mixed_ref[pl.ds(at, STEPS * SUBS), :] = values.astype(BF16)
        for step in range(STEPS):
            value = values[step * SUBS : (step + 1) * SUBS]
            states = tuple(d * s + value for d, s in zip(decay, states))
        return states

    zeros = tuple(jnp.zeros((SUBS, LANES), F32) for _ in range(modes))
    return lax.fori_loop(0, steps // STEPS, turn, zeros)


def inner_kernel(v_ref, gate_ref, taps_ref, raw_ref, tables, spec_ref, mixed_ref, state_ref, rates_ref, store, laid):
    lay_out(raw_ref, laid)
    rates_ref[...] = laid[...].reshape(rates_ref.shape)
    blocks = v_ref.shape[1] // BLOCK
    sign = 1.0 - 2.0 * (lax.broadcasted_iota(jnp.int32, (1, 2 * BLOCK), 1) % 2).astype(F32)
    for first in range(0, TILE, ROWS):
        rows = slice(first, first + ROWS)
        tap_hi, tap_lo = split(taps_ref[rows])
        spectrum = mm(twice(tap_hi), tables[:, EVEN]) + mm(tap_lo, tables[:BLOCK, EVEN])
        turned = spectrum * sign
        spec_ref[rows] = turned
        earlier = mm(twice(v_ref[rows, :BLOCK]), tables[:, EVEN])
        for block in range(1, blocks):
            at = slice(block * BLOCK, (block + 1) * BLOCK)
            later = mm(twice(v_ref[rows, at]), tables[:, ODD if block % 2 else EVEN])
            short = apply_window(earlier, later, spectrum if block % 2 else turned, tables)
            put_mixed(store, first, block - 1, short, gate_ref[rows, at])
            earlier = later
    for mode, state in enumerate(end_states(store, mixed_ref, rates_ref)):
        state_ref[mode] = state


def rim_kernel(inner, place_ref, before_ref, v_ref, gate_ref, spec_ref, rates_ref, inner_ref, tables, *rest):
    mixed_ref, *piece_refs, store, ends = rest
    for first in range(0, TILE, ROWS):
        rows = slice(first, first + ROWS)
        earlier = mm(twice(before_ref[rows]), tables[:, ODD])
        later = mm(twice(v_ref[rows]), tables[:, EVEN])
        short = apply_window(earlier, later, spec_ref[rows], tables)
        put_mixed(store, first, 0, short, gate_ref[rows])
    for mode, state in enumerate(end_states(store, mixed_ref, rates_ref)):
        ends[mode] = jnp.exp(-float(inner) * rates_ref[mode]) * state + inner_ref[mode]
    plane = len(piece_refs)
    share = ends.shape[0] // plane
    for ahead, piece in enumerate(piece_refs):
        piece[...] = ends[pl.ds((place_ref[0] + ahead) % plane * share, share)]


def decayed(rates, positions):
    return jnp.exp(-lax.convert_element_type(positions, F32) * rates)


def chip_kernel(tokens, place_ref, rates_ref, mine_ref, other_ref, total_ref):
    half = total_ref.shape[0]
    core = place_ref[0] % 2
    rates = rates_ref[pl.ds(core * half, half)]
    total_ref[...] = decayed(rates, tokens * (1 - core)) * mine_ref[...] + decayed(rates, tokens * core) * other_ref[...]


def level_kernel(tokens, size, place_ref, rates_ref, total_ref, other_ref, before_ref, joined_ref, after_ref):
    half = total_ref.shape[0]
    place = place_ref[0]
    upper = place // size % 2
    rates = rates_ref[pl.ds(place % 2 * half, half)]
    joined_ref[...] = (
        decayed(rates, tokens * size * (1 - upper)) * total_ref[...]
        + decayed(rates, tokens * size * upper) * other_ref[...]
    )
    reach = decayed(rates, tokens * (place % size // 2 * 2)) * other_ref[...]
    after_ref[...] = before_ref[...] + jnp.where(upper == 1, reach, 0.0)


def start_kernel(tokens, size, place_ref, rates_ref, other_ref, before_ref, own_ref, twin_ref, mine_ref, twins_ref):
    half = own_ref.shape[0]
    place = place_ref[0]
    core = place % 2
    upper = place // size % 2
    rates = rates_ref[pl.ds(core * half, half)]
    reach = decayed(rates, tokens * (place % size // 2 * 2)) * other_ref[...]
    first = before_ref[...] + jnp.where(upper == 1, reach, 0.0)
    second = decayed(rates, tokens) * first + jnp.where(core == 0, own_ref[...], twin_ref[...])
    mine_ref[...] = jnp.where(core == 0, first, second)
    twins_ref[...] = jnp.where(core == 0, second, first)


def outer_kernel(seq_total, place_ref, rim_ref, inner_ref, gate_ref, rates_ref, raw_ref, bias_ref, *rest):
    *start_refs, out_ref, store, begin, laid = rest
    lay_out(raw_ref, laid)
    modes, plane = rates_ref.shape[0], len(start_refs)
    share = modes // plane
    for behind, ref in enumerate(start_refs):
        begin[pl.ds((place_ref[0] + behind) % plane * share, share)] = ref[...]
    decay = [jnp.exp(-rates_ref[mode]) for mode in range(modes)]
    weights = [laid[mode * SUBS : (mode + 1) * SUBS] for mode in range(modes)]
    scaled = [weights[mode] * jnp.sqrt(2.0 * rates_ref[mode] + 2.0 / seq_total) for mode in range(modes)]
    bias = bias_ref[...]
    states = tuple(begin[mode] for mode in range(modes))
    first = 0
    for source in (rim_ref, inner_ref):

        def turn(index, states, source=source, first=first):
            at = pl.multiple_of(index * STEPS * SUBS, STEPS * SUBS)
            values = source[pl.ds(at, STEPS * SUBS), :].astype(F32)
            sums = []
            for step in range(STEPS):
                value = values[step * SUBS : (step + 1) * SUBS]
                states = tuple(d * s + value for d, s in zip(decay, states))
                terms = [c * s for c, s in zip(scaled, states)] + [bias * value]
                while len(terms) > 1:
                    terms = [sum(terms[i : i + 2][1:], terms[i]) for i in range(0, len(terms), 2)]
                sums.append(terms[0])
            store[pl.ds(first * SUBS + at, STEPS * SUBS), :] = jnp.concatenate(sums, axis=0)
            return states

        count = source.shape[0] // SUBS
        states = lax.fori_loop(0, count // STEPS, turn, states)
        first += count
    for group in range(SUBS):
        rows = slice(group * LANES, (group + 1) * LANES)
        for block in range(first // BLOCK):
            cols = slice(block * BLOCK, (block + 1) * BLOCK)
            turned = store[pl.ds(block * BLOCK * SUBS + group, BLOCK, stride=SUBS), :].T
            out_ref[rows, cols] = (gate_ref[rows, cols].astype(F32) * turned).astype(BF16)


SCALAR = pl.BlockSpec(memory_space=pltpu.SMEM)
WHOLE = pl.BlockSpec(memory_space=pltpu.VMEM)
RIM_ROOM = 40


def call(kernel, tiles, in_specs, out_specs, out_shape, scratch, flops, moved, room):
    return pl.pallas_call(
        kernel,
        grid=(tiles,),
        in_specs=in_specs,
        out_specs=out_specs,
        out_shape=out_shape,
        scratch_shapes=scratch,
        compiler_params=pltpu.CompilerParams(vmem_limit_bytes=room << 20),
        cost_estimate=pl.CostEstimate(flops=flops, bytes_accessed=moved, transcendentals=0),
    )


def rows_spec(width, column=0):
    return pl.BlockSpec((TILE, width), lambda i: (i, column))


def modes_spec(modes):
    return pl.BlockSpec((modes, SUBS, LANES), lambda i: (0, i, 0))


def steps_spec(steps):
    return pl.BlockSpec((None, steps * SUBS, LANES), lambda i: (i, 0, 0))


def steps_scratch(steps):
    return pltpu.VMEM((steps * SUBS, LANES), F32)


def on_device(v_stream, gate_one, gate_two, short_filter, decay_rates, residues, skip_bias):
    real_channels, tokens = v_stream.shape
    modes = decay_rates.shape[1]
    shards = lax.axis_size("seq")
    before = lax.ppermute(v_stream[:, tokens - BLOCK :], "seq", [(i, i + 1) for i in range(shards - 1)])
    extra = -real_channels % TILE

    def padded(array):
        return jnp.pad(array, ((0, extra),) + ((0, 0),) * (array.ndim - 1)) if extra else array

    v_stream, gate_one, gate_two, short_filter = map(padded, (v_stream, gate_one, gate_two, short_filter))
    decay_rates, residues, skip_bias, before = map(padded, (decay_rates, residues, skip_bias, before))
    channels = real_channels + extra
    tiles, groups = channels // TILE, channels // LANES
    raw_rates, raw_weights = decay_rates.T, residues.T
    bias = skip_bias.reshape(groups, LANES)
    tables = jnp.asarray(window_tables())
    tables_spec = pl.BlockSpec(tables.shape, lambda i: (0, 0))
    place = lax.axis_index("seq").astype(jnp.int32).reshape(1)
    inner = tokens - BLOCK
    shape = jax.ShapeDtypeStruct
    per_mode = shape((modes, groups, LANES), F32)
    half = shape((modes // 2, groups, LANES), F32)
    raw_spec = pl.BlockSpec((modes, TILE), lambda i: (0, i))
    rates_spec, half_spec = modes_spec(modes), modes_spec(modes // 2)
    laid = pltpu.VMEM((modes * SUBS, LANES), F32)
    spectrum, inner_mixed, inner_state, rates = call(
        inner_kernel,
        tiles,
        [rows_spec(tokens), rows_spec(tokens), rows_spec(BLOCK), raw_spec, tables_spec],
        [rows_spec(2 * BLOCK), steps_spec(inner), rates_spec, rates_spec],
        [shape((channels, 2 * BLOCK), F32), shape((tiles, inner * SUBS, LANES), BF16), per_mode, per_mode],
        [steps_scratch(inner), laid],
        channels * inner * 2600,
        channels * tokens * 8,
        56,
    )(v_stream, gate_one, short_filter, raw_rates, tables)
    rim_mixed, own_end, twin_half = call(
        functools.partial(rim_kernel, inner),
        tiles,
        [SCALAR, rows_spec(BLOCK), rows_spec(BLOCK), rows_spec(BLOCK), rows_spec(2 * BLOCK)]
        + [rates_spec, rates_spec, tables_spec],
        [steps_spec(BLOCK), half_spec, half_spec],
        [shape((tiles, BLOCK * SUBS, LANES), BF16), half, half],
        [steps_scratch(BLOCK), pltpu.VMEM((modes, SUBS, LANES), F32)],
        channels * BLOCK * 2600,
        channels * BLOCK * 16,
        RIM_ROOM,
    )(place, before, v_stream, gate_one, spectrum, rates, inner_state, tables)

    def swap(array, distance):
        return lax.ppermute(array, "seq", [(i, i ^ distance) for i in range(shards)])

    def small(kernel, outputs, *arrays):
        return pl.pallas_call(
            kernel,
            in_specs=[SCALAR] + [WHOLE] * (len(arrays) + 1),
            out_specs=[WHOLE] * outputs,
            out_shape=[half] * outputs,
            compiler_params=pltpu.CompilerParams(vmem_limit_bytes=8 << 20),
        )(place, rates, *arrays)

    twin_end = swap(twin_half, 1)
    (total,) = small(functools.partial(chip_kernel, tokens), 1, own_end, twin_end)
    ahead = jnp.zeros(half.shape, F32)
    size = 2
    while 2 * size < shards:
        total, ahead = small(functools.partial(level_kernel, tokens, size), 2, total, swap(total, size), ahead)
        size *= 2
    mine, twins = small(
        functools.partial(start_kernel, tokens, size), 2, swap(total, size), ahead, own_end, twin_end
    )
    starts = [mine, swap(twins, 1)]

    hyena_out = call(
        functools.partial(outer_kernel, tokens * shards),
        tiles,
        [SCALAR, steps_spec(BLOCK), steps_spec(inner), rows_spec(tokens), rates_spec, raw_spec]
        + [pl.BlockSpec((SUBS, LANES), lambda i: (i, 0))]
        + [half_spec] * 2,
        rows_spec(tokens),
        shape((channels, tokens), BF16),
        [steps_scratch(tokens), pltpu.VMEM((modes, SUBS, LANES), F32), laid],
        channels * tokens * 70,
        channels * tokens * 6,
        40,
    )(place, rim_mixed, inner_mixed, gate_two, rates, raw_weights, bias, *starts)
    return hyena_out[:real_channels]


def solution(mesh):
    in_specs = (
        P("chan", "seq"),
        P("chan", "seq"),
        P("chan", "seq"),
        P("chan", None),
        P("chan", None),
        P("chan", None),
        P("chan"),
    )
    out_specs = P("chan", "seq")
    return jax.shard_map(
        on_device, mesh=mesh, in_specs=in_specs, out_specs=out_specs, check_vma=False
    )
```

```python
import functools
import math

import jax
import jax.numpy as jnp
import numpy as np
from jax import lax
from jax.experimental import pallas as pl
from jax.experimental.pallas import tpu as pltpu
from jax.sharding import PartitionSpec as P

LANES = 128
SUBS = 8
TILE = LANES * SUBS
BLOCK = 128
ROWS = 1024
STEPS = 8
F32, BF16 = jnp.float32, jnp.bfloat16


def halves(table):
    high = table.astype(jnp.bfloat16)
    low = (table - high.astype(np.float64)).astype(jnp.bfloat16)
    return high, low


def window_tables():
    size = 2 * BLOCK
    phase = 2.0 * math.pi / size * np.outer(np.arange(size), np.arange(BLOCK) + 0.5)
    forward = np.concatenate([np.cos(phase), -np.sin(phase)], axis=1)
    signs = np.tile((-1.0) ** np.arange(BLOCK), 2)
    inverse = forward[BLOCK:].T / BLOCK
    even = np.concatenate(halves(forward[:BLOCK]), axis=0)
    odd = np.concatenate(halves(forward[:BLOCK] * signs), axis=0)
    back = np.concatenate(halves(inverse), axis=1)
    return np.concatenate([even, odd, back], axis=1)


EVEN, ODD, BACK = (slice(i * 2 * BLOCK, (i + 1) * 2 * BLOCK) for i in range(3))


def mm(left, right):
    return jnp.dot(left, right, preferred_element_type=F32)


def split(value):
    high = value.astype(BF16)
    return high, (value - high.astype(F32)).astype(BF16)


def twice(block):
    return jnp.concatenate([block, block], axis=1)


def parts(image):
    return image[:, :BLOCK], image[:, BLOCK:]


def apply_window(earlier, later, spectrum, tables):
    (e_re, e_im), (l_re, l_im), (h_re, h_im) = parts(earlier), parts(later), parts(spectrum)
    re, im = e_re + l_im, e_im - l_re
    high, low = split(jnp.concatenate([re * h_re - im * h_im, re * h_im + im * h_re], axis=1))
    both = mm(high, tables[:, BACK])
    return both[:, :BLOCK] + both[:, BLOCK:] + mm(low, tables[:, BACK][:, :BLOCK])


def put_mixed(store, first_row, block_at, short, gate):
    mixed = (gate.astype(F32) * short).astype(BF16).astype(F32)
    for piece in range(ROWS // LANES):
        group = first_row // LANES + piece
        turned = mixed[piece * LANES : (piece + 1) * LANES].T
        store[pl.ds(block_at * BLOCK * SUBS + group, BLOCK, stride=SUBS), :] = turned


def lay_out(rows_ref, store):
    modes = rows_ref.shape[0]
    for group in range(SUBS):
        store[pl.ds(group, modes, stride=SUBS), :] = rows_ref[:, group * LANES : (group + 1) * LANES]


def end_states(store, mixed_ref, rates_ref):
    modes = rates_ref.shape[0]
    steps = store.shape[0] // SUBS
    decay = [jnp.exp(-rates_ref[mode]) for mode in range(modes)]

    def turn(index, states):
        at = pl.multiple_of(index * STEPS * SUBS, STEPS * SUBS)
        values = store[pl.ds(at, STEPS * SUBS), :]
        mixed_ref[pl.ds(at, STEPS * SUBS), :] = values.astype(BF16)
        for step in range(STEPS):
            value = values[step * SUBS : (step + 1) * SUBS]
            states = tuple(d * s + value for d, s in zip(decay, states))
        return states

    zeros = tuple(jnp.zeros((SUBS, LANES), F32) for _ in range(modes))
    return lax.fori_loop(0, steps // STEPS, turn, zeros)


def inner_kernel(
    v_hbm, gate_hbm, taps_hbm, raw_hbm, tables_hbm,
    spec_ref, mixed_ref, state_ref, rates_ref, v_first, gate_first, tables,
    v_rest, gate_rest, taps, raw, store, laid, sems,
):
    tiles, inner = mixed_ref.shape[0], v_rest.shape[1]

    def copies(tile):
        rows = pl.ds(tile * TILE, TILE)
        pairs = [(taps_hbm.at[rows], taps.at[rows])]
        for whole, head, rest in ((v_hbm, v_first, v_rest), (gate_hbm, gate_first, gate_rest)):
            pairs.append((whole.at[rows, pl.ds(0, BLOCK)], head.at[rows]))
            pairs.append((whole.at[rows, pl.ds(BLOCK, inner)], rest.at[rows]))
        return [pltpu.make_async_copy(*pair, sems.at[tile * 5 + i]) for i, pair in enumerate(pairs)]

    small = [
        pltpu.make_async_copy(tables_hbm, tables, sems.at[tiles * 5]),
        pltpu.make_async_copy(raw_hbm, raw, sems.at[tiles * 5 + 1]),
    ]
    large = [copies(tile) for tile in range(tiles)]
    for copy in small + sum(large, []):
        copy.start()
    small[0].wait()
    sign = 1.0 - 2.0 * (lax.broadcasted_iota(jnp.int32, (1, 2 * BLOCK), 1) % 2).astype(F32)
    for tile in range(tiles):
        rows = slice(tile * TILE, (tile + 1) * TILE)
        groups = slice(tile * SUBS, (tile + 1) * SUBS)
        large[tile][0].wait()
        tap_hi, tap_lo = split(taps[rows])
        spectrum = mm(twice(tap_hi), tables[:, EVEN]) + mm(tap_lo, tables[:BLOCK, EVEN])
        turned = spectrum * sign
        spec_ref[rows] = turned
        for copy in large[tile][1:]:
            copy.wait()
        earlier = mm(twice(v_first[rows]), tables[:, EVEN])
        for block in range(1, inner // BLOCK + 1):
            at = slice((block - 1) * BLOCK, block * BLOCK)
            later = mm(twice(v_rest[rows, at]), tables[:, ODD if block % 2 else EVEN])
            short = apply_window(earlier, later, spectrum if block % 2 else turned, tables)
            put_mixed(store, 0, block - 1, short, gate_rest[rows, at])
            earlier = later
        if tile == 0:
            small[1].wait()
        lay_out(raw.at[:, pl.ds(tile * TILE, TILE)], laid)
        modes = raw.shape[0]
        rates_ref[:, groups] = laid[...].reshape(modes, SUBS, LANES)
        for mode, state in enumerate(end_states(store, mixed_ref.at[tile], rates_ref.at[:, groups])):
            state_ref[mode, groups] = state


def rim_kernel(inner, place_ref, before_ref, v_ref, gate_ref, spec_ref, rates_ref, inner_ref, tables, *rest):
    mixed_ref, own_ref, twin_ref, store, ends = rest
    half = own_ref.shape[0]
    core = place_ref[0] % 2
    for tile in range(mixed_ref.shape[0]):
        rows = slice(tile * TILE, (tile + 1) * TILE)
        groups = slice(tile * SUBS, (tile + 1) * SUBS)
        earlier = mm(twice(before_ref[rows]), tables[:, ODD])
        later = mm(twice(v_ref[rows]), tables[:, EVEN])
        short = apply_window(earlier, later, spec_ref[rows], tables)
        put_mixed(store, 0, 0, short, gate_ref[rows])
        rates = rates_ref.at[:, groups]
        for mode, state in enumerate(end_states(store, mixed_ref.at[tile], rates)):
            ends[mode] = jnp.exp(-float(inner) * rates[mode]) * state + inner_ref[mode, groups]
        own_ref[:, groups] = ends[pl.ds(core * half, half)]
        twin_ref[:, groups] = ends[pl.ds((1 - core) * half, half)]


def decayed(rates, positions):
    return jnp.exp(-lax.convert_element_type(positions, F32) * rates)


def chip_kernel(tokens, place_ref, rates_ref, mine_ref, other_ref, total_ref):
    half = total_ref.shape[0]
    core = place_ref[0] % 2
    rates = rates_ref[pl.ds(core * half, half)]
    total_ref[...] = decayed(rates, tokens * (1 - core)) * mine_ref[...] + decayed(rates, tokens * core) * other_ref[...]


def level_kernel(tokens, size, place_ref, rates_ref, total_ref, other_ref, before_ref, joined_ref, after_ref):
    half = total_ref.shape[0]
    place = place_ref[0]
    upper = place // size % 2
    rates = rates_ref[pl.ds(place % 2 * half, half)]
    joined_ref[...] = (
        decayed(rates, tokens * size * (1 - upper)) * total_ref[...]
        + decayed(rates, tokens * size * upper) * other_ref[...]
    )
    reach = decayed(rates, tokens * (place % size // 2 * 2)) * other_ref[...]
    after_ref[...] = before_ref[...] + jnp.where(upper == 1, reach, 0.0)


def start_kernel(tokens, size, place_ref, rates_ref, other_ref, before_ref, own_ref, twin_ref, mine_ref, twins_ref):
    half = own_ref.shape[0]
    place = place_ref[0]
    core = place % 2
    upper = place // size % 2
    rates = rates_ref[pl.ds(core * half, half)]
    reach = decayed(rates, tokens * (place % size // 2 * 2)) * other_ref[...]
    first = before_ref[...] + jnp.where(upper == 1, reach, 0.0)
    second = decayed(rates, tokens) * first + jnp.where(core == 0, own_ref[...], twin_ref[...])
    mine_ref[...] = jnp.where(core == 0, first, second)
    twins_ref[...] = jnp.where(core == 0, second, first)


def outer_kernel(seq_total, place_ref, rim_ref, inner_ref, gate_ref, rates_ref, raw_ref, bias_ref, *rest):
    *start_refs, out_ref, store, begin, laid = rest
    lay_out(raw_ref, laid)
    modes, plane = rates_ref.shape[0], len(start_refs)
    share = modes // plane
    for behind, ref in enumerate(start_refs):
        begin[pl.ds((place_ref[0] + behind) % plane * share, share)] = ref[...]
    decay = [jnp.exp(-rates_ref[mode]) for mode in range(modes)]
    weights = [laid[mode * SUBS : (mode + 1) * SUBS] for mode in range(modes)]
    scaled = [weights[mode] * jnp.sqrt(2.0 * rates_ref[mode] + 2.0 / seq_total) for mode in range(modes)]
    bias = bias_ref[...]
    states = tuple(begin[mode] for mode in range(modes))
    first = 0
    for source in (rim_ref, inner_ref):

        def turn(index, states, source=source, first=first):
            at = pl.multiple_of(index * STEPS * SUBS, STEPS * SUBS)
            values = source[pl.ds(at, STEPS * SUBS), :].astype(F32)
            sums = []
            for step in range(STEPS):
                value = values[step * SUBS : (step + 1) * SUBS]
                states = tuple(d * s + value for d, s in zip(decay, states))
                terms = [c * s for c, s in zip(scaled, states)] + [bias * value]
                while len(terms) > 1:
                    terms = [sum(terms[i : i + 2][1:], terms[i]) for i in range(0, len(terms), 2)]
                sums.append(terms[0])
            store[pl.ds(first * SUBS + at, STEPS * SUBS), :] = jnp.concatenate(sums, axis=0)
            return states

        count = source.shape[0] // SUBS
        states = lax.fori_loop(0, count // STEPS, turn, states)
        first += count
    for group in range(SUBS):
        rows = slice(group * LANES, (group + 1) * LANES)
        for block in range(first // BLOCK):
            cols = slice(block * BLOCK, (block + 1) * BLOCK)
            turned = store[pl.ds(block * BLOCK * SUBS + group, BLOCK, stride=SUBS), :].T
            out_ref[rows, cols] = (gate_ref[rows, cols].astype(F32) * turned).astype(BF16)


SCALAR = pl.BlockSpec(memory_space=pltpu.SMEM)
WHOLE = pl.BlockSpec(memory_space=pltpu.VMEM)
FAR = pl.BlockSpec(memory_space=pltpu.HBM)
INNER_ROOM, RIM_ROOM = 32, 24


def call(kernel, tiles, in_specs, out_specs, out_shape, scratch, flops, moved, room):
    return pl.pallas_call(
        kernel,
        grid=(tiles,),
        in_specs=in_specs,
        out_specs=out_specs,
        out_shape=out_shape,
        scratch_shapes=scratch,
        compiler_params=pltpu.CompilerParams(vmem_limit_bytes=room << 20),
        cost_estimate=pl.CostEstimate(flops=flops, bytes_accessed=moved, transcendentals=0),
    )


def rows_spec(width, column=0):
    return pl.BlockSpec((TILE, width), lambda i: (i, column))


def modes_spec(modes):
    return pl.BlockSpec((modes, SUBS, LANES), lambda i: (0, i, 0))


def steps_spec(steps):
    return pl.BlockSpec((None, steps * SUBS, LANES), lambda i: (i, 0, 0))


def steps_scratch(steps):
    return pltpu.VMEM((steps * SUBS, LANES), F32)


def kept_far(array):
    return pltpu.with_memory_space_constraint(array, pltpu.HBM)


def on_device(v_stream, gate_one, gate_two, short_filter, decay_rates, residues, skip_bias):
    real_channels, tokens = v_stream.shape
    modes = decay_rates.shape[1]
    shards = lax.axis_size("seq")
    before = lax.ppermute(v_stream[:, tokens - BLOCK :], "seq", [(i, i + 1) for i in range(shards - 1)])
    extra = -real_channels % TILE

    def padded(array):
        return jnp.pad(array, ((0, extra),) + ((0, 0),) * (array.ndim - 1)) if extra else array

    v_stream, gate_one, gate_two, short_filter = map(padded, (v_stream, gate_one, gate_two, short_filter))
    decay_rates, residues, skip_bias, before = map(padded, (decay_rates, residues, skip_bias, before))
    channels = real_channels + extra
    tiles, groups = channels // TILE, channels // LANES
    raw_rates, raw_weights = decay_rates.T, residues.T
    bias = skip_bias.reshape(groups, LANES)
    tables = jnp.asarray(window_tables())
    place = lax.axis_index("seq").astype(jnp.int32).reshape(1)
    inner = tokens - BLOCK
    shape = jax.ShapeDtypeStruct
    per_mode = shape((modes, groups, LANES), F32)
    half = shape((modes // 2, groups, LANES), F32)
    raw_spec = pl.BlockSpec((modes, TILE), lambda i: (0, i))
    rates_spec, half_spec = modes_spec(modes), modes_spec(modes // 2)
    laid = pltpu.VMEM((modes * SUBS, LANES), F32)
    tap_spectra = shape((channels, 2 * BLOCK), F32)
    head = shape((channels, BLOCK), BF16)
    spectrum, inner_mixed, inner_state, rates, v_first, gate_first, tables = pl.pallas_call(
        inner_kernel,
        in_specs=[FAR] * 5,
        out_specs=[WHOLE] * 7,
        out_shape=[tap_spectra, shape((tiles, inner * SUBS, LANES), BF16), per_mode, per_mode, head, head]
        + [shape(tables.shape, BF16)],
        scratch_shapes=[
            pltpu.VMEM((channels, inner), BF16),
            pltpu.VMEM((channels, inner), BF16),
            pltpu.VMEM((channels, BLOCK), F32),
            pltpu.VMEM((modes, channels), F32),
            steps_scratch(inner),
            laid,
            pltpu.SemaphoreType.DMA((tiles * 5 + 2,)),
        ],
        compiler_params=pltpu.CompilerParams(vmem_limit_bytes=INNER_ROOM << 20),
        cost_estimate=pl.CostEstimate(
            flops=channels * inner * 2600, bytes_accessed=channels * tokens * 8, transcendentals=0
        ),
    )(*map(kept_far, (v_stream, gate_one, short_filter, raw_rates, tables)))
    rim_mixed, own_end, twin_half = pl.pallas_call(
        functools.partial(rim_kernel, inner),
        in_specs=[SCALAR] + [WHOLE] * 7,
        out_specs=[WHOLE] * 3,
        out_shape=[shape((tiles, BLOCK * SUBS, LANES), BF16), half, half],
        scratch_shapes=[steps_scratch(BLOCK), pltpu.VMEM((modes, SUBS, LANES), F32)],
        compiler_params=pltpu.CompilerParams(vmem_limit_bytes=RIM_ROOM << 20),
        cost_estimate=pl.CostEstimate(
            flops=channels * BLOCK * 2600, bytes_accessed=channels * BLOCK * 16, transcendentals=0
        ),
    )(place, before, v_first, gate_first, spectrum, rates, inner_state, tables)

    def swap(array, distance):
        return lax.ppermute(array, "seq", [(i, i ^ distance) for i in range(shards)])

    def small(kernel, outputs, *arrays):
        return pl.pallas_call(
            kernel,
            in_specs=[SCALAR] + [WHOLE] * (len(arrays) + 1),
            out_specs=[WHOLE] * outputs,
            out_shape=[half] * outputs,
            compiler_params=pltpu.CompilerParams(vmem_limit_bytes=8 << 20),
        )(place, rates, *arrays)

    twin_end = swap(twin_half, 1)
    (total,) = small(functools.partial(chip_kernel, tokens), 1, own_end, twin_end)
    ahead = jnp.zeros(half.shape, F32)
    size = 2
    while 2 * size < shards:
        total, ahead = small(functools.partial(level_kernel, tokens, size), 2, total, swap(total, size), ahead)
        size *= 2
    mine, twins = small(
        functools.partial(start_kernel, tokens, size), 2, swap(total, size), ahead, own_end, twin_end
    )
    starts = [mine, swap(twins, 1)]

    hyena_out = call(
        functools.partial(outer_kernel, tokens * shards),
        tiles,
        [SCALAR, steps_spec(BLOCK), steps_spec(inner), rows_spec(tokens), rates_spec, raw_spec]
        + [pl.BlockSpec((SUBS, LANES), lambda i: (i, 0))]
        + [half_spec] * 2,
        rows_spec(tokens),
        shape((channels, tokens), BF16),
        [steps_scratch(tokens), pltpu.VMEM((modes, SUBS, LANES), F32), laid],
        channels * tokens * 70,
        channels * tokens * 6,
        32,
    )(place, rim_mixed, inner_mixed, gate_two, rates, raw_weights, bias, *starts)
    return hyena_out[:real_channels]


def solution(mesh):
    in_specs = (
        P("chan", "seq"),
        P("chan", "seq"),
        P("chan", "seq"),
        P("chan", None),
        P("chan", None),
        P("chan", None),
        P("chan"),
    )
    out_specs = P("chan", "seq")
    return jax.shard_map(
        on_device, mesh=mesh, in_specs=in_specs, out_specs=out_specs, check_vma=False
    )
```

```python
import functools
import math

import jax
import jax.numpy as jnp
import numpy as np
from jax import lax
from jax.experimental import pallas as pl
from jax.experimental.pallas import tpu as pltpu
from jax.sharding import PartitionSpec as P

LANES = 128
SUBS = 8
TILE = LANES * SUBS
BLOCK = 128
ROWS = 1024
STEPS = 8
F32, BF16 = jnp.float32, jnp.bfloat16


def halves(table):
    high = table.astype(jnp.bfloat16)
    low = (table - high.astype(np.float64)).astype(jnp.bfloat16)
    return high, low


def window_tables():
    size = 2 * BLOCK
    phase = 2.0 * math.pi / size * np.outer(np.arange(size), np.arange(BLOCK) + 0.5)
    forward = np.concatenate([np.cos(phase), -np.sin(phase)], axis=1)
    signs = np.tile((-1.0) ** np.arange(BLOCK), 2)
    inverse = forward[BLOCK:].T / BLOCK
    even = np.concatenate(halves(forward[:BLOCK]), axis=0)
    odd = np.concatenate(halves(forward[:BLOCK] * signs), axis=0)
    back = np.concatenate(halves(inverse), axis=1)
    return np.concatenate([even, odd, back], axis=1)


EVEN, ODD, BACK = (slice(i * 2 * BLOCK, (i + 1) * 2 * BLOCK) for i in range(3))


def mm(left, right):
    return jnp.dot(left, right, preferred_element_type=F32)


def split(value):
    high = value.astype(BF16)
    return high, (value - high.astype(F32)).astype(BF16)


def twice(block):
    return jnp.concatenate([block, block], axis=1)


def parts(image):
    return image[:, :BLOCK], image[:, BLOCK:]


def apply_window(earlier, later, spectrum, tables):
    (e_re, e_im), (l_re, l_im), (h_re, h_im) = parts(earlier), parts(later), parts(spectrum)
    re, im = e_re + l_im, e_im - l_re
    high, low = split(jnp.concatenate([re * h_re - im * h_im, re * h_im + im * h_re], axis=1))
    both = mm(high, tables[:, BACK])
    return both[:, :BLOCK] + both[:, BLOCK:] + mm(low, tables[:, BACK][:, :BLOCK])


def put_mixed(store, first_row, block_at, short, gate):
    mixed = (gate.astype(F32) * short).astype(BF16).astype(F32)
    for piece in range(ROWS // LANES):
        group = first_row // LANES + piece
        turned = mixed[piece * LANES : (piece + 1) * LANES].T
        store[pl.ds(block_at * BLOCK * SUBS + group, BLOCK, stride=SUBS), :] = turned


def lay_out(rows_ref, store):
    modes = rows_ref.shape[0]
    for group in range(SUBS):
        store[pl.ds(group, modes, stride=SUBS), :] = rows_ref[:, group * LANES : (group + 1) * LANES]


def end_states(store, mixed_ref, rates_ref):
    modes = rates_ref.shape[0]
    steps = store.shape[0] // SUBS
    decay = [jnp.exp(-rates_ref[mode]) for mode in range(modes)]

    def turn(index, states):
        at = pl.multiple_of(index * STEPS * SUBS, STEPS * SUBS)
        values = store[pl.ds(at, STEPS * SUBS), :]
        mixed_ref[pl.ds(at, STEPS * SUBS), :] = values.astype(BF16)
        for step in range(STEPS):
            value = values[step * SUBS : (step + 1) * SUBS]
            states = tuple(d * s + value for d, s in zip(decay, states))
        return states

    zeros = tuple(jnp.zeros((SUBS, LANES), F32) for _ in range(modes))
    return lax.fori_loop(0, steps // STEPS, turn, zeros)


def inner_kernel(
    seq_total,
    v_hbm, gate_hbm, taps_hbm, raw_hbm, raw_weights_hbm, tables_hbm,
    spec_ref, mixed_ref, state_ref, rates_ref, scaled_ref, v_first, gate_first, tables,
    v_rest, gate_rest, taps, raw, raw_weights, store, laid, sems,
):
    tiles, inner = mixed_ref.shape[0], v_rest.shape[1]

    def copies(tile):
        rows = pl.ds(tile * TILE, TILE)
        pairs = [(taps_hbm.at[rows], taps.at[rows])]
        for whole, head, rest in ((v_hbm, v_first, v_rest), (gate_hbm, gate_first, gate_rest)):
            pairs.append((whole.at[rows, pl.ds(0, BLOCK)], head.at[rows]))
            pairs.append((whole.at[rows, pl.ds(BLOCK, inner)], rest.at[rows]))
        return [pltpu.make_async_copy(*pair, sems.at[tile * 5 + i]) for i, pair in enumerate(pairs)]

    small = [
        pltpu.make_async_copy(tables_hbm, tables, sems.at[tiles * 5]),
        pltpu.make_async_copy(raw_hbm, raw, sems.at[tiles * 5 + 1]),
        pltpu.make_async_copy(raw_weights_hbm, raw_weights, sems.at[tiles * 5 + 2]),
    ]
    large = [copies(tile) for tile in range(tiles)]
    for copy in small + sum(large, []):
        copy.start()
    small[0].wait()
    sign = 1.0 - 2.0 * (lax.broadcasted_iota(jnp.int32, (1, 2 * BLOCK), 1) % 2).astype(F32)
    for tile in range(tiles):
        rows = slice(tile * TILE, (tile + 1) * TILE)
        groups = slice(tile * SUBS, (tile + 1) * SUBS)
        large[tile][0].wait()
        tap_hi, tap_lo = split(taps[rows])
        spectrum = mm(twice(tap_hi), tables[:, EVEN]) + mm(tap_lo, tables[:BLOCK, EVEN])
        turned = spectrum * sign
        spec_ref[rows] = turned
        for copy in large[tile][1:]:
            copy.wait()
        earlier = mm(twice(v_first[rows]), tables[:, EVEN])
        for block in range(1, inner // BLOCK + 1):
            at = slice((block - 1) * BLOCK, block * BLOCK)
            later = mm(twice(v_rest[rows, at]), tables[:, ODD if block % 2 else EVEN])
            short = apply_window(earlier, later, spectrum if block % 2 else turned, tables)
            put_mixed(store, 0, block - 1, short, gate_rest[rows, at])
            earlier = later
        if tile == 0:
            small[1].wait()
            small[2].wait()
        lay_out(raw.at[:, pl.ds(tile * TILE, TILE)], laid)
        modes = raw.shape[0]
        rates = laid[...].reshape(modes, SUBS, LANES)
        rates_ref[:, groups] = rates
        lay_out(raw_weights.at[:, pl.ds(tile * TILE, TILE)], laid)
        scaled_ref[:, groups] = laid[...].reshape(modes, SUBS, LANES) * jnp.sqrt(2.0 * rates + 2.0 / seq_total)
        for mode, state in enumerate(end_states(store, mixed_ref.at[tile], rates_ref.at[:, groups])):
            state_ref[mode, groups] = state


def rim_kernel(inner, place_ref, before_ref, v_ref, gate_ref, spec_ref, rates_ref, inner_ref, tables, *rest):
    mixed_ref, own_ref, twin_ref, store, ends = rest
    half = own_ref.shape[0]
    core = place_ref[0] % 2
    for tile in range(mixed_ref.shape[0]):
        rows = slice(tile * TILE, (tile + 1) * TILE)
        groups = slice(tile * SUBS, (tile + 1) * SUBS)
        earlier = mm(twice(before_ref[rows]), tables[:, ODD])
        later = mm(twice(v_ref[rows]), tables[:, EVEN])
        short = apply_window(earlier, later, spec_ref[rows], tables)
        put_mixed(store, 0, 0, short, gate_ref[rows])
        rates = rates_ref.at[:, groups]
        for mode, state in enumerate(end_states(store, mixed_ref.at[tile], rates)):
            ends[mode] = jnp.exp(-float(inner) * rates[mode]) * state + inner_ref[mode, groups]
        own_ref[:, groups] = ends[pl.ds(core * half, half)]
        twin_ref[:, groups] = ends[pl.ds((1 - core) * half, half)]


def decayed(rates, positions):
    return jnp.exp(-lax.convert_element_type(positions, F32) * rates)


def chip_kernel(tokens, place_ref, rates_ref, mine_ref, other_ref, total_ref):
    half = total_ref.shape[0]
    core = place_ref[0] % 2
    rates = rates_ref[pl.ds(core * half, half)]
    total_ref[...] = decayed(rates, tokens * (1 - core)) * mine_ref[...] + decayed(rates, tokens * core) * other_ref[...]


def level_kernel(tokens, size, place_ref, rates_ref, total_ref, other_ref, before_ref, joined_ref, after_ref):
    half = total_ref.shape[0]
    place = place_ref[0]
    upper = place // size % 2
    rates = rates_ref[pl.ds(place % 2 * half, half)]
    joined_ref[...] = (
        decayed(rates, tokens * size * (1 - upper)) * total_ref[...]
        + decayed(rates, tokens * size * upper) * other_ref[...]
    )
    reach = decayed(rates, tokens * (place % size // 2 * 2)) * other_ref[...]
    after_ref[...] = before_ref[...] + jnp.where(upper == 1, reach, 0.0)


def start_kernel(tokens, size, place_ref, rates_ref, other_ref, before_ref, own_ref, twin_ref, mine_ref, twins_ref):
    half = own_ref.shape[0]
    place = place_ref[0]
    core = place % 2
    upper = place // size % 2
    rates = rates_ref[pl.ds(core * half, half)]
    reach = decayed(rates, tokens * (place % size // 2 * 2)) * other_ref[...]
    first = before_ref[...] + jnp.where(upper == 1, reach, 0.0)
    second = decayed(rates, tokens) * first + jnp.where(core == 0, own_ref[...], twin_ref[...])
    mine_ref[...] = jnp.where(core == 0, first, second)
    twins_ref[...] = jnp.where(core == 0, second, first)


def added(terms):
    while len(terms) > 1:
        terms = [sum(terms[i : i + 2][1:], terms[i]) for i in range(0, len(terms), 2)]
    return terms[0]


def filtered(source, start, store, decay, scaled, bias, states):
    def turn(index, states):
        at = pl.multiple_of(index * STEPS * SUBS, STEPS * SUBS)
        values = source[pl.ds(start * SUBS + at, STEPS * SUBS), :].astype(F32)
        sums = []
        for step in range(STEPS):
            value = values[step * SUBS : (step + 1) * SUBS]
            states = tuple(d * s + value for d, s in zip(decay, states))
            sums.append(added([c * s for c, s in zip(scaled, states)] + [bias * value]))
        store[pl.ds(at, STEPS * SUBS), :] = jnp.concatenate(sums, axis=0)
        return states

    return lax.fori_loop(0, BLOCK // STEPS, turn, states)


def local_kernel(start, mixed_ref, rates_ref, scaled_ref, bias_ref, *rest):
    *earlier, sums_ref, states_ref = rest
    modes = rates_ref.shape[0]
    for tile in range(sums_ref.shape[0]):
        groups = slice(tile * SUBS, (tile + 1) * SUBS)
        decay = [jnp.exp(-rates_ref[mode, groups]) for mode in range(modes)]
        scaled = [scaled_ref[mode, groups] for mode in range(modes)]
        states = tuple(earlier[0][m, groups] if earlier else jnp.zeros((SUBS, LANES), F32) for m in range(modes))
        states = filtered(
            mixed_ref.at[tile], start, sums_ref.at[tile], decay, scaled, bias_ref[groups], states
        )
        for mode in range(modes):
            states_ref[mode, groups] = states[mode]


def outer_kernel(place_ref, mixed_ref, gate_ref, rates_ref, scaled_ref, bias_ref, mine_ref, twins_ref, local_ref, *rest):
    *sums_refs, out_hbm, store, begin, out, sems = rest
    modes, half = rates_ref.shape[0], mine_ref.shape[0]
    core = place_ref[0] % 2
    begin[pl.ds(core * half, half)] = mine_ref[...]
    begin[pl.ds((1 - core) * half, half)] = twins_ref[...]
    blocks = len(sums_refs) + 1
    copies = []
    for tile in range(mixed_ref.shape[0]):
        groups = slice(tile * SUBS, (tile + 1) * SUBS)
        decay = [jnp.exp(-rates_ref[mode, groups]) for mode in range(modes)]
        scaled = [scaled_ref[mode, groups] for mode in range(modes)]
        states = tuple(c * begin[mode, groups] for mode, c in enumerate(scaled))
        for block, sums_ref in enumerate(sums_refs):

            def carry(index, states, sums_ref=sums_ref, block=block):
                at = pl.multiple_of(index * STEPS * SUBS, STEPS * SUBS)
                for step in range(STEPS):
                    states = tuple(d * s for d, s in zip(decay, states))
                    total = sums_ref[tile, pl.ds(at + step * SUBS, SUBS), :] + added(list(states))
                    store[pl.ds(block * BLOCK * SUBS + at + step * SUBS, SUBS), :] = total
                return states

            states = lax.fori_loop(0, BLOCK // STEPS, carry, states)
        past = float((blocks - 1) * BLOCK)
        full = tuple(
            local_ref[mode, groups] + jnp.exp(-past * rates_ref[mode, groups]) * begin[mode, groups]
            for mode in range(modes)
        )
        last = (blocks - 1) * BLOCK
        filtered(
            mixed_ref.at[tile], last - BLOCK, store.at[pl.ds(last * SUBS, BLOCK * SUBS)], decay, scaled, bias_ref[groups], full
        )
        for group in range(SUBS):
            rows = slice(tile * TILE + group * LANES, tile * TILE + (group + 1) * LANES)
            for block in range(blocks):
                cols = slice(block * BLOCK, (block + 1) * BLOCK)
                turned = store[pl.ds(block * BLOCK * SUBS + group, BLOCK, stride=SUBS), :].T
                out[rows, cols] = (gate_ref[rows, cols].astype(F32) * turned).astype(BF16)
            copy = pltpu.make_async_copy(out.at[rows], out_hbm.at[rows], sems.at[tile * SUBS + group])
            copy.start()
            copies.append(copy)
    for copy in copies:
        copy.wait()


SCALAR = pl.BlockSpec(memory_space=pltpu.SMEM)
WHOLE = pl.BlockSpec(memory_space=pltpu.VMEM)
FAR = pl.BlockSpec(memory_space=pltpu.HBM)
INNER_ROOM, RIM_ROOM = 32, 24


def steps_scratch(steps):
    return pltpu.VMEM((steps * SUBS, LANES), F32)


def kept_far(array):
    return pltpu.with_memory_space_constraint(array, pltpu.HBM)


def on_device(v_stream, gate_one, gate_two, short_filter, decay_rates, residues, skip_bias):
    real_channels, tokens = v_stream.shape
    modes = decay_rates.shape[1]
    shards = lax.axis_size("seq")
    before = lax.ppermute(v_stream[:, tokens - BLOCK :], "seq", [(i, i + 1) for i in range(shards - 1)])
    extra = -real_channels % TILE

    def padded(array):
        return jnp.pad(array, ((0, extra),) + ((0, 0),) * (array.ndim - 1)) if extra else array

    v_stream, gate_one, gate_two, short_filter = map(padded, (v_stream, gate_one, gate_two, short_filter))
    decay_rates, residues, skip_bias, before = map(padded, (decay_rates, residues, skip_bias, before))
    channels = real_channels + extra
    tiles, groups = channels // TILE, channels // LANES
    raw_rates, raw_weights = decay_rates.T, residues.T
    bias = skip_bias.reshape(groups, LANES)
    tables = jnp.asarray(window_tables())
    place = lax.axis_index("seq").astype(jnp.int32).reshape(1)
    inner = tokens - BLOCK
    shape = jax.ShapeDtypeStruct
    per_mode = shape((modes, groups, LANES), F32)
    half = shape((modes // 2, groups, LANES), F32)
    laid = pltpu.VMEM((modes * SUBS, LANES), F32)
    tap_spectra = shape((channels, 2 * BLOCK), F32)
    head = shape((channels, BLOCK), BF16)
    spectrum, inner_mixed, inner_state, rates, scaled, v_first, gate_first, tables = pl.pallas_call(
        functools.partial(inner_kernel, tokens * shards),
        in_specs=[FAR] * 6,
        out_specs=[WHOLE] * 8,
        out_shape=[tap_spectra, shape((tiles, inner * SUBS, LANES), BF16)] + [per_mode] * 3 + [head, head]
        + [shape(tables.shape, BF16)],
        scratch_shapes=[
            pltpu.VMEM((channels, inner), BF16),
            pltpu.VMEM((channels, inner), BF16),
            pltpu.VMEM((channels, BLOCK), F32),
            pltpu.VMEM((modes, channels), F32),
            pltpu.VMEM((modes, channels), F32),
            steps_scratch(inner),
            laid,
            pltpu.SemaphoreType.DMA((tiles * 5 + 3,)),
        ],
        compiler_params=pltpu.CompilerParams(vmem_limit_bytes=INNER_ROOM << 20),
        cost_estimate=pl.CostEstimate(
            flops=channels * inner * 2600, bytes_accessed=channels * tokens * 8, transcendentals=0
        ),
    )(*map(kept_far, (v_stream, gate_one, short_filter, raw_rates, raw_weights, tables)))
    rim_mixed, own_end, twin_half = pl.pallas_call(
        functools.partial(rim_kernel, inner),
        in_specs=[SCALAR] + [WHOLE] * 7,
        out_specs=[WHOLE] * 3,
        out_shape=[shape((tiles, BLOCK * SUBS, LANES), BF16), half, half],
        scratch_shapes=[steps_scratch(BLOCK), pltpu.VMEM((modes, SUBS, LANES), F32)],
        compiler_params=pltpu.CompilerParams(vmem_limit_bytes=RIM_ROOM << 20),
        cost_estimate=pl.CostEstimate(
            flops=channels * BLOCK * 2600, bytes_accessed=channels * BLOCK * 16, transcendentals=0
        ),
    )(place, before, v_first, gate_first, spectrum, rates, inner_state, tables)

    def swap(array, distance):
        return lax.ppermute(array, "seq", [(i, i ^ distance) for i in range(shards)])

    def small(kernel, outputs, *arrays):
        return pl.pallas_call(
            kernel,
            in_specs=[SCALAR] + [WHOLE] * (len(arrays) + 1),
            out_specs=[WHOLE] * outputs,
            out_shape=[half] * outputs,
            compiler_params=pltpu.CompilerParams(vmem_limit_bytes=8 << 20),
        )(place, rates, *arrays)

    sums, states = [], []

    def beside(arriving, sent):
        block = len(sums)
        if block >= tokens // BLOCK - 1:
            return arriving
        source, start = (inner_mixed, (block - 1) * BLOCK) if block else (rim_mixed, 0)
        source, *earlier, _ = lax.optimization_barrier((source, *states[-1:], sent))
        done = pl.pallas_call(
            functools.partial(local_kernel, start),
            in_specs=[WHOLE] * (4 + len(earlier)),
            out_specs=[WHOLE] * 2,
            out_shape=[shape((tiles, BLOCK * SUBS, LANES), F32), per_mode],
            compiler_params=pltpu.CompilerParams(vmem_limit_bytes=8 << 20),
            cost_estimate=pl.CostEstimate(
                flops=channels * BLOCK * 2600, bytes_accessed=channels * BLOCK * 16, transcendentals=0
            ),
        )(source, rates, scaled, bias, *earlier)
        arriving, total, state = lax.optimization_barrier((arriving, *done))
        sums.append(total)
        states.append(state)
        return arriving

    twin_end = swap(twin_half, 1)
    (total,) = small(functools.partial(chip_kernel, tokens), 1, own_end, twin_end)
    ahead = jnp.zeros(half.shape, F32)
    size = 2
    while 2 * size < shards:
        other = beside(swap(total, size), total)
        total, ahead = small(functools.partial(level_kernel, tokens, size), 2, total, other, ahead)
        size *= 2
    other = beside(swap(total, size), total)
    mine, twins = small(functools.partial(start_kernel, tokens, size), 2, other, ahead, own_end, twin_end)
    twins = swap(twins, 1)
    while len(sums) < tokens // BLOCK - 1:
        beside(total, total)

    hyena_out = pl.pallas_call(
        outer_kernel,
        in_specs=[SCALAR] + [WHOLE] * (8 + len(sums)),
        out_specs=FAR,
        out_shape=shape((channels, tokens), BF16),
        scratch_shapes=[
            steps_scratch(tokens),
            pltpu.VMEM((modes, groups, LANES), F32),
            pltpu.VMEM((channels, tokens), BF16),
            pltpu.SemaphoreType.DMA((groups,)),
        ],
        compiler_params=pltpu.CompilerParams(vmem_limit_bytes=24 << 20),
        cost_estimate=pl.CostEstimate(
            flops=channels * tokens * 50, bytes_accessed=channels * tokens * 6, transcendentals=0
        ),
    )(place, inner_mixed, gate_two, rates, scaled, bias, mine, twins, states[-1], *sums)
    return hyena_out[:real_channels]


def solution(mesh):
    in_specs = (
        P("chan", "seq"),
        P("chan", "seq"),
        P("chan", "seq"),
        P("chan", None),
        P("chan", None),
        P("chan", None),
        P("chan"),
    )
    out_specs = P("chan", "seq")
    return jax.shard_map(
        on_device, mesh=mesh, in_specs=in_specs, out_specs=out_specs, check_vma=False
    )
```

```python
import functools
import math

import jax
import jax.numpy as jnp
import numpy as np
from jax import lax
from jax.experimental import pallas as pl
from jax.experimental.pallas import tpu as pltpu
from jax.sharding import PartitionSpec as P

LANES = 128
SUBS = 8
TILE = LANES * SUBS
BLOCK = 128
ROWS = 1024
STEPS = 16
LONG = 32
F32, BF16 = jnp.float32, jnp.bfloat16


def halves(table):
    high = table.astype(jnp.bfloat16)
    low = (table - high.astype(np.float64)).astype(jnp.bfloat16)
    return high, low


def window_tables():
    size = 2 * BLOCK
    phase = 2.0 * math.pi / size * np.outer(np.arange(size), np.arange(BLOCK) + 0.5)
    forward = np.concatenate([np.cos(phase), -np.sin(phase)], axis=1)
    signs = np.tile((-1.0) ** np.arange(BLOCK), 2)
    inverse = forward[BLOCK:].T / BLOCK
    even = np.concatenate(halves(forward[:BLOCK]), axis=0)
    odd = np.concatenate(halves(forward[:BLOCK] * signs), axis=0)
    back = np.concatenate(halves(inverse), axis=1)
    return np.concatenate([even, odd, back], axis=1)


EVEN, ODD, BACK = (slice(i * 2 * BLOCK, (i + 1) * 2 * BLOCK) for i in range(3))


def mm(left, right):
    return jnp.dot(left, right, preferred_element_type=F32)


def split(value):
    high = value.astype(BF16)
    return high, (value - high.astype(F32)).astype(BF16)


def twice(block):
    return jnp.concatenate([block, block], axis=1)


def parts(image):
    return image[:, :BLOCK], image[:, BLOCK:]


def apply_window(earlier, later, spectrum, tables):
    (e_re, e_im), (l_re, l_im), (h_re, h_im) = parts(earlier), parts(later), parts(spectrum)
    re, im = e_re + l_im, e_im - l_re
    high, low = split(jnp.concatenate([re * h_re - im * h_im, re * h_im + im * h_re], axis=1))
    both = mm(high, tables[:, BACK])
    return both[:, :BLOCK] + both[:, BLOCK:] + mm(low, tables[:, BACK][:, :BLOCK])


def put_mixed(store, first_row, block_at, short, gate):
    mixed = (gate.astype(F32) * short).astype(BF16).astype(F32)
    for piece in range(ROWS // LANES):
        group = first_row // LANES + piece
        turned = mixed[piece * LANES : (piece + 1) * LANES].T
        store[pl.ds(block_at * BLOCK * SUBS + group, BLOCK, stride=SUBS), :] = turned


def lay_out(rows_ref, store):
    modes = rows_ref.shape[0]
    for group in range(SUBS):
        store[pl.ds(group, modes, stride=SUBS), :] = rows_ref[:, group * LANES : (group + 1) * LANES]


def end_states(store, mixed_ref, rates_ref):
    modes = rates_ref.shape[0]
    steps = store.shape[0] // SUBS
    decay = [jnp.exp(-rates_ref[mode]) for mode in range(modes)]

    def turn(index, states):
        at = pl.multiple_of(index * STEPS * SUBS, STEPS * SUBS)
        values = store[pl.ds(at, STEPS * SUBS), :]
        mixed_ref[pl.ds(at, STEPS * SUBS), :] = values.astype(BF16)
        for step in range(STEPS):
            value = values[step * SUBS : (step + 1) * SUBS]
            states = tuple(d * s + value for d, s in zip(decay, states))
        return states

    zeros = tuple(jnp.zeros((SUBS, LANES), F32) for _ in range(modes))
    return lax.fori_loop(0, steps // STEPS, turn, zeros)


def inner_kernel(
    seq_total,
    v_hbm, gate_hbm, taps_hbm, raw_hbm, raw_weights_hbm, tables_hbm,
    spec_ref, mixed_ref, state_ref, rates_ref, scaled_ref, v_first, gate_first, tables,
    v_rest, gate_rest, taps, raw, raw_weights, store, laid, sems,
):
    tiles, inner = mixed_ref.shape[0], v_rest.shape[1]

    def copies(tile):
        rows = pl.ds(tile * TILE, TILE)
        pairs = [(taps_hbm.at[rows], taps.at[rows])]
        for whole, head, rest in ((v_hbm, v_first, v_rest), (gate_hbm, gate_first, gate_rest)):
            pairs.append((whole.at[rows, pl.ds(0, BLOCK)], head.at[rows]))
            pairs.append((whole.at[rows, pl.ds(BLOCK, inner)], rest.at[rows]))
        return [pltpu.make_async_copy(*pair, sems.at[tile * 5 + i]) for i, pair in enumerate(pairs)]

    small = [
        pltpu.make_async_copy(tables_hbm, tables, sems.at[tiles * 5]),
        pltpu.make_async_copy(raw_hbm, raw, sems.at[tiles * 5 + 1]),
        pltpu.make_async_copy(raw_weights_hbm, raw_weights, sems.at[tiles * 5 + 2]),
    ]
    large = [copies(tile) for tile in range(tiles)]
    for copy in small + large[0]:
        copy.start()
    for copy in small + large[0]:
        copy.wait()
    sign = 1.0 - 2.0 * (lax.broadcasted_iota(jnp.int32, (1, 2 * BLOCK), 1) % 2).astype(F32)
    for tile in range(tiles):
        rows = slice(tile * TILE, (tile + 1) * TILE)
        groups = slice(tile * SUBS, (tile + 1) * SUBS)
        if tile:
            for copy in large[tile]:
                copy.wait()
        if tile + 1 < tiles:
            for copy in large[tile + 1]:
                copy.start()
        tap_hi, tap_lo = split(taps[rows])
        spectrum = mm(twice(tap_hi), tables[:, EVEN]) + mm(tap_lo, tables[:BLOCK, EVEN])
        turned = spectrum * sign
        spec_ref[rows] = turned
        earlier = mm(twice(v_first[rows]), tables[:, EVEN])
        for block in range(1, inner // BLOCK + 1):
            at = slice((block - 1) * BLOCK, block * BLOCK)
            later = mm(twice(v_rest[rows, at]), tables[:, ODD if block % 2 else EVEN])
            short = apply_window(earlier, later, spectrum if block % 2 else turned, tables)
            put_mixed(store, 0, block - 1, short, gate_rest[rows, at])
            earlier = later
        lay_out(raw.at[:, pl.ds(tile * TILE, TILE)], laid)
        modes = raw.shape[0]
        rates = laid[...].reshape(modes, SUBS, LANES)
        rates_ref[:, groups] = rates
        lay_out(raw_weights.at[:, pl.ds(tile * TILE, TILE)], laid)
        scaled_ref[:, groups] = laid[...].reshape(modes, SUBS, LANES) * jnp.sqrt(2.0 * rates + 2.0 / seq_total)
        for mode, state in enumerate(end_states(store, mixed_ref.at[tile], rates_ref.at[:, groups])):
            state_ref[mode, groups] = state


def rim_kernel(inner, place_ref, before_ref, v_ref, gate_ref, spec_ref, rates_ref, inner_ref, tables, *rest):
    mixed_ref, own_ref, twin_ref, store, ends = rest
    half = own_ref.shape[0]
    core = place_ref[0] % 2
    for tile in range(mixed_ref.shape[0]):
        rows = slice(tile * TILE, (tile + 1) * TILE)
        groups = slice(tile * SUBS, (tile + 1) * SUBS)
        earlier = mm(twice(before_ref[rows]), tables[:, ODD])
        later = mm(twice(v_ref[rows]), tables[:, EVEN])
        short = apply_window(earlier, later, spec_ref[rows], tables)
        put_mixed(store, 0, 0, short, gate_ref[rows])
        rates = rates_ref.at[:, groups]
        for mode, state in enumerate(end_states(store, mixed_ref.at[tile], rates)):
            ends[mode] = jnp.exp(-float(inner) * rates[mode]) * state + inner_ref[mode, groups]
        own_ref[:, groups] = ends[pl.ds(core * half, half)]
        twin_ref[:, groups] = ends[pl.ds((1 - core) * half, half)]


def decayed(rates, positions):
    return jnp.exp(-lax.convert_element_type(positions, F32) * rates)


def chip_kernel(tokens, place_ref, rates_ref, mine_ref, other_ref, total_ref):
    half = total_ref.shape[0]
    core = place_ref[0] % 2
    rates = rates_ref[pl.ds(core * half, half)]
    total_ref[...] = decayed(rates, tokens * (1 - core)) * mine_ref[...] + decayed(rates, tokens * core) * other_ref[...]


def level_kernel(tokens, size, place_ref, rates_ref, total_ref, other_ref, before_ref, joined_ref, after_ref):
    half = total_ref.shape[0]
    place = place_ref[0]
    upper = place // size % 2
    rates = rates_ref[pl.ds(place % 2 * half, half)]
    joined_ref[...] = (
        decayed(rates, tokens * size * (1 - upper)) * total_ref[...]
        + decayed(rates, tokens * size * upper) * other_ref[...]
    )
    reach = decayed(rates, tokens * (place % size // 2 * 2)) * other_ref[...]
    after_ref[...] = before_ref[...] + jnp.where(upper == 1, reach, 0.0)


def start_kernel(tokens, size, place_ref, rates_ref, other_ref, before_ref, own_ref, twin_ref, mine_ref, twins_ref):
    half = own_ref.shape[0]
    place = place_ref[0]
    core = place % 2
    upper = place // size % 2
    rates = rates_ref[pl.ds(core * half, half)]
    reach = decayed(rates, tokens * (place % size // 2 * 2)) * other_ref[...]
    first = before_ref[...] + jnp.where(upper == 1, reach, 0.0)
    second = decayed(rates, tokens) * first + jnp.where(core == 0, own_ref[...], twin_ref[...])
    mine_ref[...] = jnp.where(core == 0, first, second)
    twins_ref[...] = jnp.where(core == 0, second, first)


def added(terms):
    while len(terms) > 1:
        terms = [sum(terms[i : i + 2][1:], terms[i]) for i in range(0, len(terms), 2)]
    return terms[0]


def filtered(source, start, store, decay, scaled, bias, states):
    def turn(index, states):
        at = pl.multiple_of(index * LONG * SUBS, LONG * SUBS)
        values = source[pl.ds(start * SUBS + at, LONG * SUBS), :].astype(F32)
        sums = []
        for step in range(LONG):
            value = values[step * SUBS : (step + 1) * SUBS]
            states = tuple(d * s + value for d, s in zip(decay, states))
            sums.append(added([c * s for c, s in zip(scaled, states)] + [bias * value]))
        store[pl.ds(at, LONG * SUBS), :] = jnp.concatenate(sums, axis=0)
        return states

    return lax.fori_loop(0, BLOCK // LONG, turn, states)


def local_kernel(start, mixed_ref, rates_ref, scaled_ref, bias_ref, *rest):
    *earlier, sums_ref, states_ref = rest
    modes = rates_ref.shape[0]
    for tile in range(sums_ref.shape[0]):
        groups = slice(tile * SUBS, (tile + 1) * SUBS)
        decay = [jnp.exp(-rates_ref[mode, groups]) for mode in range(modes)]
        scaled = [scaled_ref[mode, groups] for mode in range(modes)]
        states = tuple(earlier[0][m, groups] if earlier else jnp.zeros((SUBS, LANES), F32) for m in range(modes))
        states = filtered(
            mixed_ref.at[tile], start, sums_ref.at[tile], decay, scaled, bias_ref[groups], states
        )
        for mode in range(modes):
            states_ref[mode, groups] = states[mode]


def outer_kernel(place_ref, mixed_ref, gate_ref, rates_ref, scaled_ref, bias_ref, mine_ref, twins_ref, local_ref, *rest):
    *sums_refs, out_hbm, store, begin, out, sems = rest
    modes, half = rates_ref.shape[0], mine_ref.shape[0]
    core = place_ref[0] % 2
    begin[pl.ds(core * half, half)] = mine_ref[...]
    begin[pl.ds((1 - core) * half, half)] = twins_ref[...]
    blocks = len(sums_refs) + 1
    copies = []
    for tile in range(mixed_ref.shape[0]):
        groups = slice(tile * SUBS, (tile + 1) * SUBS)
        decay = [jnp.exp(-rates_ref[mode, groups]) for mode in range(modes)]
        scaled = [scaled_ref[mode, groups] for mode in range(modes)]
        states = tuple(c * begin[mode, groups] for mode, c in enumerate(scaled))
        for block, sums_ref in enumerate(sums_refs):

            def carry(index, states, sums_ref=sums_ref, block=block):
                at = pl.multiple_of(index * LONG * SUBS, LONG * SUBS)
                for step in range(LONG):
                    states = tuple(d * s for d, s in zip(decay, states))
                    total = sums_ref[tile, pl.ds(at + step * SUBS, SUBS), :] + added(list(states))
                    store[pl.ds(block * BLOCK * SUBS + at + step * SUBS, SUBS), :] = total
                return states

            states = lax.fori_loop(0, BLOCK // LONG, carry, states)
        past = float((blocks - 1) * BLOCK)
        full = tuple(
            local_ref[mode, groups] + jnp.exp(-past * rates_ref[mode, groups]) * begin[mode, groups]
            for mode in range(modes)
        )
        last = (blocks - 1) * BLOCK
        filtered(
            mixed_ref.at[tile], last - BLOCK, store.at[pl.ds(last * SUBS, BLOCK * SUBS)], decay, scaled, bias_ref[groups], full
        )
        for group in range(SUBS):
            rows = slice(tile * TILE + group * LANES, tile * TILE + (group + 1) * LANES)
            for block in range(blocks):
                cols = slice(block * BLOCK, (block + 1) * BLOCK)
                turned = store[pl.ds(block * BLOCK * SUBS + group, BLOCK, stride=SUBS), :].T
                out[rows, cols] = (gate_ref[rows, cols].astype(F32) * turned).astype(BF16)
            copy = pltpu.make_async_copy(out.at[rows], out_hbm.at[rows], sems.at[tile * SUBS + group])
            copy.start()
            copies.append(copy)
    for copy in copies:
        copy.wait()


SCALAR = pl.BlockSpec(memory_space=pltpu.SMEM)
WHOLE = pl.BlockSpec(memory_space=pltpu.VMEM)
FAR = pl.BlockSpec(memory_space=pltpu.HBM)
INNER_ROOM, RIM_ROOM = 32, 24


def steps_scratch(steps):
    return pltpu.VMEM((steps * SUBS, LANES), F32)


def kept_far(array):
    return pltpu.with_memory_space_constraint(array, pltpu.HBM)


def on_device(v_stream, gate_one, gate_two, short_filter, decay_rates, residues, skip_bias):
    real_channels, tokens = v_stream.shape
    modes = decay_rates.shape[1]
    shards = lax.axis_size("seq")
    before = lax.ppermute(v_stream[:, tokens - BLOCK :], "seq", [(i, i + 1) for i in range(shards - 1)])
    extra = -real_channels % TILE

    def padded(array):
        return jnp.pad(array, ((0, extra),) + ((0, 0),) * (array.ndim - 1)) if extra else array

    v_stream, gate_one, gate_two, short_filter = map(padded, (v_stream, gate_one, gate_two, short_filter))
    decay_rates, residues, skip_bias, before = map(padded, (decay_rates, residues, skip_bias, before))
    channels = real_channels + extra
    tiles, groups = channels // TILE, channels // LANES
    raw_rates, raw_weights = decay_rates.T, residues.T
    bias = skip_bias.reshape(groups, LANES)
    tables = jnp.asarray(window_tables())
    place = lax.axis_index("seq").astype(jnp.int32).reshape(1)
    inner = tokens - BLOCK
    shape = jax.ShapeDtypeStruct
    per_mode = shape((modes, groups, LANES), F32)
    half = shape((modes // 2, groups, LANES), F32)
    laid = pltpu.VMEM((modes * SUBS, LANES), F32)
    tap_spectra = shape((channels, 2 * BLOCK), F32)
    head = shape((channels, BLOCK), BF16)
    spectrum, inner_mixed, inner_state, rates, scaled, v_first, gate_first, tables = pl.pallas_call(
        functools.partial(inner_kernel, tokens * shards),
        in_specs=[FAR] * 6,
        out_specs=[WHOLE] * 8,
        out_shape=[tap_spectra, shape((tiles, inner * SUBS, LANES), BF16)] + [per_mode] * 3 + [head, head]
        + [shape(tables.shape, BF16)],
        scratch_shapes=[
            pltpu.VMEM((channels, inner), BF16),
            pltpu.VMEM((channels, inner), BF16),
            pltpu.VMEM((channels, BLOCK), F32),
            pltpu.VMEM((modes, channels), F32),
            pltpu.VMEM((modes, channels), F32),
            steps_scratch(inner),
            laid,
            pltpu.SemaphoreType.DMA((tiles * 5 + 3,)),
        ],
        compiler_params=pltpu.CompilerParams(vmem_limit_bytes=INNER_ROOM << 20),
        cost_estimate=pl.CostEstimate(
            flops=channels * inner * 2600, bytes_accessed=channels * tokens * 8, transcendentals=0
        ),
    )(*map(kept_far, (v_stream, gate_one, short_filter, raw_rates, raw_weights, tables)))
    rim_mixed, own_end, twin_half = pl.pallas_call(
        functools.partial(rim_kernel, inner),
        in_specs=[SCALAR] + [WHOLE] * 7,
        out_specs=[WHOLE] * 3,
        out_shape=[shape((tiles, BLOCK * SUBS, LANES), BF16), half, half],
        scratch_shapes=[steps_scratch(BLOCK), pltpu.VMEM((modes, SUBS, LANES), F32)],
        compiler_params=pltpu.CompilerParams(vmem_limit_bytes=RIM_ROOM << 20),
        cost_estimate=pl.CostEstimate(
            flops=channels * BLOCK * 2600, bytes_accessed=channels * BLOCK * 16, transcendentals=0
        ),
    )(place, before, v_first, gate_first, spectrum, rates, inner_state, tables)

    def swap(array, distance):
        return lax.ppermute(array, "seq", [(i, i ^ distance) for i in range(shards)])

    def small(kernel, outputs, *arrays):
        return pl.pallas_call(
            kernel,
            in_specs=[SCALAR] + [WHOLE] * (len(arrays) + 1),
            out_specs=[WHOLE] * outputs,
            out_shape=[half] * outputs,
            compiler_params=pltpu.CompilerParams(vmem_limit_bytes=8 << 20),
        )(place, rates, *arrays)

    sums, states = [], []

    def beside(arriving, sent):
        block = len(sums)
        if block >= tokens // BLOCK - 1:
            return arriving
        source, start = (inner_mixed, (block - 1) * BLOCK) if block else (rim_mixed, 0)
        source, *earlier, _ = lax.optimization_barrier((source, *states[-1:], sent))
        done = pl.pallas_call(
            functools.partial(local_kernel, start),
            in_specs=[WHOLE] * (4 + len(earlier)),
            out_specs=[WHOLE] * 2,
            out_shape=[shape((tiles, BLOCK * SUBS, LANES), F32), per_mode],
            compiler_params=pltpu.CompilerParams(vmem_limit_bytes=8 << 20),
            cost_estimate=pl.CostEstimate(
                flops=channels * BLOCK * 2600, bytes_accessed=channels * BLOCK * 16, transcendentals=0
            ),
        )(source, rates, scaled, bias, *earlier)
        arriving, total, state = lax.optimization_barrier((arriving, *done))
        sums.append(total)
        states.append(state)
        return arriving

    twin_end = swap(twin_half, 1)
    (total,) = small(functools.partial(chip_kernel, tokens), 1, own_end, twin_end)
    ahead = jnp.zeros(half.shape, F32)
    size = 2
    while 2 * size < shards:
        other = beside(swap(total, size), total)
        total, ahead = small(functools.partial(level_kernel, tokens, size), 2, total, other, ahead)
        size *= 2
    other = beside(swap(total, size), total)
    mine, twins = small(functools.partial(start_kernel, tokens, size), 2, other, ahead, own_end, twin_end)
    twins = swap(twins, 1)
    while len(sums) < tokens // BLOCK - 1:
        beside(total, total)

    hyena_out = pl.pallas_call(
        outer_kernel,
        in_specs=[SCALAR] + [WHOLE] * (8 + len(sums)),
        out_specs=FAR,
        out_shape=shape((channels, tokens), BF16),
        scratch_shapes=[
            steps_scratch(tokens),
            pltpu.VMEM((modes, groups, LANES), F32),
            pltpu.VMEM((channels, tokens), BF16),
            pltpu.SemaphoreType.DMA((groups,)),
        ],
        compiler_params=pltpu.CompilerParams(vmem_limit_bytes=24 << 20),
        cost_estimate=pl.CostEstimate(
            flops=channels * tokens * 50, bytes_accessed=channels * tokens * 6, transcendentals=0
        ),
    )(place, inner_mixed, gate_two, rates, scaled, bias, mine, twins, states[-1], *sums)
    return hyena_out[:real_channels]


def solution(mesh):
    in_specs = (
        P("chan", "seq"),
        P("chan", "seq"),
        P("chan", "seq"),
        P("chan", None),
        P("chan", None),
        P("chan", None),
        P("chan"),
    )
    out_specs = P("chan", "seq")
    return jax.shard_map(
        on_device, mesh=mesh, in_specs=in_specs, out_specs=out_specs, check_vma=False
    )
```

```python
import functools
import math

import jax
import jax.numpy as jnp
import numpy as np
from jax import lax
from jax.experimental import pallas as pl
from jax.experimental.pallas import tpu as pltpu
from jax.sharding import PartitionSpec as P

LANES = 128
SUBS = 8
TILE = LANES * SUBS
BLOCK = 128
ROWS = 1024
STEPS = 16
LONG = 32
F32, BF16 = jnp.float32, jnp.bfloat16


def halves(table):
    high = table.astype(jnp.bfloat16)
    low = (table - high.astype(np.float64)).astype(jnp.bfloat16)
    return high, low


def window_tables():
    size = 2 * BLOCK
    phase = 2.0 * math.pi / size * np.outer(np.arange(size), np.arange(BLOCK) + 0.5)
    forward = np.concatenate([np.cos(phase), -np.sin(phase)], axis=1)
    signs = np.tile((-1.0) ** np.arange(BLOCK), 2)
    inverse = forward[BLOCK:].T / BLOCK
    even = np.concatenate(halves(forward[:BLOCK]), axis=0)
    odd = np.concatenate(halves(forward[:BLOCK] * signs), axis=0)
    back = np.concatenate(halves(inverse), axis=1)
    return np.concatenate([even, odd, back], axis=1)


EVEN, ODD, BACK = (slice(i * 2 * BLOCK, (i + 1) * 2 * BLOCK) for i in range(3))


def mm(left, right):
    return jnp.dot(left, right, preferred_element_type=F32)


def split(value):
    high = value.astype(BF16)
    return high, (value - high.astype(F32)).astype(BF16)


def twice(block):
    return jnp.concatenate([block, block], axis=1)


def parts(image):
    return image[:, :BLOCK], image[:, BLOCK:]


def apply_window(earlier, later, spectrum, tables):
    (e_re, e_im), (l_re, l_im), (h_re, h_im) = parts(earlier), parts(later), parts(spectrum)
    re, im = e_re + l_im, e_im - l_re
    high, low = split(jnp.concatenate([re * h_re - im * h_im, re * h_im + im * h_re], axis=1))
    both = mm(high, tables[:, BACK])
    return both[:, :BLOCK] + both[:, BLOCK:] + mm(low, tables[:, BACK][:, :BLOCK])


def put_mixed(store, first_row, block_at, short, gate):
    mixed = (gate.astype(F32) * short).astype(BF16).astype(F32)
    for piece in range(ROWS // LANES):
        group = first_row // LANES + piece
        turned = mixed[piece * LANES : (piece + 1) * LANES].T
        store[pl.ds(block_at * BLOCK * SUBS + group, BLOCK, stride=SUBS), :] = turned


def lay_out(rows_ref, store):
    modes = rows_ref.shape[0]
    for group in range(SUBS):
        store[pl.ds(group, modes, stride=SUBS), :] = rows_ref[:, group * LANES : (group + 1) * LANES]


def end_states(store, mixed_ref, rates_ref):
    modes = rates_ref.shape[0]
    steps = store.shape[0] // SUBS
    decay = [jnp.exp(-rates_ref[mode]) for mode in range(modes)]

    def turn(index, states):
        at = pl.multiple_of(index * STEPS * SUBS, STEPS * SUBS)
        values = store[pl.ds(at, STEPS * SUBS), :]
        mixed_ref[pl.ds(at, STEPS * SUBS), :] = values.astype(BF16)
        for step in range(STEPS):
            value = values[step * SUBS : (step + 1) * SUBS]
            states = tuple(d * s + value for d, s in zip(decay, states))
        return states

    zeros = tuple(jnp.zeros((SUBS, LANES), F32) for _ in range(modes))
    return lax.fori_loop(0, steps // STEPS, turn, zeros)


def inner_kernel(
    seq_total,
    v_hbm, gate_hbm, taps_hbm, raw_hbm, raw_weights_hbm, tables_hbm,
    spec_ref, mixed_ref, state_ref, rates_ref, scaled_ref, v_first, gate_first, tables,
    v_rest, gate_rest, taps, raw, raw_weights, store, laid, sems,
):
    tiles, inner = mixed_ref.shape[0], v_rest.shape[1]

    def copies(tile):
        rows = pl.ds(tile * TILE, TILE)
        pairs = [(taps_hbm.at[rows], taps.at[rows])]
        for whole, head, rest in ((v_hbm, v_first, v_rest), (gate_hbm, gate_first, gate_rest)):
            pairs.append((whole.at[rows, pl.ds(0, BLOCK)], head.at[rows]))
            pairs.append((whole.at[rows, pl.ds(BLOCK, inner)], rest.at[rows]))
        return [pltpu.make_async_copy(*pair, sems.at[tile * 5 + i]) for i, pair in enumerate(pairs)]

    small = [
        pltpu.make_async_copy(tables_hbm, tables, sems.at[tiles * 5]),
        pltpu.make_async_copy(raw_hbm, raw, sems.at[tiles * 5 + 1]),
        pltpu.make_async_copy(raw_weights_hbm, raw_weights, sems.at[tiles * 5 + 2]),
    ]
    large = [copies(tile) for tile in range(tiles)]
    for copy in small + large[0]:
        copy.start()
    for copy in small + large[0]:
        copy.wait()
    sign = 1.0 - 2.0 * (lax.broadcasted_iota(jnp.int32, (1, 2 * BLOCK), 1) % 2).astype(F32)
    for tile in range(tiles):
        rows = slice(tile * TILE, (tile + 1) * TILE)
        groups = slice(tile * SUBS, (tile + 1) * SUBS)
        if tile:
            for copy in large[tile]:
                copy.wait()
        if tile + 1 < tiles:
            for copy in large[tile + 1]:
                copy.start()
        tap_hi, tap_lo = split(taps[rows])
        spectrum = mm(twice(tap_hi), tables[:, EVEN]) + mm(tap_lo, tables[:BLOCK, EVEN])
        turned = spectrum * sign
        spec_ref[rows] = turned
        earlier = mm(twice(v_first[rows]), tables[:, EVEN])
        for block in range(1, inner // BLOCK + 1):
            at = slice((block - 1) * BLOCK, block * BLOCK)
            later = mm(twice(v_rest[rows, at]), tables[:, ODD if block % 2 else EVEN])
            short = apply_window(earlier, later, spectrum if block % 2 else turned, tables)
            put_mixed(store, 0, block - 1, short, gate_rest[rows, at])
            earlier = later
        lay_out(raw.at[:, pl.ds(tile * TILE, TILE)], laid)
        modes = raw.shape[0]
        rates = laid[...].reshape(modes, SUBS, LANES)
        rates_ref[:, groups] = rates
        lay_out(raw_weights.at[:, pl.ds(tile * TILE, TILE)], laid)
        scaled_ref[:, groups] = laid[...].reshape(modes, SUBS, LANES) * jnp.sqrt(2.0 * rates + 2.0 / seq_total)
        for mode, state in enumerate(end_states(store, mixed_ref.at[tile], rates_ref.at[:, groups])):
            state_ref[mode, groups] = state


def rim_kernel(inner, place_ref, before_ref, v_ref, gate_ref, spec_ref, rates_ref, inner_ref, tables, *rest):
    mixed_ref, own_ref, twin_ref, store, ends = rest
    half = own_ref.shape[0]
    core = place_ref[0] % 2
    for tile in range(mixed_ref.shape[0]):
        rows = slice(tile * TILE, (tile + 1) * TILE)
        groups = slice(tile * SUBS, (tile + 1) * SUBS)
        earlier = mm(twice(before_ref[rows]), tables[:, ODD])
        later = mm(twice(v_ref[rows]), tables[:, EVEN])
        short = apply_window(earlier, later, spec_ref[rows], tables)
        put_mixed(store, 0, 0, short, gate_ref[rows])
        rates = rates_ref.at[:, groups]
        for mode, state in enumerate(end_states(store, mixed_ref.at[tile], rates)):
            ends[mode] = jnp.exp(-float(inner) * rates[mode]) * state + inner_ref[mode, groups]
        own_ref[:, groups] = ends[pl.ds(core * half, half)]
        twin_ref[:, groups] = ends[pl.ds((1 - core) * half, half)]


def decayed(rates, positions):
    return jnp.exp(-lax.convert_element_type(positions, F32) * rates)


def chip_kernel(tokens, place_ref, rates_ref, mine_ref, other_ref, total_ref):
    half = total_ref.shape[0]
    core = place_ref[0] % 2
    rates = rates_ref[pl.ds(core * half, half)]
    total_ref[...] = decayed(rates, tokens * (1 - core)) * mine_ref[...] + decayed(rates, tokens * core) * other_ref[...]


def level_kernel(tokens, size, place_ref, rates_ref, total_ref, other_ref, before_ref, joined_ref, after_ref):
    half = total_ref.shape[0]
    place = place_ref[0]
    upper = place // size % 2
    rates = rates_ref[pl.ds(place % 2 * half, half)]
    joined_ref[...] = (
        decayed(rates, tokens * size * (1 - upper)) * total_ref[...]
        + decayed(rates, tokens * size * upper) * other_ref[...]
    )
    reach = decayed(rates, tokens * (place % size // 2 * 2)) * other_ref[...]
    after_ref[...] = before_ref[...] + jnp.where(upper == 1, reach, 0.0)


def start_kernel(tokens, size, place_ref, rates_ref, other_ref, before_ref, own_ref, twin_ref, mine_ref, twins_ref):
    half = own_ref.shape[0]
    place = place_ref[0]
    core = place % 2
    upper = place // size % 2
    rates = rates_ref[pl.ds(core * half, half)]
    reach = decayed(rates, tokens * (place % size // 2 * 2)) * other_ref[...]
    first = before_ref[...] + jnp.where(upper == 1, reach, 0.0)
    second = decayed(rates, tokens) * first + jnp.where(core == 0, own_ref[...], twin_ref[...])
    mine_ref[...] = jnp.where(core == 0, first, second)
    twins_ref[...] = jnp.where(core == 0, second, first)


def added(terms):
    while len(terms) > 1:
        terms = [sum(terms[i : i + 2][1:], terms[i]) for i in range(0, len(terms), 2)]
    return terms[0]


def filtered(source, start, store, decay, scaled, bias, states):
    def turn(index, states):
        at = pl.multiple_of(index * LONG * SUBS, LONG * SUBS)
        values = source[pl.ds(start * SUBS + at, LONG * SUBS), :].astype(F32)
        sums = []
        for step in range(LONG):
            value = values[step * SUBS : (step + 1) * SUBS]
            states = tuple(d * s + value for d, s in zip(decay, states))
            sums.append(added([c * s for c, s in zip(scaled, states)] + [bias * value]))
        store[pl.ds(at, LONG * SUBS), :] = jnp.concatenate(sums, axis=0)
        return states

    return lax.fori_loop(0, BLOCK // LONG, turn, states)


def local_kernel(start, mixed_ref, rates_ref, scaled_ref, bias_ref, *rest):
    *earlier, sums_ref, states_ref = rest
    modes = rates_ref.shape[0]
    for tile in range(sums_ref.shape[0]):
        groups = slice(tile * SUBS, (tile + 1) * SUBS)
        decay = [jnp.exp(-rates_ref[mode, groups]) for mode in range(modes)]
        scaled = [scaled_ref[mode, groups] for mode in range(modes)]
        states = tuple(earlier[0][m, groups] if earlier else jnp.zeros((SUBS, LANES), F32) for m in range(modes))
        states = filtered(
            mixed_ref.at[tile], start, sums_ref.at[tile], decay, scaled, bias_ref[groups], states
        )
        for mode in range(modes):
            states_ref[mode, groups] = states[mode]


def half_modes(which, start_ref, rates_ref, scaled_ref, groups, past):
    half = start_ref.shape[0]
    rates = rates_ref[pl.ds(which * half, half), groups]
    states = scaled_ref[pl.ds(which * half, half), groups] * start_ref[:, groups]
    if past:
        states = states * jnp.exp(-float(past) * rates)
    decay = jnp.exp(-rates)
    return [decay[mode] for mode in range(half)], tuple(states[mode] for mode in range(half))


def add_carry(sums, into, decay, states):
    def turn(index, states):
        at = pl.multiple_of(index * LONG * SUBS, LONG * SUBS)
        for step in range(LONG):
            states = tuple(d * s for d, s in zip(decay, states))
            where = pl.ds(at + step * SUBS, SUBS)
            into[where, :] = sums[where, :] + added(list(states))
        return states

    return lax.fori_loop(0, BLOCK // LONG, turn, states)


def own_carry_kernel(place_ref, rates_ref, scaled_ref, mine_ref, *sums_refs):
    count = len(sums_refs) // 2
    for tile in range(sums_refs[0].shape[0]):
        groups = slice(tile * SUBS, (tile + 1) * SUBS)
        decay, states = half_modes(place_ref[0] % 2, mine_ref, rates_ref, scaled_ref, groups, 0)
        for before, after in zip(sums_refs[:count], sums_refs[count:]):
            states = add_carry(before.at[tile], after.at[tile], decay, states)


def outer_kernel(
    own_done, place_ref, mixed_ref, gate_ref, rates_ref, scaled_ref, bias_ref, mine_ref, twins_ref, local_ref, *rest
):
    *sums_refs, out_hbm, store, begin, out, sems = rest
    modes, half = rates_ref.shape[0], mine_ref.shape[0]
    core = place_ref[0] % 2
    begin[pl.ds(core * half, half)] = mine_ref[...]
    begin[pl.ds((1 - core) * half, half)] = twins_ref[...]
    blocks = len(sums_refs) + 1
    last = (blocks - 1) * BLOCK
    copies = []
    for tile in range(mixed_ref.shape[0]):
        groups = slice(tile * SUBS, (tile + 1) * SUBS)
        decay, states = half_modes(1 - core, twins_ref, rates_ref, scaled_ref, groups, 0)
        for block, sums_ref in enumerate(sums_refs):
            if block == own_done:
                more = half_modes(core, mine_ref, rates_ref, scaled_ref, groups, own_done * BLOCK)
                decay, states = decay + more[0], states + more[1]
            into = store.at[pl.ds(block * BLOCK * SUBS, BLOCK * SUBS)]
            states = add_carry(sums_ref.at[tile], into, decay, states)
        decay = [jnp.exp(-rates_ref[mode, groups]) for mode in range(modes)]
        scaled = [scaled_ref[mode, groups] for mode in range(modes)]
        full = tuple(
            local_ref[mode, groups] + jnp.exp(-float(last) * rates_ref[mode, groups]) * begin[mode, groups]
            for mode in range(modes)
        )
        into = store.at[pl.ds(last * SUBS, BLOCK * SUBS)]
        filtered(mixed_ref.at[tile], last - BLOCK, into, decay, scaled, bias_ref[groups], full)
        for group in range(SUBS):
            rows = slice(tile * TILE + group * LANES, tile * TILE + (group + 1) * LANES)
            for block in range(blocks):
                cols = slice(block * BLOCK, (block + 1) * BLOCK)
                turned = store[pl.ds(block * BLOCK * SUBS + group, BLOCK, stride=SUBS), :].T
                out[rows, cols] = (gate_ref[rows, cols].astype(F32) * turned).astype(BF16)
            copy = pltpu.make_async_copy(out.at[rows], out_hbm.at[rows], sems.at[tile * SUBS + group])
            copy.start()
            copies.append(copy)
    for copy in copies:
        copy.wait()


SCALAR = pl.BlockSpec(memory_space=pltpu.SMEM)
WHOLE = pl.BlockSpec(memory_space=pltpu.VMEM)
FAR = pl.BlockSpec(memory_space=pltpu.HBM)
OWN = 2
INNER_ROOM, RIM_ROOM = 32, 24


def steps_scratch(steps):
    return pltpu.VMEM((steps * SUBS, LANES), F32)


def kept_far(array):
    return pltpu.with_memory_space_constraint(array, pltpu.HBM)


def on_device(v_stream, gate_one, gate_two, short_filter, decay_rates, residues, skip_bias):
    real_channels, tokens = v_stream.shape
    modes = decay_rates.shape[1]
    shards = lax.axis_size("seq")
    before = lax.ppermute(v_stream[:, tokens - BLOCK :], "seq", [(i, i + 1) for i in range(shards - 1)])
    extra = -real_channels % TILE

    def padded(array):
        return jnp.pad(array, ((0, extra),) + ((0, 0),) * (array.ndim - 1)) if extra else array

    v_stream, gate_one, gate_two, short_filter = map(padded, (v_stream, gate_one, gate_two, short_filter))
    decay_rates, residues, skip_bias, before = map(padded, (decay_rates, residues, skip_bias, before))
    channels = real_channels + extra
    tiles, groups = channels // TILE, channels // LANES
    raw_rates, raw_weights = decay_rates.T, residues.T
    bias = skip_bias.reshape(groups, LANES)
    tables = jnp.asarray(window_tables())
    place = lax.axis_index("seq").astype(jnp.int32).reshape(1)
    inner = tokens - BLOCK
    shape = jax.ShapeDtypeStruct
    per_mode = shape((modes, groups, LANES), F32)
    half = shape((modes // 2, groups, LANES), F32)
    laid = pltpu.VMEM((modes * SUBS, LANES), F32)
    tap_spectra = shape((channels, 2 * BLOCK), F32)
    head = shape((channels, BLOCK), BF16)
    spectrum, inner_mixed, inner_state, rates, scaled, v_first, gate_first, tables = pl.pallas_call(
        functools.partial(inner_kernel, tokens * shards),
        in_specs=[FAR] * 6,
        out_specs=[WHOLE] * 8,
        out_shape=[tap_spectra, shape((tiles, inner * SUBS, LANES), BF16)] + [per_mode] * 3 + [head, head]
        + [shape(tables.shape, BF16)],
        scratch_shapes=[
            pltpu.VMEM((channels, inner), BF16),
            pltpu.VMEM((channels, inner), BF16),
            pltpu.VMEM((channels, BLOCK), F32),
            pltpu.VMEM((modes, channels), F32),
            pltpu.VMEM((modes, channels), F32),
            steps_scratch(inner),
            laid,
            pltpu.SemaphoreType.DMA((tiles * 5 + 3,)),
        ],
        compiler_params=pltpu.CompilerParams(vmem_limit_bytes=INNER_ROOM << 20),
        cost_estimate=pl.CostEstimate(
            flops=channels * inner * 2600, bytes_accessed=channels * tokens * 8, transcendentals=0
        ),
    )(*map(kept_far, (v_stream, gate_one, short_filter, raw_rates, raw_weights, tables)))
    rim_mixed, own_end, twin_half = pl.pallas_call(
        functools.partial(rim_kernel, inner),
        in_specs=[SCALAR] + [WHOLE] * 7,
        out_specs=[WHOLE] * 3,
        out_shape=[shape((tiles, BLOCK * SUBS, LANES), BF16), half, half],
        scratch_shapes=[steps_scratch(BLOCK), pltpu.VMEM((modes, SUBS, LANES), F32)],
        compiler_params=pltpu.CompilerParams(vmem_limit_bytes=RIM_ROOM << 20),
        cost_estimate=pl.CostEstimate(
            flops=channels * BLOCK * 2600, bytes_accessed=channels * BLOCK * 16, transcendentals=0
        ),
    )(place, before, v_first, gate_first, spectrum, rates, inner_state, tables)

    def swap(array, distance):
        return lax.ppermute(array, "seq", [(i, i ^ distance) for i in range(shards)])

    def small(kernel, outputs, *arrays):
        return pl.pallas_call(
            kernel,
            in_specs=[SCALAR] + [WHOLE] * (len(arrays) + 1),
            out_specs=[WHOLE] * outputs,
            out_shape=[half] * outputs,
            compiler_params=pltpu.CompilerParams(vmem_limit_bytes=8 << 20),
        )(place, rates, *arrays)

    sums, states = [], []

    def beside(arriving, sent):
        block = len(sums)
        if block >= tokens // BLOCK - 1:
            return arriving
        source, start = (inner_mixed, (block - 1) * BLOCK) if block else (rim_mixed, 0)
        source, *earlier, _ = lax.optimization_barrier((source, *states[-1:], sent))
        done = pl.pallas_call(
            functools.partial(local_kernel, start),
            in_specs=[WHOLE] * (4 + len(earlier)),
            out_specs=[WHOLE] * 2,
            out_shape=[shape((tiles, BLOCK * SUBS, LANES), F32), per_mode],
            compiler_params=pltpu.CompilerParams(vmem_limit_bytes=8 << 20),
            cost_estimate=pl.CostEstimate(
                flops=channels * BLOCK * 2600, bytes_accessed=channels * BLOCK * 16, transcendentals=0
            ),
        )(source, rates, scaled, bias, *earlier)
        arriving, total, state = lax.optimization_barrier((arriving, *done))
        sums.append(total)
        states.append(state)
        return arriving

    twin_end = swap(twin_half, 1)
    (total,) = small(functools.partial(chip_kernel, tokens), 1, own_end, twin_end)
    ahead = jnp.zeros(half.shape, F32)
    size = 2
    while 2 * size < shards:
        other = beside(swap(total, size), total)
        total, ahead = small(functools.partial(level_kernel, tokens, size), 2, total, other, ahead)
        size *= 2
    other = beside(swap(total, size), total)
    mine, twins = small(functools.partial(start_kernel, tokens, size), 2, other, ahead, own_end, twin_end)
    while len(sums) < tokens // BLOCK - 1:
        beside(total, total)
    twins = swap(twins, 1)
    sums[:OWN] = pl.pallas_call(
        own_carry_kernel,
        in_specs=[SCALAR] + [WHOLE] * (3 + OWN),
        out_specs=[WHOLE] * OWN,
        out_shape=[shape(sums[0].shape, F32)] * OWN,
        compiler_params=pltpu.CompilerParams(vmem_limit_bytes=8 << 20),
        cost_estimate=pl.CostEstimate(
            flops=channels * OWN * BLOCK * 600, bytes_accessed=channels * BLOCK * 16, transcendentals=0
        ),
    )(place, rates, scaled, mine, *sums[:OWN])

    hyena_out = pl.pallas_call(
        functools.partial(outer_kernel, OWN),
        in_specs=[SCALAR] + [WHOLE] * (8 + len(sums)),
        out_specs=FAR,
        out_shape=shape((channels, tokens), BF16),
        scratch_shapes=[
            steps_scratch(tokens),
            pltpu.VMEM((modes, groups, LANES), F32),
            pltpu.VMEM((channels, tokens), BF16),
            pltpu.SemaphoreType.DMA((groups,)),
        ],
        compiler_params=pltpu.CompilerParams(vmem_limit_bytes=24 << 20),
        cost_estimate=pl.CostEstimate(
            flops=channels * tokens * 50, bytes_accessed=channels * tokens * 6, transcendentals=0
        ),
    )(place, inner_mixed, gate_two, rates, scaled, bias, mine, twins, states[-1], *sums)
    return hyena_out[:real_channels]


def solution(mesh):
    in_specs = (
        P("chan", "seq"),
        P("chan", "seq"),
        P("chan", "seq"),
        P("chan", None),
        P("chan", None),
        P("chan", None),
        P("chan"),
    )
    out_specs = P("chan", "seq")
    return jax.shard_map(
        on_device, mesh=mesh, in_specs=in_specs, out_specs=out_specs, check_vma=False
    )
```

```python
import functools
import math

import jax
import jax.numpy as jnp
import numpy as np
from jax import lax
from jax.experimental import pallas as pl
from jax.experimental.pallas import tpu as pltpu
from jax.sharding import PartitionSpec as P

LANES = 128
SUBS = 8
TILE = LANES * SUBS
BLOCK = 128
ROWS = 1024
STEPS = 16
LONG = 32
F32, BF16 = jnp.float32, jnp.bfloat16


def halves(table):
    high = table.astype(jnp.bfloat16)
    low = (table - high.astype(np.float64)).astype(jnp.bfloat16)
    return high, low


def window_tables():
    size = 2 * BLOCK
    phase = 2.0 * math.pi / size * np.outer(np.arange(size), np.arange(BLOCK) + 0.5)
    forward = np.concatenate([np.cos(phase), -np.sin(phase)], axis=1)
    signs = np.tile((-1.0) ** np.arange(BLOCK), 2)
    inverse = forward[BLOCK:].T / BLOCK
    even = np.concatenate(halves(forward[:BLOCK]), axis=0)
    odd = np.concatenate(halves(forward[:BLOCK] * signs), axis=0)
    back = np.concatenate(halves(inverse), axis=1)
    return np.concatenate([even, odd, back], axis=1)


EVEN, ODD, BACK = (slice(i * 2 * BLOCK, (i + 1) * 2 * BLOCK) for i in range(3))


def mm(left, right):
    return jnp.dot(left, right, preferred_element_type=F32)


def split(value):
    high = value.astype(BF16)
    return high, (value - high.astype(F32)).astype(BF16)


def twice(block):
    return jnp.concatenate([block, block], axis=1)


def parts(image):
    return image[:, :BLOCK], image[:, BLOCK:]


def apply_window(earlier, later, spectrum, tables):
    (e_re, e_im), (l_re, l_im), (h_re, h_im) = parts(earlier), parts(later), parts(spectrum)
    re, im = e_re + l_im, e_im - l_re
    high, low = split(jnp.concatenate([re * h_re - im * h_im, re * h_im + im * h_re], axis=1))
    both = mm(high, tables[:, BACK])
    return both[:, :BLOCK] + both[:, BLOCK:] + mm(low, tables[:, BACK][:, :BLOCK])


def put_mixed(store, first_row, block_at, short, gate):
    mixed = (gate.astype(F32) * short).astype(BF16).astype(F32)
    for piece in range(ROWS // LANES):
        group = first_row // LANES + piece
        turned = mixed[piece * LANES : (piece + 1) * LANES].T
        store[pl.ds(block_at * BLOCK * SUBS + group, BLOCK, stride=SUBS), :] = turned


def lay_out(rows_ref, store):
    modes = rows_ref.shape[0]
    for group in range(SUBS):
        store[pl.ds(group, modes, stride=SUBS), :] = rows_ref[:, group * LANES : (group + 1) * LANES]


def end_states(store, mixed_ref, rates_ref):
    modes = rates_ref.shape[0]
    steps = store.shape[0] // SUBS
    decay = [jnp.exp(-rates_ref[mode]) for mode in range(modes)]

    def turn(index, states):
        at = pl.multiple_of(index * STEPS * SUBS, STEPS * SUBS)
        values = store[pl.ds(at, STEPS * SUBS), :]
        mixed_ref[pl.ds(at, STEPS * SUBS), :] = values.astype(BF16)
        for step in range(STEPS):
            value = values[step * SUBS : (step + 1) * SUBS]
            states = tuple(d * s + value for d, s in zip(decay, states))
        return states

    zeros = tuple(jnp.zeros((SUBS, LANES), F32) for _ in range(modes))
    return lax.fori_loop(0, steps // STEPS, turn, zeros)


def inner_kernel(
    seq_total,
    v_hbm, gate_hbm, taps_hbm, raw_hbm, raw_weights_hbm, tables_hbm,
    spec_ref, mixed_ref, state_ref, rates_ref, scaled_ref, v_first, gate_first, tables,
    v_rest, gate_rest, taps, raw, raw_weights, store, laid, sems,
):
    tiles, inner = mixed_ref.shape[0], v_rest.shape[1]

    def copies(tile):
        rows = pl.ds(tile * TILE, TILE)
        pairs = [(taps_hbm.at[rows], taps.at[rows])]
        for whole, head, rest in ((v_hbm, v_first, v_rest), (gate_hbm, gate_first, gate_rest)):
            pairs.append((whole.at[rows, pl.ds(0, BLOCK)], head.at[rows]))
            pairs.append((whole.at[rows, pl.ds(BLOCK, inner)], rest.at[rows]))
        return [pltpu.make_async_copy(*pair, sems.at[tile * 5 + i]) for i, pair in enumerate(pairs)]

    small = [
        pltpu.make_async_copy(tables_hbm, tables, sems.at[tiles * 5]),
        pltpu.make_async_copy(raw_hbm, raw, sems.at[tiles * 5 + 1]),
        pltpu.make_async_copy(raw_weights_hbm, raw_weights, sems.at[tiles * 5 + 2]),
    ]
    large = [copies(tile) for tile in range(tiles)]
    for copy in small + large[0]:
        copy.start()
    for copy in small + large[0]:
        copy.wait()
    sign = 1.0 - 2.0 * (lax.broadcasted_iota(jnp.int32, (1, 2 * BLOCK), 1) % 2).astype(F32)
    for tile in range(tiles):
        rows = slice(tile * TILE, (tile + 1) * TILE)
        groups = slice(tile * SUBS, (tile + 1) * SUBS)
        if tile:
            for copy in large[tile]:
                copy.wait()
        if tile + 1 < tiles:
            for copy in large[tile + 1]:
                copy.start()
        tap_hi, tap_lo = split(taps[rows])
        spectrum = mm(twice(tap_hi), tables[:, EVEN]) + mm(tap_lo, tables[:BLOCK, EVEN])
        turned = spectrum * sign
        spec_ref[rows] = turned
        earlier = mm(twice(v_first[rows]), tables[:, EVEN])
        for block in range(1, inner // BLOCK + 1):
            at = slice((block - 1) * BLOCK, block * BLOCK)
            later = mm(twice(v_rest[rows, at]), tables[:, ODD if block % 2 else EVEN])
            short = apply_window(earlier, later, spectrum if block % 2 else turned, tables)
            put_mixed(store, 0, block - 1, short, gate_rest[rows, at])
            earlier = later
        lay_out(raw.at[:, pl.ds(tile * TILE, TILE)], laid)
        modes = raw.shape[0]
        rates = laid[...].reshape(modes, SUBS, LANES)
        rates_ref[:, groups] = rates
        lay_out(raw_weights.at[:, pl.ds(tile * TILE, TILE)], laid)
        scaled_ref[:, groups] = laid[...].reshape(modes, SUBS, LANES) * jnp.sqrt(2.0 * rates + 2.0 / seq_total)
        for mode, state in enumerate(end_states(store, mixed_ref.at[tile], rates_ref.at[:, groups])):
            state_ref[mode, groups] = state


def rim_kernel(inner, place_ref, before_ref, v_ref, gate_ref, spec_ref, rates_ref, inner_ref, tables, *rest):
    mixed_ref, own_ref, twin_ref, store, ends = rest
    half = own_ref.shape[0]
    core = place_ref[0] % 2
    for tile in range(mixed_ref.shape[0]):
        rows = slice(tile * TILE, (tile + 1) * TILE)
        groups = slice(tile * SUBS, (tile + 1) * SUBS)
        earlier = mm(twice(before_ref[rows]), tables[:, ODD])
        later = mm(twice(v_ref[rows]), tables[:, EVEN])
        short = apply_window(earlier, later, spec_ref[rows], tables)
        put_mixed(store, 0, 0, short, gate_ref[rows])
        rates = rates_ref.at[:, groups]
        for mode, state in enumerate(end_states(store, mixed_ref.at[tile], rates)):
            ends[mode] = jnp.exp(-float(inner) * rates[mode]) * state + inner_ref[mode, groups]
        own_ref[:, groups] = ends[pl.ds(core * half, half)]
        twin_ref[:, groups] = ends[pl.ds((1 - core) * half, half)]


def decayed(rates, positions):
    return jnp.exp(-lax.convert_element_type(positions, F32) * rates)


def chip_kernel(tokens, place_ref, rates_ref, mine_ref, other_ref, total_ref):
    half = total_ref.shape[0]
    core = place_ref[0] % 2
    rates = rates_ref[pl.ds(core * half, half)]
    total_ref[...] = decayed(rates, tokens * (1 - core)) * mine_ref[...] + decayed(rates, tokens * core) * other_ref[...]


def level_kernel(tokens, size, place_ref, rates_ref, total_ref, other_ref, before_ref, joined_ref, after_ref):
    half = total_ref.shape[0]
    place = place_ref[0]
    upper = place // size % 2
    rates = rates_ref[pl.ds(place % 2 * half, half)]
    joined_ref[...] = (
        decayed(rates, tokens * size * (1 - upper)) * total_ref[...]
        + decayed(rates, tokens * size * upper) * other_ref[...]
    )
    reach = decayed(rates, tokens * (place % size // 2 * 2)) * other_ref[...]
    after_ref[...] = before_ref[...] + jnp.where(upper == 1, reach, 0.0)


def start_kernel(tokens, size, place_ref, rates_ref, other_ref, before_ref, own_ref, twin_ref, mine_ref, twins_ref):
    half = own_ref.shape[0]
    place = place_ref[0]
    core = place % 2
    upper = place // size % 2
    rates = rates_ref[pl.ds(core * half, half)]
    reach = decayed(rates, tokens * (place % size // 2 * 2)) * other_ref[...]
    first = before_ref[...] + jnp.where(upper == 1, reach, 0.0)
    second = decayed(rates, tokens) * first + jnp.where(core == 0, own_ref[...], twin_ref[...])
    mine_ref[...] = jnp.where(core == 0, first, second)
    twins_ref[...] = jnp.where(core == 0, second, first)


def added(terms):
    while len(terms) > 1:
        terms = [sum(terms[i : i + 2][1:], terms[i]) for i in range(0, len(terms), 2)]
    return terms[0]


def filtered(source, start, store, decay, scaled, bias, states):
    def turn(index, states):
        at = pl.multiple_of(index * LONG * SUBS, LONG * SUBS)
        values = source[pl.ds(start * SUBS + at, LONG * SUBS), :].astype(F32)
        sums = []
        for step in range(LONG):
            value = values[step * SUBS : (step + 1) * SUBS]
            states = tuple(d * s + value for d, s in zip(decay, states))
            sums.append(added([c * s for c, s in zip(scaled, states)] + [bias * value]))
        store[pl.ds(at, LONG * SUBS), :] = jnp.concatenate(sums, axis=0)
        return states

    return lax.fori_loop(0, BLOCK // LONG, turn, states)


def local_kernel(units, known, kept, rim_ref, inner_ref, rates_ref, scaled_ref, bias_ref, *rest):
    earlier, sums_refs, states_refs = rest[: len(known)], rest[len(known) :][: len(units)], rest[len(known) + len(units) :]
    modes = rates_ref.shape[0]
    held = {tile: tuple(ref[mode] for mode in range(modes)) for tile, ref in zip(known, earlier)}
    for (block, tile), sums_ref in zip(units, sums_refs):
        groups = slice(tile * SUBS, (tile + 1) * SUBS)
        decay = [jnp.exp(-rates_ref[mode, groups]) for mode in range(modes)]
        scaled = [scaled_ref[mode, groups] for mode in range(modes)]
        states = held.get(tile, tuple(jnp.zeros((SUBS, LANES), F32) for _ in range(modes)))
        source, start = (inner_ref, (block - 1) * BLOCK) if block else (rim_ref, 0)
        held[tile] = filtered(source.at[tile], start, sums_ref, decay, scaled, bias_ref[groups], states)
    for tile, states_ref in zip(kept, states_refs):
        for mode in range(modes):
            states_ref[mode] = held[tile][mode]


def half_modes(which, start_ref, rates_ref, scaled_ref, groups, past):
    half = start_ref.shape[0]
    rates = rates_ref[pl.ds(which * half, half), groups]
    states = scaled_ref[pl.ds(which * half, half), groups] * start_ref[:, groups]
    if past:
        states = states * jnp.exp(-float(past) * rates)
    decay = jnp.exp(-rates)
    return [decay[mode] for mode in range(half)], tuple(states[mode] for mode in range(half))


def add_carry(sums, into, decay, states):
    def turn(index, states):
        at = pl.multiple_of(index * LONG * SUBS, LONG * SUBS)
        for step in range(LONG):
            states = tuple(d * s for d, s in zip(decay, states))
            where = pl.ds(at + step * SUBS, SUBS)
            into[where, :] = sums[where, :] + added(list(states))
        return states

    return lax.fori_loop(0, BLOCK // LONG, turn, states)


def own_carry_kernel(tiles, place_ref, rates_ref, scaled_ref, mine_ref, *sums_refs):
    count = len(sums_refs) // 2
    for tile in range(tiles):
        groups = slice(tile * SUBS, (tile + 1) * SUBS)
        decay, states = half_modes(place_ref[0] % 2, mine_ref, rates_ref, scaled_ref, groups, 0)
        for unit in range(tile, count, tiles):
            states = add_carry(sums_refs[unit], sums_refs[count + unit], decay, states)


def outer_kernel(tiles, own_done, place_ref, gate_ref, rates_ref, scaled_ref, mine_ref, twins_ref, *rest):
    *sums_refs, out_hbm, store, out, sems = rest
    core = place_ref[0] % 2
    blocks = len(sums_refs) // tiles
    copies = []
    for tile in range(tiles):
        groups = slice(tile * SUBS, (tile + 1) * SUBS)
        decay, states = half_modes(1 - core, twins_ref, rates_ref, scaled_ref, groups, 0)
        for block in range(blocks):
            if block == own_done:
                more = half_modes(core, mine_ref, rates_ref, scaled_ref, groups, own_done * BLOCK)
                decay, states = decay + more[0], states + more[1]
            into = store.at[pl.ds(block * BLOCK * SUBS, BLOCK * SUBS)]
            states = add_carry(sums_refs[block * tiles + tile], into, decay, states)
        for group in range(SUBS):
            rows = slice(tile * TILE + group * LANES, tile * TILE + (group + 1) * LANES)
            for block in range(blocks):
                cols = slice(block * BLOCK, (block + 1) * BLOCK)
                turned = store[pl.ds(block * BLOCK * SUBS + group, BLOCK, stride=SUBS), :].T
                out[rows, cols] = (gate_ref[rows, cols].astype(F32) * turned).astype(BF16)
            copy = pltpu.make_async_copy(out.at[rows], out_hbm.at[rows], sems.at[tile * SUBS + group])
            copy.start()
            copies.append(copy)
    for copy in copies:
        copy.wait()


SCALAR = pl.BlockSpec(memory_space=pltpu.SMEM)
WHOLE = pl.BlockSpec(memory_space=pltpu.VMEM)
FAR = pl.BlockSpec(memory_space=pltpu.HBM)
OWN = 2
INNER_ROOM, RIM_ROOM = 32, 24


def steps_scratch(steps):
    return pltpu.VMEM((steps * SUBS, LANES), F32)


def kept_far(array):
    return pltpu.with_memory_space_constraint(array, pltpu.HBM)


def on_device(v_stream, gate_one, gate_two, short_filter, decay_rates, residues, skip_bias):
    real_channels, tokens = v_stream.shape
    modes = decay_rates.shape[1]
    shards = lax.axis_size("seq")
    before = lax.ppermute(v_stream[:, tokens - BLOCK :], "seq", [(i, i + 1) for i in range(shards - 1)])
    extra = -real_channels % TILE

    def padded(array):
        return jnp.pad(array, ((0, extra),) + ((0, 0),) * (array.ndim - 1)) if extra else array

    v_stream, gate_one, gate_two, short_filter = map(padded, (v_stream, gate_one, gate_two, short_filter))
    decay_rates, residues, skip_bias, before = map(padded, (decay_rates, residues, skip_bias, before))
    channels = real_channels + extra
    tiles, groups = channels // TILE, channels // LANES
    raw_rates, raw_weights = decay_rates.T, residues.T
    bias = skip_bias.reshape(groups, LANES)
    tables = jnp.asarray(window_tables())
    place = lax.axis_index("seq").astype(jnp.int32).reshape(1)
    inner = tokens - BLOCK
    shape = jax.ShapeDtypeStruct
    per_mode = shape((modes, groups, LANES), F32)
    half = shape((modes // 2, groups, LANES), F32)
    laid = pltpu.VMEM((modes * SUBS, LANES), F32)
    tap_spectra = shape((channels, 2 * BLOCK), F32)
    head = shape((channels, BLOCK), BF16)
    spectrum, inner_mixed, inner_state, rates, scaled, v_first, gate_first, tables = pl.pallas_call(
        functools.partial(inner_kernel, tokens * shards),
        in_specs=[FAR] * 6,
        out_specs=[WHOLE] * 8,
        out_shape=[tap_spectra, shape((tiles, inner * SUBS, LANES), BF16)] + [per_mode] * 3 + [head, head]
        + [shape(tables.shape, BF16)],
        scratch_shapes=[
            pltpu.VMEM((channels, inner), BF16),
            pltpu.VMEM((channels, inner), BF16),
            pltpu.VMEM((channels, BLOCK), F32),
            pltpu.VMEM((modes, channels), F32),
            pltpu.VMEM((modes, channels), F32),
            steps_scratch(inner),
            laid,
            pltpu.SemaphoreType.DMA((tiles * 5 + 3,)),
        ],
        compiler_params=pltpu.CompilerParams(vmem_limit_bytes=INNER_ROOM << 20),
        cost_estimate=pl.CostEstimate(
            flops=channels * inner * 2600, bytes_accessed=channels * tokens * 8, transcendentals=0
        ),
    )(*map(kept_far, (v_stream, gate_one, short_filter, raw_rates, raw_weights, tables)))
    rim_mixed, own_end, twin_half = pl.pallas_call(
        functools.partial(rim_kernel, inner),
        in_specs=[SCALAR] + [WHOLE] * 7,
        out_specs=[WHOLE] * 3,
        out_shape=[shape((tiles, BLOCK * SUBS, LANES), BF16), half, half],
        scratch_shapes=[steps_scratch(BLOCK), pltpu.VMEM((modes, SUBS, LANES), F32)],
        compiler_params=pltpu.CompilerParams(vmem_limit_bytes=RIM_ROOM << 20),
        cost_estimate=pl.CostEstimate(
            flops=channels * BLOCK * 2600, bytes_accessed=channels * BLOCK * 16, transcendentals=0
        ),
    )(place, before, v_first, gate_first, spectrum, rates, inner_state, tables)

    def swap(array, distance):
        return lax.ppermute(array, "seq", [(i, i ^ distance) for i in range(shards)])

    def small(kernel, outputs, *arrays):
        return pl.pallas_call(
            kernel,
            in_specs=[SCALAR] + [WHOLE] * (len(arrays) + 1),
            out_specs=[WHOLE] * outputs,
            out_shape=[half] * outputs,
            compiler_params=pltpu.CompilerParams(vmem_limit_bytes=8 << 20),
        )(place, rates, *arrays)

    blocks = tokens // BLOCK
    sums, states = [], {}
    one_tile = shape((modes, SUBS, LANES), F32)

    def beside(arriving, sent, count):
        units = [divmod(len(sums) + i, tiles) for i in range(count) if len(sums) + i < blocks * tiles]
        if not units:
            return arriving
        touched = sorted({tile for _, tile in units})
        known = [tile for tile in touched if tile in states]
        kept = [tile for tile in touched if (blocks - 1, tile) not in units]
        rim, *earlier, _ = lax.optimization_barrier((rim_mixed, *(states[tile] for tile in known), sent))
        done = pl.pallas_call(
            functools.partial(local_kernel, units, known, kept),
            in_specs=[WHOLE] * (5 + len(known)),
            out_specs=[WHOLE] * (len(units) + len(kept)),
            out_shape=[shape((BLOCK * SUBS, LANES), F32)] * len(units) + [one_tile] * len(kept),
            compiler_params=pltpu.CompilerParams(vmem_limit_bytes=8 << 20),
            cost_estimate=pl.CostEstimate(
                flops=len(units) * TILE * BLOCK * 2600, bytes_accessed=TILE * BLOCK * 16, transcendentals=0
            ),
        )(rim, inner_mixed, rates, scaled, bias, *earlier)
        arriving, *done = lax.optimization_barrier((arriving, *done))
        sums.extend(done[: len(units)])
        states.update(zip(kept, done[len(units) :]))
        return arriving

    levels = shards.bit_length() - 2
    early = blocks * tiles // 8
    quotas = [(blocks * tiles - early + levels - 1 - i) // levels for i in range(levels)]
    twin_end = beside(swap(twin_half, 1), twin_half, early)
    (total,) = small(functools.partial(chip_kernel, tokens), 1, own_end, twin_end)
    ahead = jnp.zeros(half.shape, F32)
    size = 2
    for quota in quotas[:-1]:
        other = beside(swap(total, size), total, quota)
        total, ahead = small(functools.partial(level_kernel, tokens, size), 2, total, other, ahead)
        size *= 2
    other = beside(swap(total, size), total, quotas[-1])
    mine, twins = small(functools.partial(start_kernel, tokens, size), 2, other, ahead, own_end, twin_end)
    twins = swap(twins, 1)
    own = OWN * tiles
    sums[:own] = pl.pallas_call(
        functools.partial(own_carry_kernel, tiles),
        in_specs=[SCALAR] + [WHOLE] * (3 + own),
        out_specs=[WHOLE] * own,
        out_shape=[shape(sums[0].shape, F32)] * own,
        compiler_params=pltpu.CompilerParams(vmem_limit_bytes=8 << 20),
        cost_estimate=pl.CostEstimate(
            flops=channels * OWN * BLOCK * 600, bytes_accessed=channels * BLOCK * 16, transcendentals=0
        ),
    )(place, rates, scaled, mine, *sums[:own])

    hyena_out = pl.pallas_call(
        functools.partial(outer_kernel, tiles, OWN),
        in_specs=[SCALAR] + [WHOLE] * (5 + len(sums)),
        out_specs=FAR,
        out_shape=shape((channels, tokens), BF16),
        scratch_shapes=[
            steps_scratch(tokens),
            pltpu.VMEM((channels, tokens), BF16),
            pltpu.SemaphoreType.DMA((groups,)),
        ],
        compiler_params=pltpu.CompilerParams(vmem_limit_bytes=24 << 20),
        cost_estimate=pl.CostEstimate(
            flops=channels * tokens * 50, bytes_accessed=channels * tokens * 6, transcendentals=0
        ),
    )(place, gate_two, rates, scaled, mine, twins, *sums)
    return hyena_out[:real_channels]


def solution(mesh):
    in_specs = (
        P("chan", "seq"),
        P("chan", "seq"),
        P("chan", "seq"),
        P("chan", None),
        P("chan", None),
        P("chan", None),
        P("chan"),
    )
    out_specs = P("chan", "seq")
    return jax.shard_map(
        on_device, mesh=mesh, in_specs=in_specs, out_specs=out_specs, check_vma=False
    )
```

```python
import functools
import math

import jax
import jax.numpy as jnp
import numpy as np
from jax import lax
from jax.experimental import pallas as pl
from jax.experimental.pallas import tpu as pltpu
from jax.sharding import PartitionSpec as P

LANES = 128
SUBS = 8
TILE = LANES * SUBS
BLOCK = 128
ROWS = 1024
STEPS = 16
LONG = 32
F32, BF16 = jnp.float32, jnp.bfloat16


def halves(table):
    high = table.astype(jnp.bfloat16)
    low = (table - high.astype(np.float64)).astype(jnp.bfloat16)
    return high, low


def window_tables():
    size = 2 * BLOCK
    phase = 2.0 * math.pi / size * np.outer(np.arange(size), np.arange(BLOCK) + 0.5)
    forward = np.concatenate([np.cos(phase), -np.sin(phase)], axis=1)
    signs = np.tile((-1.0) ** np.arange(BLOCK), 2)
    inverse = forward[BLOCK:].T / BLOCK
    even = np.concatenate(halves(forward[:BLOCK]), axis=0)
    odd = np.concatenate(halves(forward[:BLOCK] * signs), axis=0)
    back = np.concatenate(halves(inverse), axis=1)
    return np.concatenate([even, odd, back], axis=1)


EVEN, ODD, BACK = (slice(i * 2 * BLOCK, (i + 1) * 2 * BLOCK) for i in range(3))


def mm(left, right):
    return jnp.dot(left, right, preferred_element_type=F32)


def split(value):
    high = value.astype(BF16)
    return high, (value - high.astype(F32)).astype(BF16)


def twice(block):
    return jnp.concatenate([block, block], axis=1)


def parts(image):
    return image[:, :BLOCK], image[:, BLOCK:]


def apply_window(earlier, later, spectrum, tables):
    (e_re, e_im), (l_re, l_im), (h_re, h_im) = parts(earlier), parts(later), parts(spectrum)
    re, im = e_re + l_im, e_im - l_re
    product = jnp.concatenate([re * h_re - im * h_im, re * h_im + im * h_re], axis=1)
    both = mm(product.astype(BF16), tables[:, BACK])
    return both[:, :BLOCK] + both[:, BLOCK:]


def put_mixed(store, first_row, block_at, short, gate):
    mixed = (gate.astype(F32) * short).astype(BF16).astype(F32)
    for piece in range(ROWS // LANES):
        group = first_row // LANES + piece
        turned = mixed[piece * LANES : (piece + 1) * LANES].T
        store[pl.ds(block_at * BLOCK * SUBS + group, BLOCK, stride=SUBS), :] = turned


def lay_out(rows_ref, store):
    modes = rows_ref.shape[0]
    for group in range(SUBS):
        store[pl.ds(group, modes, stride=SUBS), :] = rows_ref[:, group * LANES : (group + 1) * LANES]


def end_states(store, mixed_ref, rates_ref):
    modes = rates_ref.shape[0]
    steps = store.shape[0] // SUBS
    decay = [jnp.exp(-rates_ref[mode]) for mode in range(modes)]

    def turn(index, states):
        at = pl.multiple_of(index * STEPS * SUBS, STEPS * SUBS)
        values = store[pl.ds(at, STEPS * SUBS), :]
        mixed_ref[pl.ds(at, STEPS * SUBS), :] = values.astype(BF16)
        for step in range(STEPS):
            value = values[step * SUBS : (step + 1) * SUBS]
            states = tuple(d * s + value for d, s in zip(decay, states))
        return states

    zeros = tuple(jnp.zeros((SUBS, LANES), F32) for _ in range(modes))
    return lax.fori_loop(0, steps // STEPS, turn, zeros)


def inner_kernel(
    seq_total,
    v_hbm, gate_hbm, taps_hbm, raw_hbm, raw_weights_hbm, tables_hbm,
    spec_ref, mixed_ref, state_ref, rates_ref, scaled_ref, v_first, gate_first, tables,
    v_rest, gate_rest, taps, raw, raw_weights, store, laid, sems,
):
    tiles, inner = mixed_ref.shape[0], v_rest.shape[1]

    def copies(tile):
        rows = pl.ds(tile * TILE, TILE)
        pairs = [(taps_hbm.at[rows], taps.at[rows])]
        for whole, head, rest in ((v_hbm, v_first, v_rest), (gate_hbm, gate_first, gate_rest)):
            pairs.append((whole.at[rows, pl.ds(0, BLOCK)], head.at[rows]))
            pairs.append((whole.at[rows, pl.ds(BLOCK, inner)], rest.at[rows]))
        return [pltpu.make_async_copy(*pair, sems.at[tile * 5 + i]) for i, pair in enumerate(pairs)]

    small = [
        pltpu.make_async_copy(tables_hbm, tables, sems.at[tiles * 5]),
        pltpu.make_async_copy(raw_hbm, raw, sems.at[tiles * 5 + 1]),
        pltpu.make_async_copy(raw_weights_hbm, raw_weights, sems.at[tiles * 5 + 2]),
    ]
    large = [copies(tile) for tile in range(tiles)]
    for copy in small + large[0]:
        copy.start()
    for copy in small + large[0]:
        copy.wait()
    sign = 1.0 - 2.0 * (lax.broadcasted_iota(jnp.int32, (1, 2 * BLOCK), 1) % 2).astype(F32)
    for tile in range(tiles):
        rows = slice(tile * TILE, (tile + 1) * TILE)
        groups = slice(tile * SUBS, (tile + 1) * SUBS)
        if tile:
            for copy in large[tile]:
                copy.wait()
        if tile + 1 < tiles:
            for copy in large[tile + 1]:
                copy.start()
        tap_hi, tap_lo = split(taps[rows])
        spectrum = mm(twice(tap_hi), tables[:, EVEN]) + mm(tap_lo, tables[:BLOCK, EVEN])
        turned = spectrum * sign
        spec_ref[rows] = turned
        earlier = mm(twice(v_first[rows]), tables[:, EVEN])
        for block in range(1, inner // BLOCK + 1):
            at = slice((block - 1) * BLOCK, block * BLOCK)
            later = mm(twice(v_rest[rows, at]), tables[:, ODD if block % 2 else EVEN])
            short = apply_window(earlier, later, spectrum if block % 2 else turned, tables)
            put_mixed(store, 0, block - 1, short, gate_rest[rows, at])
            earlier = later
        lay_out(raw.at[:, pl.ds(tile * TILE, TILE)], laid)
        modes = raw.shape[0]
        rates = laid[...].reshape(modes, SUBS, LANES)
        rates_ref[:, groups] = rates
        lay_out(raw_weights.at[:, pl.ds(tile * TILE, TILE)], laid)
        scaled_ref[:, groups] = laid[...].reshape(modes, SUBS, LANES) * jnp.sqrt(2.0 * rates + 2.0 / seq_total)
        for mode, state in enumerate(end_states(store, mixed_ref.at[tile], rates_ref.at[:, groups])):
            state_ref[mode, groups] = state


def rim_kernel(inner, place_ref, before_ref, v_ref, gate_ref, spec_ref, rates_ref, inner_ref, tables, *rest):
    mixed_ref, own_ref, twin_ref, store, ends = rest
    half = own_ref.shape[0]
    core = place_ref[0] % 2
    for tile in range(mixed_ref.shape[0]):
        rows = slice(tile * TILE, (tile + 1) * TILE)
        groups = slice(tile * SUBS, (tile + 1) * SUBS)
        earlier = mm(twice(before_ref[rows]), tables[:, ODD])
        later = mm(twice(v_ref[rows]), tables[:, EVEN])
        short = apply_window(earlier, later, spec_ref[rows], tables)
        put_mixed(store, 0, 0, short, gate_ref[rows])
        rates = rates_ref.at[:, groups]
        for mode, state in enumerate(end_states(store, mixed_ref.at[tile], rates)):
            ends[mode] = jnp.exp(-float(inner) * rates[mode]) * state + inner_ref[mode, groups]
        own_ref[:, groups] = ends[pl.ds(core * half, half)]
        twin_ref[:, groups] = ends[pl.ds((1 - core) * half, half)]


def decayed(rates, positions):
    return jnp.exp(-lax.convert_element_type(positions, F32) * rates)


def chip_kernel(tokens, place_ref, rates_ref, mine_ref, other_ref, total_ref):
    half = total_ref.shape[0]
    core = place_ref[0] % 2
    rates = rates_ref[pl.ds(core * half, half)]
    total_ref[...] = decayed(rates, tokens * (1 - core)) * mine_ref[...] + decayed(rates, tokens * core) * other_ref[...]


def level_kernel(tokens, size, place_ref, rates_ref, total_ref, other_ref, before_ref, joined_ref, after_ref):
    half = total_ref.shape[0]
    place = place_ref[0]
    upper = place // size % 2
    rates = rates_ref[pl.ds(place % 2 * half, half)]
    joined_ref[...] = (
        decayed(rates, tokens * size * (1 - upper)) * total_ref[...]
        + decayed(rates, tokens * size * upper) * other_ref[...]
    )
    reach = decayed(rates, tokens * (place % size // 2 * 2)) * other_ref[...]
    after_ref[...] = before_ref[...] + jnp.where(upper == 1, reach, 0.0)


def start_kernel(tokens, size, place_ref, rates_ref, other_ref, before_ref, own_ref, twin_ref, mine_ref, twins_ref):
    half = own_ref.shape[0]
    place = place_ref[0]
    core = place % 2
    upper = place // size % 2
    rates = rates_ref[pl.ds(core * half, half)]
    reach = decayed(rates, tokens * (place % size // 2 * 2)) * other_ref[...]
    first = before_ref[...] + jnp.where(upper == 1, reach, 0.0)
    second = decayed(rates, tokens) * first + jnp.where(core == 0, own_ref[...], twin_ref[...])
    mine_ref[...] = jnp.where(core == 0, first, second)
    twins_ref[...] = jnp.where(core == 0, second, first)


def added(terms):
    while len(terms) > 1:
        terms = [sum(terms[i : i + 2][1:], terms[i]) for i in range(0, len(terms), 2)]
    return terms[0]


def filtered(source, start, store, decay, scaled, bias, states):
    def turn(index, states):
        at = pl.multiple_of(index * LONG * SUBS, LONG * SUBS)
        values = source[pl.ds(start * SUBS + at, LONG * SUBS), :].astype(F32)
        sums = []
        for step in range(LONG):
            value = values[step * SUBS : (step + 1) * SUBS]
            states = tuple(d * s + value for d, s in zip(decay, states))
            sums.append(added([c * s for c, s in zip(scaled, states)] + [bias * value]))
        store[pl.ds(at, LONG * SUBS), :] = jnp.concatenate(sums, axis=0)
        return states

    return lax.fori_loop(0, BLOCK // LONG, turn, states)


def local_kernel(units, known, kept, rim_ref, inner_ref, rates_ref, scaled_ref, bias_ref, *rest):
    earlier, sums_refs, states_refs = rest[: len(known)], rest[len(known) :][: len(units)], rest[len(known) + len(units) :]
    modes = rates_ref.shape[0]
    held = {tile: tuple(ref[mode] for mode in range(modes)) for tile, ref in zip(known, earlier)}
    for (block, tile), sums_ref in zip(units, sums_refs):
        groups = slice(tile * SUBS, (tile + 1) * SUBS)
        decay = [jnp.exp(-rates_ref[mode, groups]) for mode in range(modes)]
        scaled = [scaled_ref[mode, groups] for mode in range(modes)]
        states = held.get(tile, tuple(jnp.zeros((SUBS, LANES), F32) for _ in range(modes)))
        source, start = (inner_ref, (block - 1) * BLOCK) if block else (rim_ref, 0)
        held[tile] = filtered(source.at[tile], start, sums_ref, decay, scaled, bias_ref[groups], states)
    for tile, states_ref in zip(kept, states_refs):
        for mode in range(modes):
            states_ref[mode] = held[tile][mode]


def half_modes(which, start_ref, rates_ref, scaled_ref, groups, past):
    half = start_ref.shape[0]
    rates = rates_ref[pl.ds(which * half, half), groups]
    states = scaled_ref[pl.ds(which * half, half), groups] * start_ref[:, groups]
    if past:
        states = states * jnp.exp(-float(past) * rates)
    decay = jnp.exp(-rates)
    return [decay[mode] for mode in range(half)], tuple(states[mode] for mode in range(half))


def add_carry(sums, into, decay, states):
    def turn(index, states):
        at = pl.multiple_of(index * LONG * SUBS, LONG * SUBS)
        for step in range(LONG):
            states = tuple(d * s for d, s in zip(decay, states))
            where = pl.ds(at + step * SUBS, SUBS)
            into[where, :] = sums[where, :] + added(list(states))
        return states

    return lax.fori_loop(0, BLOCK // LONG, turn, states)


def own_carry_kernel(tiles, place_ref, rates_ref, scaled_ref, mine_ref, *sums_refs):
    count = len(sums_refs) // 2
    for tile in range(tiles):
        groups = slice(tile * SUBS, (tile + 1) * SUBS)
        decay, states = half_modes(place_ref[0] % 2, mine_ref, rates_ref, scaled_ref, groups, 0)
        for unit in range(tile, count, tiles):
            states = add_carry(sums_refs[unit], sums_refs[count + unit], decay, states)


def outer_kernel(tiles, own_done, place_ref, gate_ref, rates_ref, scaled_ref, mine_ref, twins_ref, *rest):
    *sums_refs, out_hbm, store, out, sems = rest
    core = place_ref[0] % 2
    blocks = len(sums_refs) // tiles
    copies = []
    for tile in range(tiles):
        groups = slice(tile * SUBS, (tile + 1) * SUBS)
        decay, states = half_modes(1 - core, twins_ref, rates_ref, scaled_ref, groups, 0)
        for block in range(blocks):
            if block == own_done:
                more = half_modes(core, mine_ref, rates_ref, scaled_ref, groups, own_done * BLOCK)
                decay, states = decay + more[0], states + more[1]
            into = store.at[pl.ds(block * BLOCK * SUBS, BLOCK * SUBS)]
            states = add_carry(sums_refs[block * tiles + tile], into, decay, states)
        for group in range(SUBS):
            rows = slice(tile * TILE + group * LANES, tile * TILE + (group + 1) * LANES)
            for block in range(blocks):
                cols = slice(block * BLOCK, (block + 1) * BLOCK)
                turned = store[pl.ds(block * BLOCK * SUBS + group, BLOCK, stride=SUBS), :].T
                out[rows, cols] = (gate_ref[rows, cols].astype(F32) * turned).astype(BF16)
            copy = pltpu.make_async_copy(out.at[rows], out_hbm.at[rows], sems.at[tile * SUBS + group])
            copy.start()
            copies.append(copy)
    for copy in copies:
        copy.wait()


SCALAR = pl.BlockSpec(memory_space=pltpu.SMEM)
WHOLE = pl.BlockSpec(memory_space=pltpu.VMEM)
FAR = pl.BlockSpec(memory_space=pltpu.HBM)
OWN = 2
INNER_ROOM, RIM_ROOM = 32, 24


def steps_scratch(steps):
    return pltpu.VMEM((steps * SUBS, LANES), F32)


def kept_far(array):
    return pltpu.with_memory_space_constraint(array, pltpu.HBM)


def on_device(v_stream, gate_one, gate_two, short_filter, decay_rates, residues, skip_bias):
    real_channels, tokens = v_stream.shape
    modes = decay_rates.shape[1]
    shards = lax.axis_size("seq")
    before = lax.ppermute(v_stream[:, tokens - BLOCK :], "seq", [(i, i + 1) for i in range(shards - 1)])
    extra = -real_channels % TILE

    def padded(array):
        return jnp.pad(array, ((0, extra),) + ((0, 0),) * (array.ndim - 1)) if extra else array

    v_stream, gate_one, gate_two, short_filter = map(padded, (v_stream, gate_one, gate_two, short_filter))
    decay_rates, residues, skip_bias, before = map(padded, (decay_rates, residues, skip_bias, before))
    channels = real_channels + extra
    tiles, groups = channels // TILE, channels // LANES
    raw_rates, raw_weights = decay_rates.T, residues.T
    bias = skip_bias.reshape(groups, LANES)
    tables = jnp.asarray(window_tables())
    place = lax.axis_index("seq").astype(jnp.int32).reshape(1)
    inner = tokens - BLOCK
    shape = jax.ShapeDtypeStruct
    per_mode = shape((modes, groups, LANES), F32)
    half = shape((modes // 2, groups, LANES), F32)
    laid = pltpu.VMEM((modes * SUBS, LANES), F32)
    tap_spectra = shape((channels, 2 * BLOCK), F32)
    head = shape((channels, BLOCK), BF16)
    spectrum, inner_mixed, inner_state, rates, scaled, v_first, gate_first, tables = pl.pallas_call(
        functools.partial(inner_kernel, tokens * shards),
        in_specs=[FAR] * 6,
        out_specs=[WHOLE] * 8,
        out_shape=[tap_spectra, shape((tiles, inner * SUBS, LANES), BF16)] + [per_mode] * 3 + [head, head]
        + [shape(tables.shape, BF16)],
        scratch_shapes=[
            pltpu.VMEM((channels, inner), BF16),
            pltpu.VMEM((channels, inner), BF16),
            pltpu.VMEM((channels, BLOCK), F32),
            pltpu.VMEM((modes, channels), F32),
            pltpu.VMEM((modes, channels), F32),
            steps_scratch(inner),
            laid,
            pltpu.SemaphoreType.DMA((tiles * 5 + 3,)),
        ],
        compiler_params=pltpu.CompilerParams(vmem_limit_bytes=INNER_ROOM << 20),
        cost_estimate=pl.CostEstimate(
            flops=channels * inner * 2600, bytes_accessed=channels * tokens * 8, transcendentals=0
        ),
    )(*map(kept_far, (v_stream, gate_one, short_filter, raw_rates, raw_weights, tables)))
    rim_mixed, own_end, twin_half = pl.pallas_call(
        functools.partial(rim_kernel, inner),
        in_specs=[SCALAR] + [WHOLE] * 7,
        out_specs=[WHOLE] * 3,
        out_shape=[shape((tiles, BLOCK * SUBS, LANES), BF16), half, half],
        scratch_shapes=[steps_scratch(BLOCK), pltpu.VMEM((modes, SUBS, LANES), F32)],
        compiler_params=pltpu.CompilerParams(vmem_limit_bytes=RIM_ROOM << 20),
        cost_estimate=pl.CostEstimate(
            flops=channels * BLOCK * 2600, bytes_accessed=channels * BLOCK * 16, transcendentals=0
        ),
    )(place, before, v_first, gate_first, spectrum, rates, inner_state, tables)

    def swap(array, distance):
        return lax.ppermute(array, "seq", [(i, i ^ distance) for i in range(shards)])

    def small(kernel, outputs, *arrays):
        return pl.pallas_call(
            kernel,
            in_specs=[SCALAR] + [WHOLE] * (len(arrays) + 1),
            out_specs=[WHOLE] * outputs,
            out_shape=[half] * outputs,
            compiler_params=pltpu.CompilerParams(vmem_limit_bytes=8 << 20),
        )(place, rates, *arrays)

    blocks = tokens // BLOCK
    sums, states = [], {}
    one_tile = shape((modes, SUBS, LANES), F32)

    def beside(arriving, sent, count):
        units = [divmod(len(sums) + i, tiles) for i in range(count) if len(sums) + i < blocks * tiles]
        if not units:
            return arriving
        touched = sorted({tile for _, tile in units})
        known = [tile for tile in touched if tile in states]
        kept = [tile for tile in touched if (blocks - 1, tile) not in units]
        rim, *earlier, _ = lax.optimization_barrier((rim_mixed, *(states[tile] for tile in known), sent))
        done = pl.pallas_call(
            functools.partial(local_kernel, units, known, kept),
            in_specs=[WHOLE] * (5 + len(known)),
            out_specs=[WHOLE] * (len(units) + len(kept)),
            out_shape=[shape((BLOCK * SUBS, LANES), F32)] * len(units) + [one_tile] * len(kept),
            compiler_params=pltpu.CompilerParams(vmem_limit_bytes=8 << 20),
            cost_estimate=pl.CostEstimate(
                flops=len(units) * TILE * BLOCK * 2600, bytes_accessed=TILE * BLOCK * 16, transcendentals=0
            ),
        )(rim, inner_mixed, rates, scaled, bias, *earlier)
        arriving, *done = lax.optimization_barrier((arriving, *done))
        sums.extend(done[: len(units)])
        states.update(zip(kept, done[len(units) :]))
        return arriving

    levels = shards.bit_length() - 2
    early = blocks * tiles // 8
    quotas = [(blocks * tiles - early + levels - 1 - i) // levels for i in range(levels)]
    twin_end = beside(swap(twin_half, 1), twin_half, early)
    (total,) = small(functools.partial(chip_kernel, tokens), 1, own_end, twin_end)
    ahead = jnp.zeros(half.shape, F32)
    size = 2
    for quota in quotas[:-1]:
        other = beside(swap(total, size), total, quota)
        total, ahead = small(functools.partial(level_kernel, tokens, size), 2, total, other, ahead)
        size *= 2
    other = beside(swap(total, size), total, quotas[-1])
    mine, twins = small(functools.partial(start_kernel, tokens, size), 2, other, ahead, own_end, twin_end)
    twins = swap(twins, 1)
    own = OWN * tiles
    sums[:own] = pl.pallas_call(
        functools.partial(own_carry_kernel, tiles),
        in_specs=[SCALAR] + [WHOLE] * (3 + own),
        out_specs=[WHOLE] * own,
        out_shape=[shape(sums[0].shape, F32)] * own,
        compiler_params=pltpu.CompilerParams(vmem_limit_bytes=8 << 20),
        cost_estimate=pl.CostEstimate(
            flops=channels * OWN * BLOCK * 600, bytes_accessed=channels * BLOCK * 16, transcendentals=0
        ),
    )(place, rates, scaled, mine, *sums[:own])

    hyena_out = pl.pallas_call(
        functools.partial(outer_kernel, tiles, OWN),
        in_specs=[SCALAR] + [WHOLE] * (5 + len(sums)),
        out_specs=FAR,
        out_shape=shape((channels, tokens), BF16),
        scratch_shapes=[
            steps_scratch(tokens),
            pltpu.VMEM((channels, tokens), BF16),
            pltpu.SemaphoreType.DMA((groups,)),
        ],
        compiler_params=pltpu.CompilerParams(vmem_limit_bytes=24 << 20),
        cost_estimate=pl.CostEstimate(
            flops=channels * tokens * 50, bytes_accessed=channels * tokens * 6, transcendentals=0
        ),
    )(place, gate_two, rates, scaled, mine, twins, *sums)
    return hyena_out[:real_channels]


def solution(mesh):
    in_specs = (
        P("chan", "seq"),
        P("chan", "seq"),
        P("chan", "seq"),
        P("chan", None),
        P("chan", None),
        P("chan", None),
        P("chan"),
    )
    out_specs = P("chan", "seq")
    return jax.shard_map(
        on_device, mesh=mesh, in_specs=in_specs, out_specs=out_specs, check_vma=False
    )
```

```python
import functools
import math

import jax
import jax.numpy as jnp
import numpy as np
from jax import lax
from jax.experimental import pallas as pl
from jax.experimental.pallas import tpu as pltpu
from jax.sharding import PartitionSpec as P

LANES = 128
SUBS = 8
TILE = LANES * SUBS
BLOCK = 128
ROWS = 1024
STEPS = 16
LONG = 32
F32, BF16 = jnp.float32, jnp.bfloat16


def halves(table):
    high = table.astype(jnp.bfloat16)
    low = (table - high.astype(np.float64)).astype(jnp.bfloat16)
    return high, low


def window_tables():
    size = 2 * BLOCK
    phase = 2.0 * math.pi / size * np.outer(np.arange(size), np.arange(BLOCK) + 0.5)
    forward = np.concatenate([np.cos(phase), -np.sin(phase)], axis=1)
    signs = np.tile((-1.0) ** np.arange(BLOCK), 2)
    inverse = forward[BLOCK:].T / BLOCK
    even = np.concatenate(halves(forward[:BLOCK]), axis=0)
    odd = np.concatenate(halves(forward[:BLOCK] * signs), axis=0)
    back = np.concatenate(halves(inverse), axis=1)
    return np.concatenate([even, odd, back], axis=1)


EVEN, ODD, BACK = (slice(i * 2 * BLOCK, (i + 1) * 2 * BLOCK) for i in range(3))


def mm(left, right):
    return jnp.dot(left, right, preferred_element_type=F32)


def split(value):
    high = value.astype(BF16)
    return high, (value - high.astype(F32)).astype(BF16)


def twice(block):
    return jnp.concatenate([block, block], axis=1)


def parts(image):
    return image[:, :BLOCK], image[:, BLOCK:]


def apply_window(earlier, later, spectrum, tables, fine=False):
    (e_re, e_im), (l_re, l_im), (h_re, h_im) = parts(earlier), parts(later), parts(spectrum)
    re, im = e_re + l_im, e_im - l_re
    product = jnp.concatenate([re * h_re - im * h_im, re * h_im + im * h_re], axis=1)
    high, low = split(product)
    both = mm(high, tables[:, BACK])
    result = both[:, :BLOCK] + both[:, BLOCK:]
    return result + mm(low, tables[:, BACK][:, :BLOCK]) if fine else result


def put_mixed(store, first_row, block_at, short, gate):
    mixed = (gate.astype(F32) * short).astype(BF16).astype(F32)
    for piece in range(ROWS // LANES):
        group = first_row // LANES + piece
        turned = mixed[piece * LANES : (piece + 1) * LANES].T
        store[pl.ds(block_at * BLOCK * SUBS + group, BLOCK, stride=SUBS), :] = turned


def lay_out(rows_ref, store):
    modes = rows_ref.shape[0]
    for group in range(SUBS):
        store[pl.ds(group, modes, stride=SUBS), :] = rows_ref[:, group * LANES : (group + 1) * LANES]


def end_states(store, mixed_ref, rates_ref):
    modes = rates_ref.shape[0]
    steps = store.shape[0] // SUBS
    decay = [jnp.exp(-rates_ref[mode]) for mode in range(modes)]

    def turn(index, states):
        at = pl.multiple_of(index * STEPS * SUBS, STEPS * SUBS)
        values = store[pl.ds(at, STEPS * SUBS), :]
        mixed_ref[pl.ds(at, STEPS * SUBS), :] = values.astype(BF16)
        for step in range(STEPS):
            value = values[step * SUBS : (step + 1) * SUBS]
            states = tuple(d * s + value for d, s in zip(decay, states))
        return states

    zeros = tuple(jnp.zeros((SUBS, LANES), F32) for _ in range(modes))
    return lax.fori_loop(0, steps // STEPS, turn, zeros)


def inner_kernel(
    seq_total,
    v_hbm, gate_hbm, taps_hbm, raw_hbm, raw_weights_hbm, tables_hbm,
    spec_ref, mixed_ref, state_ref, rates_ref, scaled_ref, v_first, gate_first, tables,
    v_rest, gate_rest, taps, raw, raw_weights, store, laid, sems,
):
    tiles, inner = mixed_ref.shape[0], v_rest.shape[1]

    def copies(tile):
        rows = pl.ds(tile * TILE, TILE)
        pairs = [(taps_hbm.at[rows], taps.at[rows])]
        for whole, head, rest in ((v_hbm, v_first, v_rest), (gate_hbm, gate_first, gate_rest)):
            pairs.append((whole.at[rows, pl.ds(0, BLOCK)], head.at[rows]))
            pairs.append((whole.at[rows, pl.ds(BLOCK, inner)], rest.at[rows]))
        return [pltpu.make_async_copy(*pair, sems.at[tile * 5 + i]) for i, pair in enumerate(pairs)]

    small = [
        pltpu.make_async_copy(tables_hbm, tables, sems.at[tiles * 5]),
        pltpu.make_async_copy(raw_hbm, raw, sems.at[tiles * 5 + 1]),
        pltpu.make_async_copy(raw_weights_hbm, raw_weights, sems.at[tiles * 5 + 2]),
    ]
    large = [copies(tile) for tile in range(tiles)]
    for copy in small + large[0]:
        copy.start()
    for copy in small + large[0]:
        copy.wait()
    sign = 1.0 - 2.0 * (lax.broadcasted_iota(jnp.int32, (1, 2 * BLOCK), 1) % 2).astype(F32)
    for tile in range(tiles):
        rows = slice(tile * TILE, (tile + 1) * TILE)
        groups = slice(tile * SUBS, (tile + 1) * SUBS)
        if tile:
            for copy in large[tile]:
                copy.wait()
        if tile + 1 < tiles:
            for copy in large[tile + 1]:
                copy.start()
        tap_hi, tap_lo = split(taps[rows])
        spectrum = mm(twice(tap_hi), tables[:, EVEN]) + mm(tap_lo, tables[:BLOCK, EVEN])
        turned = spectrum * sign
        spec_ref[rows] = turned
        earlier = mm(twice(v_first[rows]), tables[:, EVEN])
        for block in range(1, inner // BLOCK + 1):
            at = slice((block - 1) * BLOCK, block * BLOCK)
            later = mm(twice(v_rest[rows, at]), tables[:, ODD if block % 2 else EVEN])
            short = apply_window(earlier, later, spectrum if block % 2 else turned, tables)
            put_mixed(store, 0, block - 1, short, gate_rest[rows, at])
            earlier = later
        lay_out(raw.at[:, pl.ds(tile * TILE, TILE)], laid)
        modes = raw.shape[0]
        rates = laid[...].reshape(modes, SUBS, LANES)
        rates_ref[:, groups] = rates
        lay_out(raw_weights.at[:, pl.ds(tile * TILE, TILE)], laid)
        scaled_ref[:, groups] = laid[...].reshape(modes, SUBS, LANES) * jnp.sqrt(2.0 * rates + 2.0 / seq_total)
        for mode, state in enumerate(end_states(store, mixed_ref.at[tile], rates_ref.at[:, groups])):
            state_ref[mode, groups] = state


def rim_kernel(inner, place_ref, before_ref, v_ref, gate_ref, spec_ref, rates_ref, inner_ref, tables, *rest):
    mixed_ref, own_ref, twin_ref, store, ends = rest
    half = own_ref.shape[0]
    core = place_ref[0] % 2
    for tile in range(mixed_ref.shape[0]):
        rows = slice(tile * TILE, (tile + 1) * TILE)
        groups = slice(tile * SUBS, (tile + 1) * SUBS)
        earlier = mm(twice(before_ref[rows]), tables[:, ODD])
        later = mm(twice(v_ref[rows]), tables[:, EVEN])
        short = apply_window(earlier, later, spec_ref[rows], tables, fine=True)
        put_mixed(store, 0, 0, short, gate_ref[rows])
        rates = rates_ref.at[:, groups]
        for mode, state in enumerate(end_states(store, mixed_ref.at[tile], rates)):
            ends[mode] = jnp.exp(-float(inner) * rates[mode]) * state + inner_ref[mode, groups]
        own_ref[:, groups] = ends[pl.ds(core * half, half)]
        twin_ref[:, groups] = ends[pl.ds((1 - core) * half, half)]


def decayed(rates, positions):
    return jnp.exp(-lax.convert_element_type(positions, F32) * rates)


def chip_kernel(tokens, place_ref, rates_ref, mine_ref, other_ref, total_ref):
    half = total_ref.shape[0]
    core = place_ref[0] % 2
    rates = rates_ref[pl.ds(core * half, half)]
    total_ref[...] = decayed(rates, tokens * (1 - core)) * mine_ref[...] + decayed(rates, tokens * core) * other_ref[...]


def level_kernel(tokens, size, place_ref, rates_ref, total_ref, other_ref, before_ref, joined_ref, after_ref):
    half = total_ref.shape[0]
    place = place_ref[0]
    upper = place // size % 2
    rates = rates_ref[pl.ds(place % 2 * half, half)]
    joined_ref[...] = (
        decayed(rates, tokens * size * (1 - upper)) * total_ref[...]
        + decayed(rates, tokens * size * upper) * other_ref[...]
    )
    reach = decayed(rates, tokens * (place % size // 2 * 2)) * other_ref[...]
    after_ref[...] = before_ref[...] + jnp.where(upper == 1, reach, 0.0)


def start_kernel(tokens, size, place_ref, rates_ref, other_ref, before_ref, own_ref, twin_ref, mine_ref, twins_ref):
    half = own_ref.shape[0]
    place = place_ref[0]
    core = place % 2
    upper = place // size % 2
    rates = rates_ref[pl.ds(core * half, half)]
    reach = decayed(rates, tokens * (place % size // 2 * 2)) * other_ref[...]
    first = before_ref[...] + jnp.where(upper == 1, reach, 0.0)
    second = decayed(rates, tokens) * first + jnp.where(core == 0, own_ref[...], twin_ref[...])
    mine_ref[...] = jnp.where(core == 0, first, second)
    twins_ref[...] = jnp.where(core == 0, second, first)


def added(terms):
    while len(terms) > 1:
        terms = [sum(terms[i : i + 2][1:], terms[i]) for i in range(0, len(terms), 2)]
    return terms[0]


def filtered(source, start, store, decay, scaled, bias, states):
    def turn(index, states):
        at = pl.multiple_of(index * LONG * SUBS, LONG * SUBS)
        values = source[pl.ds(start * SUBS + at, LONG * SUBS), :].astype(F32)
        sums = []
        for step in range(LONG):
            value = values[step * SUBS : (step + 1) * SUBS]
            states = tuple(d * s + value for d, s in zip(decay, states))
            sums.append(added([c * s for c, s in zip(scaled, states)] + [bias * value]))
        store[pl.ds(at, LONG * SUBS), :] = jnp.concatenate(sums, axis=0)
        return states

    return lax.fori_loop(0, BLOCK // LONG, turn, states)


def local_kernel(units, known, kept, rim_ref, inner_ref, rates_ref, scaled_ref, bias_ref, *rest):
    earlier, sums_refs, states_refs = rest[: len(known)], rest[len(known) :][: len(units)], rest[len(known) + len(units) :]
    modes = rates_ref.shape[0]
    held = {tile: tuple(ref[mode] for mode in range(modes)) for tile, ref in zip(known, earlier)}
    for (block, tile), sums_ref in zip(units, sums_refs):
        groups = slice(tile * SUBS, (tile + 1) * SUBS)
        decay = [jnp.exp(-rates_ref[mode, groups]) for mode in range(modes)]
        scaled = [scaled_ref[mode, groups] for mode in range(modes)]
        states = held.get(tile, tuple(jnp.zeros((SUBS, LANES), F32) for _ in range(modes)))
        source, start = (inner_ref, (block - 1) * BLOCK) if block else (rim_ref, 0)
        held[tile] = filtered(source.at[tile], start, sums_ref, decay, scaled, bias_ref[groups], states)
    for tile, states_ref in zip(kept, states_refs):
        for mode in range(modes):
            states_ref[mode] = held[tile][mode]


def half_modes(which, start_ref, rates_ref, scaled_ref, groups, past):
    half = start_ref.shape[0]
    rates = rates_ref[pl.ds(which * half, half), groups]
    states = scaled_ref[pl.ds(which * half, half), groups] * start_ref[:, groups]
    if past:
        states = states * jnp.exp(-float(past) * rates)
    decay = jnp.exp(-rates)
    return [decay[mode] for mode in range(half)], tuple(states[mode] for mode in range(half))


def add_carry(sums, into, decay, states):
    def turn(index, states):
        at = pl.multiple_of(index * LONG * SUBS, LONG * SUBS)
        for step in range(LONG):
            states = tuple(d * s for d, s in zip(decay, states))
            where = pl.ds(at + step * SUBS, SUBS)
            into[where, :] = sums[where, :] + added(list(states))
        return states

    return lax.fori_loop(0, BLOCK // LONG, turn, states)


def own_carry_kernel(tiles, place_ref, rates_ref, scaled_ref, mine_ref, *sums_refs):
    count = len(sums_refs) // 2
    for tile in range(tiles):
        groups = slice(tile * SUBS, (tile + 1) * SUBS)
        decay, states = half_modes(place_ref[0] % 2, mine_ref, rates_ref, scaled_ref, groups, 0)
        for unit in range(tile, count, tiles):
            states = add_carry(sums_refs[unit], sums_refs[count + unit], decay, states)


def outer_kernel(tiles, own_done, place_ref, gate_ref, rates_ref, scaled_ref, mine_ref, twins_ref, *rest):
    *sums_refs, out_hbm, store, out, sems = rest
    core = place_ref[0] % 2
    blocks = len(sums_refs) // tiles
    copies = []
    for tile in range(tiles):
        groups = slice(tile * SUBS, (tile + 1) * SUBS)
        decay, states = half_modes(1 - core, twins_ref, rates_ref, scaled_ref, groups, 0)
        for block in range(blocks):
            if block == own_done:
                more = half_modes(core, mine_ref, rates_ref, scaled_ref, groups, own_done * BLOCK)
                decay, states = decay + more[0], states + more[1]
            into = store.at[pl.ds(block * BLOCK * SUBS, BLOCK * SUBS)]
            states = add_carry(sums_refs[block * tiles + tile], into, decay, states)
        for group in range(SUBS):
            rows = slice(tile * TILE + group * LANES, tile * TILE + (group + 1) * LANES)
            for block in range(blocks):
                cols = slice(block * BLOCK, (block + 1) * BLOCK)
                turned = store[pl.ds(block * BLOCK * SUBS + group, BLOCK, stride=SUBS), :].T
                out[rows, cols] = (gate_ref[rows, cols].astype(F32) * turned).astype(BF16)
            copy = pltpu.make_async_copy(out.at[rows], out_hbm.at[rows], sems.at[tile * SUBS + group])
            copy.start()
            copies.append(copy)
    for copy in copies:
        copy.wait()


SCALAR = pl.BlockSpec(memory_space=pltpu.SMEM)
WHOLE = pl.BlockSpec(memory_space=pltpu.VMEM)
FAR = pl.BlockSpec(memory_space=pltpu.HBM)
OWN = 2
INNER_ROOM, RIM_ROOM = 32, 24


def steps_scratch(steps):
    return pltpu.VMEM((steps * SUBS, LANES), F32)


def kept_far(array):
    return pltpu.with_memory_space_constraint(array, pltpu.HBM)


def on_device(v_stream, gate_one, gate_two, short_filter, decay_rates, residues, skip_bias):
    real_channels, tokens = v_stream.shape
    modes = decay_rates.shape[1]
    shards = lax.axis_size("seq")
    before = lax.ppermute(v_stream[:, tokens - BLOCK :], "seq", [(i, i + 1) for i in range(shards - 1)])
    extra = -real_channels % TILE

    def padded(array):
        return jnp.pad(array, ((0, extra),) + ((0, 0),) * (array.ndim - 1)) if extra else array

    v_stream, gate_one, gate_two, short_filter = map(padded, (v_stream, gate_one, gate_two, short_filter))
    decay_rates, residues, skip_bias, before = map(padded, (decay_rates, residues, skip_bias, before))
    channels = real_channels + extra
    tiles, groups = channels // TILE, channels // LANES
    raw_rates, raw_weights = decay_rates.T, residues.T
    bias = skip_bias.reshape(groups, LANES)
    tables = jnp.asarray(window_tables())
    place = lax.axis_index("seq").astype(jnp.int32).reshape(1)
    inner = tokens - BLOCK
    shape = jax.ShapeDtypeStruct
    per_mode = shape((modes, groups, LANES), F32)
    half = shape((modes // 2, groups, LANES), F32)
    laid = pltpu.VMEM((modes * SUBS, LANES), F32)
    tap_spectra = shape((channels, 2 * BLOCK), F32)
    head = shape((channels, BLOCK), BF16)
    spectrum, inner_mixed, inner_state, rates, scaled, v_first, gate_first, tables = pl.pallas_call(
        functools.partial(inner_kernel, tokens * shards),
        in_specs=[FAR] * 6,
        out_specs=[WHOLE] * 8,
        out_shape=[tap_spectra, shape((tiles, inner * SUBS, LANES), BF16)] + [per_mode] * 3 + [head, head]
        + [shape(tables.shape, BF16)],
        scratch_shapes=[
            pltpu.VMEM((channels, inner), BF16),
            pltpu.VMEM((channels, inner), BF16),
            pltpu.VMEM((channels, BLOCK), F32),
            pltpu.VMEM((modes, channels), F32),
            pltpu.VMEM((modes, channels), F32),
            steps_scratch(inner),
            laid,
            pltpu.SemaphoreType.DMA((tiles * 5 + 3,)),
        ],
        compiler_params=pltpu.CompilerParams(vmem_limit_bytes=INNER_ROOM << 20),
        cost_estimate=pl.CostEstimate(
            flops=channels * inner * 2600, bytes_accessed=channels * tokens * 8, transcendentals=0
        ),
    )(*map(kept_far, (v_stream, gate_one, short_filter, raw_rates, raw_weights, tables)))
    rim_mixed, own_end, twin_half = pl.pallas_call(
        functools.partial(rim_kernel, inner),
        in_specs=[SCALAR] + [WHOLE] * 7,
        out_specs=[WHOLE] * 3,
        out_shape=[shape((tiles, BLOCK * SUBS, LANES), BF16), half, half],
        scratch_shapes=[steps_scratch(BLOCK), pltpu.VMEM((modes, SUBS, LANES), F32)],
        compiler_params=pltpu.CompilerParams(vmem_limit_bytes=RIM_ROOM << 20),
        cost_estimate=pl.CostEstimate(
            flops=channels * BLOCK * 2600, bytes_accessed=channels * BLOCK * 16, transcendentals=0
        ),
    )(place, before, v_first, gate_first, spectrum, rates, inner_state, tables)

    def swap(array, distance):
        return lax.ppermute(array, "seq", [(i, i ^ distance) for i in range(shards)])

    def small(kernel, outputs, *arrays):
        return pl.pallas_call(
            kernel,
            in_specs=[SCALAR] + [WHOLE] * (len(arrays) + 1),
            out_specs=[WHOLE] * outputs,
            out_shape=[half] * outputs,
            compiler_params=pltpu.CompilerParams(vmem_limit_bytes=8 << 20),
        )(place, rates, *arrays)

    blocks = tokens // BLOCK
    sums, states = [], {}
    one_tile = shape((modes, SUBS, LANES), F32)

    def beside(arriving, sent, count):
        units = [divmod(len(sums) + i, tiles) for i in range(count) if len(sums) + i < blocks * tiles]
        if not units:
            return arriving
        touched = sorted({tile for _, tile in units})
        known = [tile for tile in touched if tile in states]
        kept = [tile for tile in touched if (blocks - 1, tile) not in units]
        rim, *earlier, _ = lax.optimization_barrier((rim_mixed, *(states[tile] for tile in known), sent))
        done = pl.pallas_call(
            functools.partial(local_kernel, units, known, kept),
            in_specs=[WHOLE] * (5 + len(known)),
            out_specs=[WHOLE] * (len(units) + len(kept)),
            out_shape=[shape((BLOCK * SUBS, LANES), F32)] * len(units) + [one_tile] * len(kept),
            compiler_params=pltpu.CompilerParams(vmem_limit_bytes=8 << 20),
            cost_estimate=pl.CostEstimate(
                flops=len(units) * TILE * BLOCK * 2600, bytes_accessed=TILE * BLOCK * 16, transcendentals=0
            ),
        )(rim, inner_mixed, rates, scaled, bias, *earlier)
        arriving, *done = lax.optimization_barrier((arriving, *done))
        sums.extend(done[: len(units)])
        states.update(zip(kept, done[len(units) :]))
        return arriving

    levels = shards.bit_length() - 2
    early = blocks * tiles // 8
    quotas = [(blocks * tiles - early + levels - 1 - i) // levels for i in range(levels)]
    twin_end = beside(swap(twin_half, 1), twin_half, early)
    (total,) = small(functools.partial(chip_kernel, tokens), 1, own_end, twin_end)
    ahead = jnp.zeros(half.shape, F32)
    size = 2
    for quota in quotas[:-1]:
        other = beside(swap(total, size), total, quota)
        total, ahead = small(functools.partial(level_kernel, tokens, size), 2, total, other, ahead)
        size *= 2
    other = beside(swap(total, size), total, quotas[-1])
    mine, twins = small(functools.partial(start_kernel, tokens, size), 2, other, ahead, own_end, twin_end)
    twins = swap(twins, 1)
    own = OWN * tiles
    sums[:own] = pl.pallas_call(
        functools.partial(own_carry_kernel, tiles),
        in_specs=[SCALAR] + [WHOLE] * (3 + own),
        out_specs=[WHOLE] * own,
        out_shape=[shape(sums[0].shape, F32)] * own,
        compiler_params=pltpu.CompilerParams(vmem_limit_bytes=8 << 20),
        cost_estimate=pl.CostEstimate(
            flops=channels * OWN * BLOCK * 600, bytes_accessed=channels * BLOCK * 16, transcendentals=0
        ),
    )(place, rates, scaled, mine, *sums[:own])

    hyena_out = pl.pallas_call(
        functools.partial(outer_kernel, tiles, OWN),
        in_specs=[SCALAR] + [WHOLE] * (5 + len(sums)),
        out_specs=FAR,
        out_shape=shape((channels, tokens), BF16),
        scratch_shapes=[
            steps_scratch(tokens),
            pltpu.VMEM((channels, tokens), BF16),
            pltpu.SemaphoreType.DMA((groups,)),
        ],
        compiler_params=pltpu.CompilerParams(vmem_limit_bytes=24 << 20),
        cost_estimate=pl.CostEstimate(
            flops=channels * tokens * 50, bytes_accessed=channels * tokens * 6, transcendentals=0
        ),
    )(place, gate_two, rates, scaled, mine, twins, *sums)
    return hyena_out[:real_channels]


def solution(mesh):
    in_specs = (
        P("chan", "seq"),
        P("chan", "seq"),
        P("chan", "seq"),
        P("chan", None),
        P("chan", None),
        P("chan", None),
        P("chan"),
    )
    out_specs = P("chan", "seq")
    return jax.shard_map(
        on_device, mesh=mesh, in_specs=in_specs, out_specs=out_specs, check_vma=False
    )
```
